32 devices in a mesh: slide: 4 (over y, x), seq: 8 (over z, core).
Axes of the slice: x: 2, y: 2, z: 4, core: 2. Of those that a mesh axis runs over, the one named last changes fastest.
Arguments:
- embeds: bfloat16 [12288, 1536], P(('slide', 'seq'))
- destination: int32 [12288, 1], P(('slide', 'seq')), may hold values from 0 to 31; in each aligned block of 384 rows (0 to 383, 384 to 767, ...) at most 24 rows name the same one
- norm_gain: float32 [1536], replicated, may hold values from 0.1 to 1.9
- qkv_weight: bfloat16 [1536, 4608], replicated
- out_weight: bfloat16 [1536, 1536], replicated, may hold values from -0.15625 to 0.15625
- finding_queries: bfloat16 [256, 1536], replicated
Outputs:
- layer_out: bfloat16 [24576, 1536], P(('slide', 'seq'))
- heatmap: float32 [24576, 256], P(('slide', 'seq'))
The draws below stay inside these ranges and needn't reach their ends.
Inputs may be any that keep to these rules, and one draw needn't show every extreme that they name: `destination`: each block of 384 rows (one encoder device) names any one device at most 24 times, and some block names some device exactly 24 times; every device is named by some row.
All inputs are finite; a program needn't handle non-finite values.
Results may differ from the reference program's by a relative error of at most 0.01225.
The reference program's roundings to bfloat16 on the way (of `tiles`, `normed`, `projected`, `weights`, `mixed` and `keys_find`) count: a program that leaves them out, or rounds other values in their place, can miss the bound.
Values may be sent and summed in bfloat16 or wider, within the bound.
A program may use at most 192 MiB of HBM per device.

```python
import math
import jax
import jax.numpy as jnp
import numpy as np
from jax import lax

D = 1536
HEADS = 12
HEAD_DIM = 128
FIND = 256
TOK_DEV = 768
PAIR_CAP = 24
ENC_DEV = 384
ENC_ROWS = 12288
SLOTS = 24576
SLIDE_LEN = 6144
SLIDES = 4
DEVICES = 32


def draw_embeds(key, part):
    value_key = jax.random.fold_in(key, 11)
    blank_key = jax.random.fold_in(key, 12)
    values_drawn = jnp.clip(jax.random.normal(value_key, (ENC_ROWS, D), jnp.float32), -6.0, 6.0)
    present_row = jax.random.randint(blank_key, (ENC_ROWS, 1), 0, 16) != 0
    return jnp.where(present_row, values_drawn, 0.0).astype(jnp.bfloat16)


def draw_qkv_weight(key, part):
    return (jax.random.normal(key, (D, 3 * D), jnp.float32) * D ** (-0.5)).astype(jnp.bfloat16)


def draw_finding_queries(key, part):
    return jax.random.normal(key, (FIND, D), jnp.float32).astype(jnp.bfloat16)


def routed_block(stream_key, own, number, rows, amount, top, limit, lean):
    order = jax.random.permutation(stream_key, amount)
    crowded, usual = load_shares(amount, rows * top, limit, lean, True), load_shares(amount, rows * top, limit, lean, False)
    places = jnp.arange(amount)

    def named(tallies, turn):
        used = int((tallies > 0).sum())
        fixed = max(1, used // 4)
        shifted = fixed + (places - fixed + turn * (used - fixed)) % max(1, amount - fixed)
        return jnp.zeros((amount,), jnp.int32).at[order[jnp.where(places < fixed, places, shifted)]].set(jnp.asarray(tallies, jnp.int32))

    tallies = jnp.where(number % 4 == 0, named(crowded, number // 4), named(usual, number - number // 4 - 1))
    mixed = jax.random.permutation(jax.random.fold_in(own, 3), amount)
    donor, taker = mixed[0:amount // 2 * 2:2], mixed[1:amount // 2 * 2:2]
    margin = jnp.minimum(tallies[donor] - 1, limit - tallies[taker]) // 2
    margin = jnp.where((donor == order[0]) | (taker == order[0]) | (tallies[taker] == 0), 0, jnp.maximum(margin, 0))
    shifted = jax.random.randint(jax.random.fold_in(own, 4), (amount // 2,), 0, 1 << 20) % (margin + 1)
    tallies = tallies.at[donor].add(-shifted).at[taker].add(shifted)
    members = jnp.searchsorted(jnp.cumsum(tallies), jnp.arange(rows * top), side="right").astype(jnp.int32)
    grid = members.reshape(top, rows).T
    grid = grid[jax.random.permutation(jax.random.fold_in(own, 1), rows)]
    turn = jax.random.randint(jax.random.fold_in(own, 2), (rows, 1), 0, top)
    return jnp.take_along_axis(grid, (jnp.arange(top)[None, :] + turn) % top, axis=1)


def load_shares(amount, total, reach, slope, full):
    loads = [(1 << 20) // math.isqrt(rank ** slope) + 1 for rank in range(1, amount + 1)]
    largest = reach if full else min(reach, max(-(-total // amount), total * loads[0] // sum(loads)))
    least = 1 if total - largest >= amount - 1 else 0
    given, rest = [largest] + [least] * (amount - 1), total - largest - least * (amount - 1)
    while rest > 0:
        free = [i for i in range(1, amount) if given[i] < largest] or [i for i in range(1, amount) if given[i] < reach]
        whole, budget = sum([loads[i] for i in free]), rest
        for i in free:
            more = min(reach - given[i], max(1, budget * loads[i] // whole), rest)
            given[i] = given[i] + more
            rest = rest - more
    return np.array(given)


def scatter_about(own_key, shape, width, most, kind=jnp.bfloat16):
    return jnp.clip(width * jax.random.normal(own_key, shape, jnp.float32), -most, most).astype(kind)


def setup_inputs(seed: int = 0) -> dict:
    key_of = jax.random.split(jax.random.key(seed), 7)
    embeds = draw_embeds(jax.random.fold_in(key_of[6], 71), 0)
    destination_keys = jax.random.split(jax.random.fold_in(key_of[1], 1), ENC_ROWS // ENC_DEV)
    destination_turns = jax.random.permutation(jax.random.fold_in(key_of[1], 3), ENC_ROWS // ENC_DEV)
    destination = jax.vmap(lambda own, number: routed_block(jax.random.fold_in(key_of[1], 2), own, number, ENC_DEV, DEVICES, 1, PAIR_CAP, 2))(destination_keys, destination_turns).reshape((ENC_ROWS, 1))
    norm_gain = jnp.clip(1.0 + 0.18 * jax.random.normal(key_of[2], (D,), jnp.float32), 0.1, 1.9)
    qkv_weight = draw_qkv_weight(jax.random.fold_in(key_of[6], 71), 0)
    out_weight = scatter_about(key_of[4], (D, D), D ** -0.5, 0.15625)
    finding_queries = draw_finding_queries(jax.random.fold_in(key_of[6], 71), 0)
    return dict(embeds=embeds, destination=destination, norm_gain=norm_gain, qkv_weight=qkv_weight, out_weight=out_weight, finding_queries=finding_queries)


MASKED = -1e+30
EPSILON = 1e-06

def choose_heads(rate, spread):
    return jnp.arange(rate)[:, None] == jnp.arange(HEADS)[None, :] // spread % rate

def select(rows, rate, spread):
    count = rows.shape[0]
    grouped = rows.reshape(count // rate, rate, rows.shape[1], rows.shape[2])
    chosen = choose_heads(rate, spread)
    return lax.optimization_barrier(jnp.sum(jnp.where(chosen[None, :, :, None], grouped, jnp.zeros((), rows.dtype)), axis=1))

def spread_back(rows, rate, fill):
    count = rows.shape[0]
    chosen = choose_heads(rate, 1)
    widened = jnp.where(chosen[None, :, :, None], rows[:, None], jnp.asarray(fill, rows.dtype))
    return widened.reshape(count * rate, rows.shape[1], rows.shape[2])

def attend_exact(query, key_rows, value, keep):
    scale = query.shape[-1] ** (-0.5)
    scores = jnp.einsum('qhe,khe->hqk', query.astype(jnp.float32), key_rows.astype(jnp.float32)) * scale
    allowed = (keep[:, :, 0] > 0.5).T[:, None, :]
    scores = jnp.where(allowed, scores, MASKED)
    peak = lax.optimization_barrier(jnp.max(scores, axis=2, keepdims=True))
    exp_scores = jnp.where(allowed, jnp.exp(scores - peak), 0.0)
    total = lax.optimization_barrier(jnp.sum(exp_scores, axis=2))
    rounded = exp_scores.astype(jnp.bfloat16)
    weights = lax.optimization_barrier(rounded).astype(jnp.float32)
    weighted = jnp.einsum('hqk,khe->qhe', weights, value.astype(jnp.float32))
    bounded = jnp.maximum(total, 1.0)
    result = weighted / bounded.T[:, :, None]
    log_total = jnp.where(total > 0.0, peak[:, :, 0] + jnp.log(bounded), MASKED).T[:, :, None]
    return (result, log_total)

def arrange(embeds, destination):
    target = destination[:, 0].reshape(DEVICES, ENC_DEV)
    one_hot = (target[:, :, None] == jnp.arange(DEVICES, dtype=jnp.int32)[None, None, :]).astype(jnp.int32)
    rank = lax.optimization_barrier(jnp.sum(jnp.cumsum(one_hot, axis=1) * one_hot, axis=2)) - 1
    source = jnp.arange(DEVICES, dtype=jnp.int32)[:, None]
    place = (target * TOK_DEV + source * PAIR_CAP + rank).reshape(-1).astype(jnp.int32)
    tiles = jnp.zeros((SLOTS, D), jnp.bfloat16).at[place].set(embeds)
    valid = jnp.zeros((SLOTS,), jnp.int32).at[place].set(1)
    return (tiles, valid)

def one_slide(tiles, valid, norm_gain, qkv_weight, out_weight, finding_queries):
    tile_f32 = tiles.astype(jnp.float32)
    normed = (tile_f32 * lax.rsqrt(lax.optimization_barrier(jnp.mean(tile_f32 * tile_f32, axis=1, keepdims=True)) + EPSILON) * norm_gain).astype(jnp.bfloat16)
    projected = jnp.dot(normed, qkv_weight, preferred_element_type=jnp.float32).astype(jnp.bfloat16)
    projected = projected.reshape(SLIDE_LEN, 3, HEADS, HEAD_DIM)
    query, key_rows, value = (projected[:, 0], projected[:, 1], projected[:, 2])
    keep = jnp.broadcast_to(valid.astype(jnp.float32)[:, None, None], (SLIDE_LEN, HEADS, 1))
    results = []
    logs = []
    for rate in (1, 2, 4):
        picked = [select(member, rate, 1) for member in (query, key_rows, value, keep)]
        segments = picked[0].shape[0] // TOK_DEV
        shaped = tuple((member.reshape(segments, TOK_DEV, HEADS, member.shape[-1]) for member in picked))
        branch, log_total = lax.map(lambda pack: attend_exact(pack[0], pack[1], pack[2], pack[3]), shaped)
        results.append(spread_back(branch.reshape(-1, HEADS, HEAD_DIM), rate, 0.0))
        logs.append(spread_back(log_total.reshape(-1, HEADS, 1), rate, MASKED))
    stacked = jnp.stack(logs)
    top = lax.optimization_barrier(jnp.max(stacked, axis=0))
    factors = jnp.exp(stacked - top)
    mixed = (factors[0] * results[0] + factors[1] * results[1] + factors[2] * results[2]) / lax.optimization_barrier(jnp.sum(factors, axis=0))
    mixed = mixed.astype(jnp.bfloat16).reshape(SLIDE_LEN, D)
    layer_out = (tile_f32 + jnp.dot(mixed, out_weight, preferred_element_type=jnp.float32)).astype(jnp.bfloat16)
    out_f32 = layer_out.astype(jnp.float32)
    keys_find = (out_f32 * lax.rsqrt(lax.optimization_barrier(jnp.mean(out_f32 * out_f32, axis=1, keepdims=True)) + EPSILON)).astype(jnp.bfloat16)
    keys_find = keys_find.reshape(SLIDE_LEN, HEADS, HEAD_DIM).astype(jnp.float32)
    queries_find = finding_queries.reshape(FIND, HEADS, HEAD_DIM).astype(jnp.float32)
    scores = jnp.einsum('fhe,the->hft', queries_find, keys_find) * HEAD_DIM ** (-0.5)
    allowed = (valid > 0)[None, None, :]
    scores = jnp.where(allowed, scores, MASKED)
    peak = lax.optimization_barrier(jnp.max(scores, axis=2, keepdims=True))
    exp_scores = jnp.where(allowed, jnp.exp(scores - peak), 0.0)
    probs = exp_scores / lax.optimization_barrier(jnp.sum(exp_scores, axis=2, keepdims=True))
    heat = lax.optimization_barrier(jnp.sum(probs, axis=0)).T * (SLIDE_LEN / HEADS)
    return (layer_out, heat)

def reference(embeds, destination, norm_gain, qkv_weight, out_weight, finding_queries):
    tiles, valid = arrange(embeds, destination)
    tiles_slides = tiles.reshape(SLIDES, SLIDE_LEN, D)
    valid_slides = valid.reshape(SLIDES, SLIDE_LEN)
    layer_out, heat = lax.map(lambda pack: one_slide(pack[0], pack[1], norm_gain, qkv_weight, out_weight, finding_queries), (tiles_slides, valid_slides))
    return (layer_out.reshape(SLOTS, D), heat.reshape(SLOTS, FIND))
```

```python
import functools
import math

import jax
import jax.numpy as jnp
from jax import lax
from jax.experimental import pallas as pl
from jax.experimental.pallas import tpu as pltpu
from jax.sharding import PartitionSpec as P

HEADS = 12
HEAD = 128
GROUP = 4
WIDE = GROUP * HEAD
MASKED = -1e30
EPSILON = 1e-06
FACTOR = math.log2(math.e) / math.sqrt(HEAD)
F32 = jnp.float32
BF16 = jnp.bfloat16
QUARTER_OF = (0, 2, 1, 3)
VMEM_LIMIT = 56 * 1024 * 1024
SMALL_LIMIT = 34 * 1024 * 1024


def params(limit=VMEM_LIMIT, **more):
    return pltpu.CompilerParams(vmem_limit_bytes=limit, **more)


def dispatch_kernel(capacity, row_ref, embeds_ref, buffer_ref, counts_ref):
    rows = embeds_ref.shape[0]
    slots = buffer_ref.shape[0]
    row = row_ref[...]
    col = jnp.transpose(jnp.broadcast_to(row.astype(F32), (128, rows)))[:, 0:1].astype(jnp.int32)
    first = lax.broadcasted_iota(jnp.int32, (rows, rows), 0)
    second = lax.broadcasted_iota(jnp.int32, (rows, rows), 1)
    same = jnp.logical_and(col == row, first < second)
    rank = jnp.sum(same.astype(F32), axis=0, keepdims=True).astype(jnp.int32)
    place = row * capacity + rank
    lanes = lax.broadcasted_iota(jnp.int32, (rows, counts_ref.shape[1]), 1)
    counts_ref[...] = jnp.sum((col == lanes).astype(F32), axis=0, keepdims=True).astype(jnp.int32)
    chosen = (lax.broadcasted_iota(jnp.int32, (slots, rows), 0) == place).astype(F32).astype(BF16)
    for start in range(0, embeds_ref.shape[1], WIDE):
        part = embeds_ref[:, start : start + WIDE]
        buffer_ref[:, start : start + WIDE] = jnp.dot(
            chosen, part, preferred_element_type=F32
        ).astype(BF16)


def dispatch(destination, embeds, devices, capacity):
    rows, width = embeds.shape
    slots = devices * capacity
    return pl.pallas_call(
        functools.partial(dispatch_kernel, capacity),
        out_shape=(
            jax.ShapeDtypeStruct((slots, width), BF16),
            jax.ShapeDtypeStruct((1, max(128, devices)), jnp.int32),
        ),
        compiler_params=params(),
        name="dispatch",
    )(destination.reshape(1, rows), embeds)


def original_of(index, quarter):
    block = (
        (index >= quarter).astype(jnp.int32)
        + (index >= 2 * quarter).astype(jnp.int32)
        + (index >= 3 * quarter).astype(jnp.int32)
    )
    phase = 2 * jnp.where((block == 1) | (block == 3), 1, 0) + (block >= 2).astype(jnp.int32)
    return 4 * (index - quarter * block) + phase


def route_kernel(devices, seq_count, buffer_ref, counts_ref, tiles_ref, all_ref, send, recv, count_send, count_recv, own_sem):
    me = lax.axis_index("slide") * seq_count + lax.axis_index("seq")
    barrier = pltpu.get_barrier_semaphore()

    def place_of(hop):
        peer = lax.rem(me + hop, devices)
        return peer, (peer // seq_count, lax.rem(peer, seq_count))

    def greet(hop, carry):
        pl.semaphore_signal(
            barrier, inc=1, device_id=place_of(hop)[1], device_id_type=pl.DeviceIdType.MESH
        )
        return carry

    lax.fori_loop(1, devices, greet, 0)
    pl.semaphore_wait(barrier, devices - 1)

    def copies(hop):
        peer, where = place_of(hop)
        rows = pltpu.make_async_remote_copy(
            src_ref=buffer_ref.at[peer],
            dst_ref=tiles_ref.at[me],
            send_sem=send.at[hop],
            recv_sem=recv.at[hop],
            device_id=where,
            device_id_type=pl.DeviceIdType.MESH,
        )
        count = pltpu.make_async_remote_copy(
            src_ref=counts_ref.at[0],
            dst_ref=all_ref.at[me],
            send_sem=count_send.at[hop],
            recv_sem=count_recv.at[hop],
            device_id=where,
            device_id_type=pl.DeviceIdType.MESH,
        )
        return rows, count

    def begin(hop, carry):
        for copy in copies(hop):
            copy.start()
        return carry

    def end(hop, carry):
        for copy in copies(hop):
            copy.wait()
        return carry

    own_rows = pltpu.make_async_copy(buffer_ref.at[me], tiles_ref.at[me], own_sem.at[0])
    own_count = pltpu.make_async_copy(counts_ref.at[0], all_ref.at[me], own_sem.at[1])
    lax.fori_loop(1, devices, begin, 0)
    own_rows.start()
    own_count.start()
    own_rows.wait()
    own_count.wait()
    lax.fori_loop(1, devices, end, 0)


def route(buffer, counts, devices, seq_count):
    capacity, width = buffer.shape[1:]
    lanes = counts.shape[2]
    return pl.pallas_call(
        functools.partial(route_kernel, devices, seq_count),
        in_specs=[pl.BlockSpec(memory_space=pl.ANY)] * 2,
        out_specs=[pl.BlockSpec(memory_space=pl.ANY)] * 2,
        out_shape=(
            jax.ShapeDtypeStruct((devices, capacity, width), BF16),
            jax.ShapeDtypeStruct((devices, 1, lanes), jnp.int32),
        ),
        scratch_shapes=[pltpu.SemaphoreType.DMA((devices,))] * 4
        + [pltpu.SemaphoreType.DMA((2,))],
        compiler_params=pltpu.CompilerParams(collective_id=1, has_side_effects=True),
        name="route",
    )(buffer, counts)


def write_masks(capacity, seq_count, counts_ref, bias_ref, mask_ref):
    devices, lanes = counts_ref.shape
    slots = mask_ref.shape[0]
    half, quarter = slots // 2, slots // 4
    slide = lax.axis_index("slide")
    seq = lax.axis_index("seq")
    core = lax.rem(seq, 2)
    chip = lax.rem(seq // 2, 2)
    base = slide * seq_count + seq - core - 2 * chip
    members = [
        base + core + 2 * chip,
        base + (1 - core) + 2 * chip,
        base + core + 2 * (1 - chip),
        base + (1 - core) + 2 * (1 - chip),
    ]
    counts = counts_ref[...].astype(F32)
    lane = lax.broadcasted_iota(jnp.int32, (devices, lanes), 1)
    columns = [
        jnp.sum(jnp.where(lane == member, counts, 0.0), axis=1, keepdims=True)
        for member in members
    ]
    sender = lax.broadcasted_iota(jnp.int32, (devices, slots), 0) * capacity
    index = lax.broadcasted_iota(jnp.int32, (devices, slots), 1)

    def row(position, reached):
        place = (position - sender).astype(F32)
        inside = jnp.logical_and(place >= 0.0, place < reached)
        return (jnp.sum(inside.astype(F32), axis=0, keepdims=True) - 1.0) * (-MASKED)

    bias_ref[0:1, :] = row(original_of(index, quarter), columns[0])
    within = jnp.where(index >= half, index - half, index)
    for parity in range(2):
        reached = jnp.where(index >= half, columns[1], columns[0])
        bias_ref[1 + parity : 2 + parity, :] = row(
            original_of(within + parity * half, quarter), reached
        )
    for phase in range(4):
        block = (
            (index >= quarter).astype(jnp.int32)
            + (index >= 2 * quarter).astype(jnp.int32)
            + (index >= 3 * quarter).astype(jnp.int32)
        )
        reached = jnp.where(
            index >= half,
            jnp.where(index >= 3 * quarter, columns[3], columns[2]),
            jnp.where(index >= quarter, columns[1], columns[0]),
        )
        bias_ref[3 + phase : 4 + phase, :] = row(4 * (index - quarter * block) + phase, reached)
    bias_ref[7:8, :] = jnp.zeros((1, slots), F32)
    own = (lax.broadcasted_iota(jnp.int32, (8, lanes), 1) == members[0]).astype(F32)
    reached = lax.dot_general(
        own, counts, (((1,), (1,)), ((), ())), preferred_element_type=F32
    )[0:1, :]
    place = (
        lax.broadcasted_iota(jnp.int32, (slots, devices), 0)
        - lax.broadcasted_iota(jnp.int32, (slots, devices), 1) * capacity
    ).astype(F32)
    inside = jnp.logical_and(place >= 0.0, place < reached)
    mask_ref[...] = (jnp.sum(inside.astype(F32), axis=1, keepdims=True) - 1.0) * (-MASKED)


def project_kernel(capacity, seq_count, tiles_ref, gain_ref, counts_ref, weight_ref, out_ref, near_ref, far_ref, normed_ref, bias_ref, mask_ref):
    step = pl.program_id(0)
    slots, width = tiles_ref.shape
    quarter = slots // 4
    half = slots // 2

    @pl.when(step == 0)
    def _():
        tile = tiles_ref[...].astype(F32)
        mean = jnp.mean(tile * tile, axis=1, keepdims=True)
        normed = (tile * lax.rsqrt(mean + EPSILON) * gain_ref[...]).astype(BF16)
        index = lax.broadcasted_iota(jnp.int32, (slots, slots), 0)
        position = lax.broadcasted_iota(jnp.int32, (slots, slots), 1)
        order = (original_of(index, quarter) == position).astype(F32).astype(BF16)
        for start in range(0, width, WIDE):
            normed_ref[:, start : start + WIDE] = jnp.dot(
                order, normed[:, start : start + WIDE], preferred_element_type=F32
            ).astype(BF16)
        write_masks(capacity, seq_count, counts_ref, bias_ref, mask_ref)

    value = jnp.dot(normed_ref[...], weight_ref[...], preferred_element_type=F32).astype(BF16)
    out_ref[...] = value
    for j in range(GROUP):
        cols = slice(j * HEAD, (j + 1) * HEAD)
        near_ref[:, cols] = value[(j % 2) * half : (j % 2 + 1) * half, cols]
        begin = QUARTER_OF[j] * quarter
        far_ref[:, cols] = value[begin : begin + quarter, cols]


def project(tiles, gain, counts, weight, capacity, seq_count):
    slots, width = tiles.shape
    steps = width // WIDE
    whole = lambda i: (0, 0)
    return pl.pallas_call(
        functools.partial(project_kernel, capacity, seq_count),
        grid=(2 * steps,),
        in_specs=[
            pl.BlockSpec((slots, width), whole),
            pl.BlockSpec((1, width), whole),
            pl.BlockSpec(counts.shape, whole),
            pl.BlockSpec((width, WIDE), lambda i: (0, i + steps)),
        ],
        out_specs=[
            pl.BlockSpec((slots, WIDE), lambda i: (0, i)),
            pl.BlockSpec((slots // 2, WIDE), lambda i: (0, i)),
            pl.BlockSpec((slots // 4, WIDE), lambda i: (0, i)),
            pl.BlockSpec((slots, width), whole),
            pl.BlockSpec((8, slots), whole),
            pl.BlockSpec((slots, 1), whole),
        ],
        out_shape=(
            jax.ShapeDtypeStruct((slots, 2 * width), BF16),
            jax.ShapeDtypeStruct((slots // 2, 2 * width), BF16),
            jax.ShapeDtypeStruct((slots // 4, 2 * width), BF16),
            jax.ShapeDtypeStruct((slots, width), BF16),
            jax.ShapeDtypeStruct((8, slots), F32),
            jax.ShapeDtypeStruct((slots, 1), F32),
        ),
        compiler_params=params(),
        name="project",
    )(tiles, gain.reshape(1, width), counts, weight)


def query_kernel(normed_ref, weight_ref, out_ref):
    out_ref[...] = jnp.dot(
        normed_ref[...], weight_ref[...], preferred_element_type=F32
    ).astype(BF16)


def project_query(normed, weight):
    slots, width = normed.shape
    return pl.pallas_call(
        query_kernel,
        grid=(width // WIDE,),
        in_specs=[
            pl.BlockSpec((slots, width), lambda i: (0, 0)),
            pl.BlockSpec((width, WIDE), lambda i: (0, i)),
        ],
        out_specs=pl.BlockSpec((slots, WIDE), lambda i: (0, i)),
        out_shape=jax.ShapeDtypeStruct((slots, width), BF16),
        compiler_params=params(),
        cost_estimate=pl.CostEstimate(
            flops=2 * slots * width * width, bytes_accessed=10_000_000, transcendentals=0
        ),
        name="project_query",
    )(normed, weight)


def softmax_parts(query, keys, values, bias):
    scores = lax.dot_general(
        query, keys, (((1,), (1,)), ((), ())), preferred_element_type=F32
    )
    scores = scores * FACTOR + bias
    peak = jnp.max(scores, axis=1, keepdims=True)
    weights = jnp.exp2(scores - peak)
    total = jnp.sum(weights, axis=1, keepdims=True)
    summed = jnp.dot(weights.astype(BF16), values, preferred_element_type=F32)
    return summed, peak, total


def merge(parts):
    top = parts[0][1]
    for _, peak, _ in parts[1:]:
        top = jnp.maximum(top, peak)
    above, below = 0.0, 0.0
    for summed, peak, total in parts:
        factor = jnp.exp2(peak - top)
        above = above + factor * summed
        below = below + factor * total
    return above, top, below


def ratio(above, below):
    return (above * (1.0 / jnp.maximum(below, 1.0))).astype(BF16)


def near_attention_kernel(
    q_ref, k_ref, v_ref, bias_ref, pair_k, pair_v, mixed_ref, summed_ref, stats_ref, query_ref
):
    slots = q_ref.shape[0]
    half, quarter = slots // 2, slots // 4
    lanes = lax.broadcasted_iota(jnp.int32, (quarter, HEAD), 1)
    stats = jnp.zeros((quarter, HEAD), F32)
    for j in range(GROUP):
        cols = slice(j * HEAD, (j + 1) * HEAD)
        start = (j % 2) * half
        inside = QUARTER_OF[j] * quarter - start
        mine = slice(start, start + half)
        other = slice(half - start, 2 * half - start)
        summed, _, total = softmax_parts(
            q_ref[other, cols], k_ref[:, cols], v_ref[:, cols], bias_ref[0:1, :]
        )
        mixed_ref[other, cols] = ratio(summed, total)
        one = softmax_parts(q_ref[mine, cols], k_ref[:, cols], v_ref[:, cols], bias_ref[0:1, :])
        keys = jnp.concatenate([k_ref[mine, cols], pair_k[:, cols]], axis=0)
        values = jnp.concatenate([v_ref[mine, cols], pair_v[:, cols]], axis=0)
        two = softmax_parts(q_ref[mine, cols], keys, values, bias_ref[1 + j % 2 : 2 + j % 2, :])
        above, top, below = merge([one, two])
        done = quarter - inside
        mixed_ref[start + done : start + done + quarter, cols] = ratio(
            above[done : done + quarter], below[done : done + quarter]
        )
        begin = start + inside
        fourth = slice(begin, begin + quarter)
        within = slice(inside, inside + quarter)
        keys = jnp.concatenate([k_ref[fourth, cols], pair_k[within, cols]], axis=0)
        values = jnp.concatenate([v_ref[fourth, cols], pair_v[within, cols]], axis=0)
        four = softmax_parts(q_ref[fourth, cols], keys, values, bias_ref[3 + j : 4 + j, :half])
        above, top, below = merge([(above[within], top[within], below[within]), four])
        summed_ref[:, cols] = above
        stats = jnp.where(lanes == 2 * j, top, jnp.where(lanes == 2 * j + 1, below, stats))
        query_ref[:, cols] = q_ref[fourth, cols]
        mixed_ref[fourth, cols] = jnp.zeros((quarter, HEAD), BF16)
    stats_ref[...] = stats


def halves(array, steps):
    rows = array.shape[0]
    return [
        pl.BlockSpec((rows, WIDE), lambda i: (0, i)),
        pl.BlockSpec((rows, WIDE), lambda i: (0, i + steps)),
    ]


def near_attention(query, pairs, bias, pair):
    slots, width = query.shape
    quarter = slots // 4
    steps = width // WIDE
    return pl.pallas_call(
        near_attention_kernel,
        grid=(steps,),
        in_specs=[
            pl.BlockSpec((slots, WIDE), lambda i: (0, i)),
            *halves(pairs, steps),
            pl.BlockSpec(bias.shape, lambda i: (0, 0)),
            *halves(pair, steps),
        ],
        out_specs=[
            pl.BlockSpec((slots, WIDE), lambda i: (0, i)),
            pl.BlockSpec((quarter, WIDE), lambda i: (0, i)),
            pl.BlockSpec((quarter, HEAD), lambda i: (0, i)),
            pl.BlockSpec((quarter, WIDE), lambda i: (0, i)),
        ],
        out_shape=(
            jax.ShapeDtypeStruct((slots, width), BF16),
            jax.ShapeDtypeStruct((quarter, width), F32),
            jax.ShapeDtypeStruct((quarter, steps * HEAD), F32),
            jax.ShapeDtypeStruct((quarter, width), BF16),
        ),
        compiler_params=params(SMALL_LIMIT),
        cost_estimate=pl.CostEstimate(
            flops=12 * slots * slots * width,
            bytes_accessed=14_000_000,
            transcendentals=6 * slots * slots * HEADS,
        ),
        name="near_attention",
    )(query, pairs, pairs, bias, pair, pair)


def far_attention_kernel(
    q_ref, bias_ref, one_k, one_v, two_k, two_v, summed_ref, stats_ref, mixed_ref
):
    half = bias_ref.shape[1] // 2
    for j in range(GROUP):
        cols = slice(j * HEAD, (j + 1) * HEAD)
        keys = jnp.concatenate([one_k[:, cols], two_k[:, cols]], axis=0)
        values = jnp.concatenate([one_v[:, cols], two_v[:, cols]], axis=0)
        four = softmax_parts(q_ref[:, cols], keys, values, bias_ref[3 + j : 4 + j, half:])
        before = (
            summed_ref[:, cols],
            stats_ref[:, 2 * j : 2 * j + 1],
            stats_ref[:, 2 * j + 1 : 2 * j + 2],
        )
        above, _, below = merge([before, four])
        mixed_ref[:, cols] = ratio(above, below)


def far_attention(query, bias, one, two, summed, stats):
    quarter, width = query.shape
    steps = width // WIDE
    block = pl.BlockSpec((quarter, WIDE), lambda i: (0, i))
    return pl.pallas_call(
        far_attention_kernel,
        grid=(steps,),
        in_specs=[
            block,
            pl.BlockSpec(bias.shape, lambda i: (0, 0)),
            *halves(one, steps),
            *halves(two, steps),
            block,
            pl.BlockSpec((quarter, HEAD), lambda i: (0, i)),
        ],
        out_specs=block,
        out_shape=jax.ShapeDtypeStruct((quarter, width), BF16),
        compiler_params=params(SMALL_LIMIT),
        name="far_attention",
    )(query, bias, one, one, two, two, summed, stats)


def finish_kernel(mixed_ref, last_ref, tiles_ref, weight_ref, finding_ref, mask_ref, layer_ref, keys_ref, stats_ref, plain_ref):
    slots, width = tiles_ref.shape
    quarter = slots // 4
    position = lax.broadcasted_iota(jnp.int32, (slots, slots), 0)
    index = lax.broadcasted_iota(jnp.int32, (slots, slots), 1)
    order = (original_of(index, quarter) == position).astype(F32).astype(BF16)
    for start in range(0, width, WIDE):
        heads = []
        for j in range(GROUP):
            cols = slice(start + j * HEAD, start + (j + 1) * HEAD)
            begin = QUARTER_OF[j] * quarter
            pieces = [last_ref[:, cols]]
            if begin > 0:
                pieces.insert(0, mixed_ref[:begin, cols])
            if begin + quarter < slots:
                pieces.append(mixed_ref[begin + quarter :, cols])
            heads.append(jnp.concatenate(pieces, axis=0))
        plain_ref[:, start : start + WIDE] = jnp.dot(
            order, jnp.concatenate(heads, axis=1), preferred_element_type=F32
        ).astype(BF16)
    square = jnp.zeros((slots, 1), F32)
    for start in range(0, width, WIDE):
        cols = slice(start, start + WIDE)
        added = jnp.dot(plain_ref[...], weight_ref[:, cols], preferred_element_type=F32)
        out = (tiles_ref[:, cols].astype(F32) + added).astype(BF16)
        layer_ref[:, cols] = out
        wide = out.astype(F32)
        square = square + jnp.sum(wide * wide, axis=1, keepdims=True)
    inverse = lax.rsqrt(square * (1.0 / width) + EPSILON)
    mask = mask_ref[...]
    for h in range(HEADS):
        cols = slice(h * HEAD, (h + 1) * HEAD)
        keys = (layer_ref[:, cols].astype(F32) * inverse).astype(BF16)
        keys_ref[:, cols] = keys
        scores = lax.dot_general(
            keys, finding_ref[:, cols], (((1,), (1,)), ((), ())), preferred_element_type=F32
        )
        scores = scores * FACTOR + mask
        peak = jnp.max(scores, axis=0, keepdims=True)
        stats_ref[h : h + 1, :] = peak
        stats_ref[HEADS + h : HEADS + h + 1, :] = jnp.sum(
            jnp.exp2(scores - peak), axis=0, keepdims=True
        )


def finish(mixed, last, tiles, weight, finding, mask):
    slots, width = tiles.shape
    return pl.pallas_call(
        finish_kernel,
        out_shape=(
            jax.ShapeDtypeStruct((slots, width), BF16),
            jax.ShapeDtypeStruct((slots, width), BF16),
            jax.ShapeDtypeStruct((2 * HEADS, finding.shape[0]), F32),
        ),
        scratch_shapes=[pltpu.VMEM((slots, width), BF16)],
        compiler_params=params(SMALL_LIMIT),
        name="finish",
    )(mixed, last, tiles, weight, finding, mask)


def heat_kernel(count, scale, stats_ref, keys_ref, finding_ref, mask_ref, heat_ref, held, kept, send_sem, recv_sem):
    slide = lax.axis_index("slide")
    me = lax.axis_index("seq")
    barrier = pltpu.get_barrier_semaphore()
    for hop in range(1, count):
        peer = lax.rem(me + hop, count)
        pl.semaphore_signal(
            barrier, inc=1, device_id=(slide, peer), device_id_type=pl.DeviceIdType.MESH
        )
    pl.semaphore_wait(barrier, count - 1)
    copies = []
    for hop in range(1, count):
        peer = lax.rem(me + hop, count)
        copy = pltpu.make_async_remote_copy(
            src_ref=stats_ref,
            dst_ref=held.at[hop],
            send_sem=send_sem.at[hop],
            recv_sem=recv_sem.at[hop],
            device_id=(slide, peer),
            device_id_type=pl.DeviceIdType.MESH,
        )
        copy.start()
        copies.append(copy)
    mask = mask_ref[...]
    for h in range(HEADS):
        cols = slice(h * HEAD, (h + 1) * HEAD)
        scores = lax.dot_general(
            keys_ref[:, cols], finding_ref[:, cols], (((1,), (1,)), ((), ())),
            preferred_element_type=F32,
        )
        kept[h] = jnp.exp2(scores * FACTOR + mask - stats_ref[h : h + 1, :])
    for copy in copies:
        copy.wait()
    everything = [stats_ref[...]] + [held[hop] for hop in range(1, count)]
    peaks = everything[0][:HEADS]
    for part in everything[1:]:
        peaks = jnp.maximum(peaks, part[:HEADS])
    totals = jnp.zeros_like(peaks)
    for part in everything:
        totals = totals + part[HEADS:] * jnp.exp2(part[:HEADS] - peaks)
    factors = jnp.exp2(everything[0][:HEADS] - peaks) * (scale / totals)
    slots = keys_ref.shape[0]
    chunk = 64
    for start in range(0, slots, chunk):
        rows = slice(start, start + chunk)
        total = kept[0, rows, :] * factors[0:1]
        for h in range(1, HEADS):
            total = total + kept[h, rows, :] * factors[h : h + 1]
        heat_ref[rows, :] = total


def heat_map(count, stats, keys, finding, mask):
    slots = keys.shape[0]
    finds = finding.shape[0]
    return pl.pallas_call(
        functools.partial(heat_kernel, count, count * slots / HEADS),
        in_specs=[pl.BlockSpec(memory_space=pltpu.VMEM)] * 4,
        out_specs=pl.BlockSpec(memory_space=pltpu.VMEM),
        out_shape=jax.ShapeDtypeStruct((slots, finds), F32),
        scratch_shapes=[
            pltpu.VMEM((count, 2 * HEADS, finds), F32),
            pltpu.VMEM((HEADS, slots, finds), F32),
            pltpu.SemaphoreType.DMA((count,)),
            pltpu.SemaphoreType.DMA((count,)),
        ],
        compiler_params=params(SMALL_LIMIT, collective_id=0, has_side_effects=True),
        name="heat_map",
    )(stats, keys, finding, mask)


def exchange(value, mask):
    pairs = [(source, source ^ mask) for source in range(lax.axis_size("seq"))]
    return lax.ppermute(value, "seq", pairs)


def shards(embeds, destination, norm_gain, qkv_weight, out_weight, finding_queries):
    devices = lax.axis_size(("slide", "seq"))
    seq_count = lax.axis_size("seq")
    slots = embeds.shape[0] * 2
    capacity = slots // devices
    padded = -(-capacity // 8) * 8
    width = embeds.shape[1]
    buffer, counts = dispatch(destination, embeds, devices, padded)
    received, counts = route(
        buffer.reshape(devices, padded, width), counts[None], devices, seq_count
    )
    tiles = received[:, :capacity].reshape(slots, width)
    pairs, near, far, normed, bias, mask = project(
        tiles, norm_gain, counts[:, 0], qkv_weight, capacity, seq_count
    )
    one = exchange(far, 2)
    pair = exchange(near, 1)
    query = project_query(normed, qkv_weight)
    mixed, summed, stats, quarter_query = near_attention(query, pairs, bias, pair)
    one, mixed = lax.optimization_barrier((one, mixed))
    two = exchange(one, 1)
    last = far_attention(quarter_query, bias, one, two, summed, stats)
    layer_out, keys, stats = finish(mixed, last, tiles, out_weight, finding_queries, mask)
    heat = heat_map(seq_count, stats, keys, finding_queries, mask)
    return (layer_out, heat)


def split(index, size):
    block = ((index.astype(F32) + 0.5) * (1.0 / size)).astype(jnp.int32)
    return block, index - block * size


def chunk_position(index, quarter):
    block, inner = split(index, quarter)
    phase = 2 * jnp.where((block == 1) | (block == 3), 1, 0) + (block >= 2).astype(jnp.int32)
    return 4 * inner + phase


def chunk_masks(capacity, chunk, seq_count, counts, bias_ref, mask_ref):
    devices, lanes = counts.shape
    slots = mask_ref.shape[0]
    half, quarter = chunk // 2, chunk // 4
    slide = lax.axis_index("slide")
    seq = lax.axis_index("seq")
    core = lax.rem(seq, 2)
    chip = lax.rem(seq // 2, 2)
    base = slide * seq_count + seq - core - 2 * chip
    members = [
        base + core + 2 * chip,
        base + (1 - core) + 2 * chip,
        base + core + 2 * (1 - chip),
        base + (1 - core) + 2 * (1 - chip),
    ]
    counts = counts.astype(F32)
    lane = lax.broadcasted_iota(jnp.int32, (devices, lanes), 1)
    columns = [
        jnp.sum(jnp.where(lane == member, counts, 0.0), axis=1, keepdims=True)
        for member in members
    ]
    sender = lax.broadcasted_iota(jnp.int32, (devices, slots), 0) * capacity
    index = lax.broadcasted_iota(jnp.int32, (1, slots), 1)

    def row(position, reached):
        place = (position - sender).astype(F32)
        inside = jnp.logical_and(place >= 0.0, place < reached)
        return (jnp.sum(inside.astype(F32), axis=0, keepdims=True) - 1.0) * (-MASKED)

    part, inner = split(index, chunk)
    bias_ref[0:1, :] = row(chunk * part + chunk_position(inner, quarter), columns[0])
    member, within = split(index, slots // 2)
    part, inner = split(within, half)
    sub, inner = split(inner, quarter)
    reached = jnp.where(member > 0, columns[1], columns[0])
    for parity in range(2):
        bias_ref[1 + parity : 2 + parity, :] = row(
            chunk * part + 4 * inner + parity + 2 * sub, reached
        )
    member, within = split(index, slots // 4)
    part, inner = split(within, quarter)
    reached = jnp.where(
        member >= 2,
        jnp.where(member == 3, columns[3], columns[2]),
        jnp.where(member == 1, columns[1], columns[0]),
    )
    for phase in range(4):
        bias_ref[3 + phase : 4 + phase, :] = row(chunk * part + 4 * inner + phase, reached)
    bias_ref[7:8, :] = jnp.zeros((1, slots), F32)
    own = (lax.broadcasted_iota(jnp.int32, (8, lanes), 1) == members[0]).astype(F32)
    reached = lax.dot_general(
        own, counts, (((1,), (1,)), ((), ())), preferred_element_type=F32
    )[0:1, :]
    place = (
        lax.broadcasted_iota(jnp.int32, (slots, devices), 0)
        - lax.broadcasted_iota(jnp.int32, (slots, devices), 1) * capacity
    ).astype(F32)
    inside = jnp.logical_and(place >= 0.0, place < reached)
    mask_ref[...] = (jnp.sum(inside.astype(F32), axis=1, keepdims=True) - 1.0) * (-MASKED)


def gather_kernel(
    capacity, slides, seq_count,
    row_ref, embeds_ref, gain_ref, weight_ref,
    tiles_ref, query_ref, keys_ref, pair_ref, far_ref, bias_ref, mask_ref,
    sending, received, counts_ref, all_ref, weight, tiles, query, keys, near, far, normed_ref,
    send, recv, count_send, count_recv, own_sem, weight_sem, near_send, near_recv, out_sem,
):
    rows, width = embeds_ref.shape
    devices = slides * seq_count
    chunk = seq_count * capacity
    half, quarter = chunk // 2, chunk // 4
    lanes = counts_ref.shape[1]
    slide = lax.axis_index("slide")
    seq = lax.axis_index("seq")
    me = slide * seq_count + seq
    other = seq + 1 - 2 * lax.rem(seq, 2)
    barrier = pltpu.get_barrier_semaphore()

    def place_of(hop):
        return (lax.rem(slide + hop // seq_count, slides), lax.rem(seq + lax.rem(hop, seq_count), seq_count))

    def greet(hop, carry):
        pl.semaphore_signal(
            barrier, inc=1, device_id=place_of(hop), device_id_type=pl.DeviceIdType.MESH
        )
        return carry

    lax.fori_loop(1, devices, greet, 0)
    load = pltpu.make_async_copy(weight_ref, weight, weight_sem)
    load.start()

    row = row_ref[...]
    col = jnp.transpose(jnp.broadcast_to(row.astype(F32), (128, rows)))[:, 0:1].astype(jnp.int32)
    first = lax.broadcasted_iota(jnp.int32, (rows, rows), 0)
    second = lax.broadcasted_iota(jnp.int32, (rows, rows), 1)
    same = jnp.logical_and(col == row, first < second)
    rank = jnp.sum(same.astype(F32), axis=0, keepdims=True).astype(jnp.int32)
    place = row * capacity + rank
    lane = lax.broadcasted_iota(jnp.int32, (rows, lanes), 1)
    tally = jnp.sum((col == lane).astype(F32), axis=0, keepdims=True).astype(jnp.int32)
    counts_ref[...] = jnp.broadcast_to(tally, counts_ref.shape)

    def count_copy(hop):
        return pltpu.make_async_remote_copy(
            src_ref=counts_ref,
            dst_ref=all_ref.at[me],
            send_sem=count_send.at[hop],
            recv_sem=count_recv.at[hop],
            device_id=place_of(hop),
            device_id_type=pl.DeviceIdType.MESH,
        )

    def row_copy(hop):
        where = place_of(hop)
        return pltpu.make_async_remote_copy(
            src_ref=sending.at[where[0] * seq_count + where[1]],
            dst_ref=received.at[me],
            send_sem=send.at[hop],
            recv_sem=recv.at[hop],
            device_id=where,
            device_id_type=pl.DeviceIdType.MESH,
        )

    def each(make, method, low, high):
        def step(hop, carry):
            getattr(make(hop), method)()
            return carry

        lax.fori_loop(low, high, step, 0)

    def fill(k):
        column = lax.rem(slide + k, slides)
        wanted = lax.broadcasted_iota(jnp.int32, (chunk, rows), 0) + column * chunk
        chosen = (wanted == place).astype(F32).astype(BF16)
        for start in range(0, width, WIDE):
            part = jnp.dot(
                chosen, embeds_ref[:, start : start + WIDE], preferred_element_type=F32
            )
            sending[pl.ds(column * seq_count, seq_count), :, start : start + WIDE] = part.reshape(
                seq_count, capacity, WIDE
            ).astype(BF16)

    fill(0)
    pl.semaphore_wait(barrier, devices - 1)
    each(count_copy, "start", 1, devices)
    each(row_copy, "start", 1, seq_count)
    own = pltpu.make_async_copy(sending.at[me], received.at[me], own_sem)
    own.start()
    all_ref[pl.ds(me, 1)] = counts_ref[...][None]

    def fill_next(k, carry):
        fill(k)
        each(row_copy, "start", k * seq_count, (k + 1) * seq_count)
        return carry

    lax.fori_loop(1, slides, fill_next, 0)
    each(count_copy, "wait", 1, devices)
    chunk_masks(capacity, chunk, seq_count, jnp.max(all_ref[...], axis=1), bias_ref, mask_ref)

    def near_copy(c):
        part = pl.ds(pl.multiple_of(c * half, half), half)
        return pltpu.make_async_remote_copy(
            src_ref=near.at[part],
            dst_ref=pair_ref.at[part],
            send_sem=near_send.at[c],
            recv_sem=near_recv.at[c],
            device_id=(slide, other),
            device_id_type=pl.DeviceIdType.MESH,
        )

    def out_copies(c):
        part = pl.ds(pl.multiple_of(c * chunk, chunk), chunk)
        small = pl.ds(pl.multiple_of(c * quarter, quarter), quarter)
        return [
            pltpu.make_async_copy(tiles.at[part], tiles_ref.at[part], out_sem.at[0, c]),
            pltpu.make_async_copy(keys.at[part], keys_ref.at[part], out_sem.at[1, c]),
            pltpu.make_async_copy(far.at[small], far_ref.at[small], out_sem.at[2, c]),
            pltpu.make_async_copy(query.at[part], query_ref.at[part], out_sem.at[3, c]),
        ]

    def work(k):
        c = lax.rem(slide - k + slides, slides)
        part = pl.ds(pl.multiple_of(c * chunk, chunk), chunk)
        group = pl.ds(c * seq_count, seq_count)
        square = jnp.zeros((chunk, 1), F32)
        for start in range(0, width, WIDE):
            tile = received[group, :, start : start + WIDE].astype(F32).reshape(chunk, WIDE)
            tiles[part, start : start + WIDE] = tile.astype(BF16)
            square = square + jnp.sum(tile * tile, axis=1, keepdims=True)
        inverse = lax.rsqrt(square * (1.0 / width) + EPSILON)
        index = lax.broadcasted_iota(jnp.int32, (chunk, 1), 0)
        position = lax.broadcasted_iota(jnp.int32, (chunk, chunk), 1)
        order = (chunk_position(index, quarter) == position).astype(F32).astype(BF16)
        for start in range(0, width, WIDE):
            tile = received[group, :, start : start + WIDE].astype(F32).reshape(chunk, WIDE)
            normed = (tile * inverse * gain_ref[:, start : start + WIDE]).astype(BF16)
            normed_ref[:, start : start + WIDE] = jnp.dot(
                order, normed, preferred_element_type=F32
            ).astype(BF16)

        def pairs(g, carry):
            at = pl.multiple_of(g * WIDE, WIDE)
            value = jnp.dot(
                normed_ref[...], weight[:, pl.ds(at + width, WIDE)], preferred_element_type=F32
            ).astype(BF16)
            keys[part, pl.ds(at, WIDE)] = value
            for j in range(GROUP):
                cols = pl.ds(at + j * HEAD, HEAD)
                begin = (j % 2) * half
                near[pl.ds(pl.multiple_of(c * half, half), half), cols] = value[
                    begin : begin + half, j * HEAD : (j + 1) * HEAD
                ]
                begin = QUARTER_OF[j] * quarter
                far[pl.ds(pl.multiple_of(c * quarter, quarter), quarter), cols] = value[
                    begin : begin + quarter, j * HEAD : (j + 1) * HEAD
                ]
            return carry

        def single(g, carry):
            at = pl.multiple_of(g * WIDE, WIDE)
            query[part, pl.ds(at, WIDE)] = jnp.dot(
                normed_ref[...], weight[:, pl.ds(at, WIDE)], preferred_element_type=F32
            ).astype(BF16)
            return carry

        lax.fori_loop(0, 2 * width // WIDE, pairs, 0)
        near_copy(c).start()
        copies = out_copies(c)
        for copy in copies[:3]:
            copy.start()
        lax.fori_loop(0, width // WIDE, single, 0)
        copies[3].start()

    own.wait()
    load.wait()

    def step(k, carry):
        each(row_copy, "wait_recv", jnp.maximum(k * seq_count, 1), (k + 1) * seq_count)
        work(k)
        return carry

    lax.fori_loop(0, slides, step, 0)
    each(row_copy, "wait_send", 1, devices)

    def end(c, carry):
        near_copy(c).wait()
        for copy in out_copies(c):
            copy.wait()
        return carry

    lax.fori_loop(0, slides, end, 0)


def gather(destination, embeds, gain, weight, capacity, slides, seq_count):
    rows, width = embeds.shape
    devices = slides * seq_count
    slots = devices * capacity
    chunk = seq_count * capacity
    lanes = max(128, devices)
    vmem = pl.BlockSpec(memory_space=pltpu.VMEM)
    anywhere = pl.BlockSpec(memory_space=pl.ANY)
    dma = pltpu.SemaphoreType.DMA
    return pl.pallas_call(
        functools.partial(gather_kernel, capacity, slides, seq_count),
        in_specs=[vmem, vmem, vmem, anywhere],
        out_specs=[anywhere] * 5 + [vmem] * 2,
        out_shape=(
            jax.ShapeDtypeStruct((slots, width), BF16),
            jax.ShapeDtypeStruct((slots, width), BF16),
            jax.ShapeDtypeStruct((slots, 2 * width), BF16),
            jax.ShapeDtypeStruct((slots // 2, 2 * width), BF16),
            jax.ShapeDtypeStruct((slots // 4, 2 * width), BF16),
            jax.ShapeDtypeStruct((8, slots), F32),
            jax.ShapeDtypeStruct((slots, 1), F32),
        ),
        scratch_shapes=[
            pltpu.VMEM((devices, capacity, width), BF16),
            pltpu.VMEM((devices, capacity, width), BF16),
            pltpu.VMEM((8, lanes), jnp.int32),
            pltpu.VMEM((devices, 8, lanes), jnp.int32),
            pltpu.VMEM(weight.shape, BF16),
            pltpu.VMEM((slots, width), BF16),
            pltpu.VMEM((slots, width), BF16),
            pltpu.VMEM((slots, 2 * width), BF16),
            pltpu.VMEM((slots // 2, 2 * width), BF16),
            pltpu.VMEM((slots // 4, 2 * width), BF16),
            pltpu.VMEM((chunk, width), BF16),
            dma((devices,)),
            dma((devices,)),
            dma((devices,)),
            dma((devices,)),
            dma,
            dma,
            dma((slides,)),
            dma((slides,)),
            dma((4, slides)),
        ],
        compiler_params=params(collective_id=2, has_side_effects=True),
        cost_estimate=pl.CostEstimate(
            flops=6 * slots * width * width, bytes_accessed=100_000_000, transcendentals=0
        ),
        name="gather",
    )(destination.reshape(1, rows), embeds, gain.reshape(1, width), weight)


def pick(ref, parts, start, size, cols):
    step = ref.shape[0] // parts
    return jnp.concatenate(
        [ref[c * step + start : c * step + start + size, cols] for c in range(parts)], axis=0
    )


def pick_rows(value, parts, start, size):
    step = value.shape[0] // parts
    return jnp.concatenate(
        [value[c * step + start : c * step + start + size] for c in range(parts)], axis=0
    )


def put(ref, parts, start, cols, value):
    step, size = ref.shape[0] // parts, value.shape[0] // parts
    for c in range(parts):
        ref[c * step + start : c * step + start + size, cols] = value[c * size : (c + 1) * size]


def chunk_attention_kernel(
    parts, q_ref, k_ref, v_ref, bias_ref, pair_k, pair_v, mixed_ref, summed_ref, stats_ref, query_ref
):
    slots = q_ref.shape[0]
    count = slots // 4
    half, quarter = slots // parts // 2, slots // parts // 4
    lanes = lax.broadcasted_iota(jnp.int32, (count, HEAD), 1)
    stats = jnp.zeros((count, HEAD), F32)
    for j in range(GROUP):
        cols = slice(j * HEAD, (j + 1) * HEAD)
        start = (j % 2) * half
        inside = QUARTER_OF[j] * quarter - start
        summed, _, total = softmax_parts(
            pick(q_ref, parts, half - start, half, cols), k_ref[:, cols], v_ref[:, cols], bias_ref[0:1, :]
        )
        put(mixed_ref, parts, half - start, cols, ratio(summed, total))
        mine = pick(q_ref, parts, start, half, cols)
        one = softmax_parts(mine, k_ref[:, cols], v_ref[:, cols], bias_ref[0:1, :])
        keys = jnp.concatenate([pick(k_ref, parts, start, half, cols), pair_k[:, cols]], axis=0)
        values = jnp.concatenate([pick(v_ref, parts, start, half, cols), pair_v[:, cols]], axis=0)
        two = softmax_parts(mine, keys, values, bias_ref[1 + j % 2 : 2 + j % 2, :])
        above, top, below = merge([one, two])
        done = quarter - inside
        put(
            mixed_ref, parts, start + done, cols,
            ratio(pick_rows(above, parts, done, quarter), pick_rows(below, parts, done, quarter)),
        )
        fourth = pick(q_ref, parts, start + inside, quarter, cols)
        keys = jnp.concatenate(
            [pick(k_ref, parts, start + inside, quarter, cols), pick(pair_k, parts, inside, quarter, cols)], axis=0
        )
        values = jnp.concatenate(
            [pick(v_ref, parts, start + inside, quarter, cols), pick(pair_v, parts, inside, quarter, cols)], axis=0
        )
        four = softmax_parts(fourth, keys, values, bias_ref[3 + j : 4 + j, : slots // 2])
        before = tuple(pick_rows(value, parts, inside, quarter) for value in (above, top, below))
        above, top, below = merge([before, four])
        summed_ref[:, cols] = above
        stats = jnp.where(lanes == 2 * j, top, jnp.where(lanes == 2 * j + 1, below, stats))
        query_ref[:, cols] = fourth
        put(mixed_ref, parts, start + inside, cols, jnp.zeros((count, HEAD), BF16))
    stats_ref[...] = stats


def chunk_attention(query, pairs, bias, pair, parts):
    slots, width = query.shape
    quarter = slots // 4
    steps = width // WIDE
    return pl.pallas_call(
        functools.partial(chunk_attention_kernel, parts),
        grid=(steps,),
        in_specs=[
            pl.BlockSpec((slots, WIDE), lambda i: (0, i)),
            *halves(pairs, steps),
            pl.BlockSpec(bias.shape, lambda i: (0, 0)),
            *halves(pair, steps),
        ],
        out_specs=[
            pl.BlockSpec((slots, WIDE), lambda i: (0, i)),
            pl.BlockSpec((quarter, WIDE), lambda i: (0, i)),
            pl.BlockSpec((quarter, HEAD), lambda i: (0, i)),
            pl.BlockSpec((quarter, WIDE), lambda i: (0, i)),
        ],
        out_shape=(
            jax.ShapeDtypeStruct((slots, width), BF16),
            jax.ShapeDtypeStruct((quarter, width), F32),
            jax.ShapeDtypeStruct((quarter, steps * HEAD), F32),
            jax.ShapeDtypeStruct((quarter, width), BF16),
        ),
        compiler_params=params(SMALL_LIMIT),
        cost_estimate=pl.CostEstimate(
            flops=12 * slots * slots * width,
            bytes_accessed=14_000_000,
            transcendentals=6 * slots * slots * HEADS,
        ),
        name="chunk_attention",
    )(query, pairs, pairs, bias, pair, pair)


def chunk_finish_kernel(parts, mixed_ref, last_ref, tiles_ref, weight_ref, finding_ref, mask_ref, layer_ref, keys_ref, stats_ref, plain_ref):
    slots, width = tiles_ref.shape
    chunk = slots // parts
    quarter = chunk // 4
    position = lax.broadcasted_iota(jnp.int32, (chunk, chunk), 0)
    index = lax.broadcasted_iota(jnp.int32, (1, chunk), 1)
    order = (chunk_position(index, quarter) == position).astype(F32).astype(BF16)
    for c in range(parts):
        base = c * chunk
        for start in range(0, width, WIDE):
            heads = []
            for j in range(GROUP):
                cols = slice(start + j * HEAD, start + (j + 1) * HEAD)
                begin = QUARTER_OF[j] * quarter
                pieces = [last_ref[c * quarter : (c + 1) * quarter, cols]]
                if begin > 0:
                    pieces.insert(0, mixed_ref[base : base + begin, cols])
                if begin + quarter < chunk:
                    pieces.append(mixed_ref[base + begin + quarter : base + chunk, cols])
                heads.append(jnp.concatenate(pieces, axis=0))
            plain_ref[base : base + chunk, start : start + WIDE] = jnp.dot(
                order, jnp.concatenate(heads, axis=1), preferred_element_type=F32
            ).astype(BF16)
    square = jnp.zeros((slots, 1), F32)
    for start in range(0, width, WIDE):
        cols = slice(start, start + WIDE)
        added = jnp.dot(plain_ref[...], weight_ref[:, cols], preferred_element_type=F32)
        out = (tiles_ref[:, cols].astype(F32) + added).astype(BF16)
        layer_ref[:, cols] = out
        wide = out.astype(F32)
        square = square + jnp.sum(wide * wide, axis=1, keepdims=True)
    inverse = lax.rsqrt(square * (1.0 / width) + EPSILON)
    mask = mask_ref[...]
    for h in range(HEADS):
        cols = slice(h * HEAD, (h + 1) * HEAD)
        keys = (layer_ref[:, cols].astype(F32) * inverse).astype(BF16)
        keys_ref[:, cols] = keys
        scores = lax.dot_general(
            keys, finding_ref[:, cols], (((1,), (1,)), ((), ())), preferred_element_type=F32
        )
        scores = scores * FACTOR + mask
        peak = jnp.max(scores, axis=0, keepdims=True)
        stats_ref[h : h + 1, :] = peak
        stats_ref[HEADS + h : HEADS + h + 1, :] = jnp.sum(
            jnp.exp2(scores - peak), axis=0, keepdims=True
        )


def chunk_finish(mixed, last, tiles, weight, finding, mask, parts):
    slots, width = tiles.shape
    return pl.pallas_call(
        functools.partial(chunk_finish_kernel, parts),
        out_shape=(
            jax.ShapeDtypeStruct((slots, width), BF16),
            jax.ShapeDtypeStruct((slots, width), BF16),
            jax.ShapeDtypeStruct((2 * HEADS, finding.shape[0]), F32),
        ),
        scratch_shapes=[pltpu.VMEM((slots, width), BF16)],
        compiler_params=params(SMALL_LIMIT),
        name="chunk_finish",
    )(mixed, last, tiles, weight, finding, mask)


def chunk_shards(embeds, destination, norm_gain, qkv_weight, out_weight, finding_queries):
    slides = lax.axis_size("slide")
    seq_count = lax.axis_size("seq")
    slots = embeds.shape[0] * 2
    capacity = slots // (slides * seq_count)
    tiles, query, pairs, pair, far, bias, mask = gather(
        destination, embeds, norm_gain, qkv_weight, capacity, slides, seq_count
    )
    one = exchange(far, 2)
    mixed, summed, stats, quarter_query = chunk_attention(query, pairs, bias, pair, slides)
    one, mixed = lax.optimization_barrier((one, mixed))
    two = exchange(one, 1)
    last = far_attention(quarter_query, bias, one, two, summed, stats)
    layer_out, keys, stats = chunk_finish(
        mixed, last, tiles, out_weight, finding_queries, mask, slides
    )
    heat = heat_map(seq_count, stats, keys, finding_queries, mask)
    return (layer_out, heat)


def solution(mesh):
    in_specs = (P(("slide", "seq"), None), P(("slide", "seq"), None), P(), P(), P(), P())
    out_specs = (P(("slide", "seq"), None), P(("slide", "seq"), None))

    def program(embeds, *rest):
        devices = mesh.shape["slide"] * mesh.shape["seq"]
        capacity = embeds.shape[0] * 2 // devices // devices
        chunk = capacity * mesh.shape["seq"]
        body = chunk_shards if capacity % 8 == 0 and chunk % 64 == 0 else shards
        return jax.shard_map(
            body, mesh=mesh, in_specs=in_specs, out_specs=out_specs, check_vma=False
        )(embeds, *rest)

    return program
```

```python
import functools
import math

import jax
import jax.numpy as jnp
from jax import lax
from jax.experimental import pallas as pl
from jax.experimental.pallas import tpu as pltpu
from jax.sharding import PartitionSpec as P

HEADS = 12
HEAD = 128
GROUP = 4
WIDE = GROUP * HEAD
MASKED = -1e30
EPSILON = 1e-06
FACTOR = math.log2(math.e) / math.sqrt(HEAD)
F32 = jnp.float32
BF16 = jnp.bfloat16
QUARTER_OF = (0, 2, 1, 3)
VMEM_LIMIT = 56 * 1024 * 1024
SMALL_LIMIT = 34 * 1024 * 1024


def params(limit=VMEM_LIMIT, **more):
    return pltpu.CompilerParams(vmem_limit_bytes=limit, **more)


def dispatch_kernel(capacity, row_ref, embeds_ref, buffer_ref, counts_ref):
    rows = embeds_ref.shape[0]
    slots = buffer_ref.shape[0]
    row = row_ref[...]
    col = jnp.transpose(jnp.broadcast_to(row.astype(F32), (128, rows)))[:, 0:1].astype(jnp.int32)
    first = lax.broadcasted_iota(jnp.int32, (rows, rows), 0)
    second = lax.broadcasted_iota(jnp.int32, (rows, rows), 1)
    same = jnp.logical_and(col == row, first < second)
    rank = jnp.sum(same.astype(F32), axis=0, keepdims=True).astype(jnp.int32)
    place = row * capacity + rank
    lanes = lax.broadcasted_iota(jnp.int32, (rows, counts_ref.shape[1]), 1)
    counts_ref[...] = jnp.sum((col == lanes).astype(F32), axis=0, keepdims=True).astype(jnp.int32)
    chosen = (lax.broadcasted_iota(jnp.int32, (slots, rows), 0) == place).astype(F32).astype(BF16)
    for start in range(0, embeds_ref.shape[1], WIDE):
        part = embeds_ref[:, start : start + WIDE]
        buffer_ref[:, start : start + WIDE] = jnp.dot(
            chosen, part, preferred_element_type=F32
        ).astype(BF16)


def dispatch(destination, embeds, devices, capacity):
    rows, width = embeds.shape
    slots = devices * capacity
    return pl.pallas_call(
        functools.partial(dispatch_kernel, capacity),
        out_shape=(
            jax.ShapeDtypeStruct((slots, width), BF16),
            jax.ShapeDtypeStruct((1, max(128, devices)), jnp.int32),
        ),
        compiler_params=params(),
        name="dispatch",
    )(destination.reshape(1, rows), embeds)


def original_of(index, quarter):
    block = (
        (index >= quarter).astype(jnp.int32)
        + (index >= 2 * quarter).astype(jnp.int32)
        + (index >= 3 * quarter).astype(jnp.int32)
    )
    phase = 2 * jnp.where((block == 1) | (block == 3), 1, 0) + (block >= 2).astype(jnp.int32)
    return 4 * (index - quarter * block) + phase


def route_kernel(devices, seq_count, buffer_ref, counts_ref, tiles_ref, all_ref, send, recv, count_send, count_recv, own_sem):
    me = lax.axis_index("slide") * seq_count + lax.axis_index("seq")
    barrier = pltpu.get_barrier_semaphore()

    def place_of(hop):
        peer = lax.rem(me + hop, devices)
        return peer, (peer // seq_count, lax.rem(peer, seq_count))

    def greet(hop, carry):
        pl.semaphore_signal(
            barrier, inc=1, device_id=place_of(hop)[1], device_id_type=pl.DeviceIdType.MESH
        )
        return carry

    lax.fori_loop(1, devices, greet, 0)
    pl.semaphore_wait(barrier, devices - 1)

    def copies(hop):
        peer, where = place_of(hop)
        rows = pltpu.make_async_remote_copy(
            src_ref=buffer_ref.at[peer],
            dst_ref=tiles_ref.at[me],
            send_sem=send.at[hop],
            recv_sem=recv.at[hop],
            device_id=where,
            device_id_type=pl.DeviceIdType.MESH,
        )
        count = pltpu.make_async_remote_copy(
            src_ref=counts_ref.at[0],
            dst_ref=all_ref.at[me],
            send_sem=count_send.at[hop],
            recv_sem=count_recv.at[hop],
            device_id=where,
            device_id_type=pl.DeviceIdType.MESH,
        )
        return rows, count

    def begin(hop, carry):
        for copy in copies(hop):
            copy.start()
        return carry

    def end(hop, carry):
        for copy in copies(hop):
            copy.wait()
        return carry

    own_rows = pltpu.make_async_copy(buffer_ref.at[me], tiles_ref.at[me], own_sem.at[0])
    own_count = pltpu.make_async_copy(counts_ref.at[0], all_ref.at[me], own_sem.at[1])
    lax.fori_loop(1, devices, begin, 0)
    own_rows.start()
    own_count.start()
    own_rows.wait()
    own_count.wait()
    lax.fori_loop(1, devices, end, 0)


def route(buffer, counts, devices, seq_count):
    capacity, width = buffer.shape[1:]
    lanes = counts.shape[2]
    return pl.pallas_call(
        functools.partial(route_kernel, devices, seq_count),
        in_specs=[pl.BlockSpec(memory_space=pl.ANY)] * 2,
        out_specs=[pl.BlockSpec(memory_space=pl.ANY)] * 2,
        out_shape=(
            jax.ShapeDtypeStruct((devices, capacity, width), BF16),
            jax.ShapeDtypeStruct((devices, 1, lanes), jnp.int32),
        ),
        scratch_shapes=[pltpu.SemaphoreType.DMA((devices,))] * 4
        + [pltpu.SemaphoreType.DMA((2,))],
        compiler_params=pltpu.CompilerParams(collective_id=1, has_side_effects=True),
        name="route",
    )(buffer, counts)


def write_masks(capacity, seq_count, counts_ref, bias_ref, mask_ref):
    devices, lanes = counts_ref.shape
    slots = mask_ref.shape[0]
    half, quarter = slots // 2, slots // 4
    slide = lax.axis_index("slide")
    seq = lax.axis_index("seq")
    core = lax.rem(seq, 2)
    chip = lax.rem(seq // 2, 2)
    base = slide * seq_count + seq - core - 2 * chip
    members = [
        base + core + 2 * chip,
        base + (1 - core) + 2 * chip,
        base + core + 2 * (1 - chip),
        base + (1 - core) + 2 * (1 - chip),
    ]
    counts = counts_ref[...].astype(F32)
    lane = lax.broadcasted_iota(jnp.int32, (devices, lanes), 1)
    columns = [
        jnp.sum(jnp.where(lane == member, counts, 0.0), axis=1, keepdims=True)
        for member in members
    ]
    sender = lax.broadcasted_iota(jnp.int32, (devices, slots), 0) * capacity
    index = lax.broadcasted_iota(jnp.int32, (devices, slots), 1)

    def row(position, reached):
        place = (position - sender).astype(F32)
        inside = jnp.logical_and(place >= 0.0, place < reached)
        return (jnp.sum(inside.astype(F32), axis=0, keepdims=True) - 1.0) * (-MASKED)

    bias_ref[0:1, :] = row(original_of(index, quarter), columns[0])
    within = jnp.where(index >= half, index - half, index)
    for parity in range(2):
        reached = jnp.where(index >= half, columns[1], columns[0])
        bias_ref[1 + parity : 2 + parity, :] = row(
            original_of(within + parity * half, quarter), reached
        )
    for phase in range(4):
        block = (
            (index >= quarter).astype(jnp.int32)
            + (index >= 2 * quarter).astype(jnp.int32)
            + (index >= 3 * quarter).astype(jnp.int32)
        )
        reached = jnp.where(
            index >= half,
            jnp.where(index >= 3 * quarter, columns[3], columns[2]),
            jnp.where(index >= quarter, columns[1], columns[0]),
        )
        bias_ref[3 + phase : 4 + phase, :] = row(4 * (index - quarter * block) + phase, reached)
    bias_ref[7:8, :] = jnp.zeros((1, slots), F32)
    own = (lax.broadcasted_iota(jnp.int32, (8, lanes), 1) == members[0]).astype(F32)
    reached = lax.dot_general(
        own, counts, (((1,), (1,)), ((), ())), preferred_element_type=F32
    )[0:1, :]
    place = (
        lax.broadcasted_iota(jnp.int32, (slots, devices), 0)
        - lax.broadcasted_iota(jnp.int32, (slots, devices), 1) * capacity
    ).astype(F32)
    inside = jnp.logical_and(place >= 0.0, place < reached)
    mask_ref[...] = (jnp.sum(inside.astype(F32), axis=1, keepdims=True) - 1.0) * (-MASKED)


def project_kernel(capacity, seq_count, tiles_ref, gain_ref, counts_ref, weight_ref, out_ref, near_ref, far_ref, normed_ref, bias_ref, mask_ref):
    step = pl.program_id(0)
    slots, width = tiles_ref.shape
    quarter = slots // 4
    half = slots // 2

    @pl.when(step == 0)
    def _():
        tile = tiles_ref[...].astype(F32)
        mean = jnp.mean(tile * tile, axis=1, keepdims=True)
        normed = (tile * lax.rsqrt(mean + EPSILON) * gain_ref[...]).astype(BF16)
        index = lax.broadcasted_iota(jnp.int32, (slots, slots), 0)
        position = lax.broadcasted_iota(jnp.int32, (slots, slots), 1)
        order = (original_of(index, quarter) == position).astype(F32).astype(BF16)
        for start in range(0, width, WIDE):
            normed_ref[:, start : start + WIDE] = jnp.dot(
                order, normed[:, start : start + WIDE], preferred_element_type=F32
            ).astype(BF16)
        write_masks(capacity, seq_count, counts_ref, bias_ref, mask_ref)

    value = jnp.dot(normed_ref[...], weight_ref[...], preferred_element_type=F32).astype(BF16)
    out_ref[...] = value
    for j in range(GROUP):
        cols = slice(j * HEAD, (j + 1) * HEAD)
        near_ref[:, cols] = value[(j % 2) * half : (j % 2 + 1) * half, cols]
        begin = QUARTER_OF[j] * quarter
        far_ref[:, cols] = value[begin : begin + quarter, cols]


def project(tiles, gain, counts, weight, capacity, seq_count):
    slots, width = tiles.shape
    steps = width // WIDE
    whole = lambda i: (0, 0)
    return pl.pallas_call(
        functools.partial(project_kernel, capacity, seq_count),
        grid=(2 * steps,),
        in_specs=[
            pl.BlockSpec((slots, width), whole),
            pl.BlockSpec((1, width), whole),
            pl.BlockSpec(counts.shape, whole),
            pl.BlockSpec((width, WIDE), lambda i: (0, i + steps)),
        ],
        out_specs=[
            pl.BlockSpec((slots, WIDE), lambda i: (0, i)),
            pl.BlockSpec((slots // 2, WIDE), lambda i: (0, i)),
            pl.BlockSpec((slots // 4, WIDE), lambda i: (0, i)),
            pl.BlockSpec((slots, width), whole),
            pl.BlockSpec((8, slots), whole),
            pl.BlockSpec((slots, 1), whole),
        ],
        out_shape=(
            jax.ShapeDtypeStruct((slots, 2 * width), BF16),
            jax.ShapeDtypeStruct((slots // 2, 2 * width), BF16),
            jax.ShapeDtypeStruct((slots // 4, 2 * width), BF16),
            jax.ShapeDtypeStruct((slots, width), BF16),
            jax.ShapeDtypeStruct((8, slots), F32),
            jax.ShapeDtypeStruct((slots, 1), F32),
        ),
        compiler_params=params(),
        name="project",
    )(tiles, gain.reshape(1, width), counts, weight)


def query_kernel(normed_ref, weight_ref, out_ref):
    out_ref[...] = jnp.dot(
        normed_ref[...], weight_ref[...], preferred_element_type=F32
    ).astype(BF16)


def project_query(normed, weight):
    slots, width = normed.shape
    return pl.pallas_call(
        query_kernel,
        grid=(width // WIDE,),
        in_specs=[
            pl.BlockSpec((slots, width), lambda i: (0, 0)),
            pl.BlockSpec((width, WIDE), lambda i: (0, i)),
        ],
        out_specs=pl.BlockSpec((slots, WIDE), lambda i: (0, i)),
        out_shape=jax.ShapeDtypeStruct((slots, width), BF16),
        compiler_params=params(),
        cost_estimate=pl.CostEstimate(
            flops=2 * slots * width * width, bytes_accessed=10_000_000, transcendentals=0
        ),
        name="project_query",
    )(normed, weight)


def softmax_parts(query, keys, values, bias):
    scores = lax.dot_general(
        query, keys, (((1,), (1,)), ((), ())), preferred_element_type=F32
    )
    scores = scores * FACTOR + bias
    peak = jnp.max(scores, axis=1, keepdims=True)
    weights = jnp.exp2(scores - peak)
    total = jnp.sum(weights, axis=1, keepdims=True)
    summed = jnp.dot(weights.astype(BF16), values, preferred_element_type=F32)
    return summed, peak, total


def merge(parts):
    top = parts[0][1]
    for _, peak, _ in parts[1:]:
        top = jnp.maximum(top, peak)
    above, below = 0.0, 0.0
    for summed, peak, total in parts:
        factor = jnp.exp2(peak - top)
        above = above + factor * summed
        below = below + factor * total
    return above, top, below


def ratio(above, below):
    return (above * (1.0 / jnp.maximum(below, 1.0))).astype(BF16)


def near_attention_kernel(
    q_ref, k_ref, v_ref, bias_ref, pair_k, pair_v, mixed_ref, summed_ref, stats_ref, query_ref
):
    slots = q_ref.shape[0]
    half, quarter = slots // 2, slots // 4
    lanes = lax.broadcasted_iota(jnp.int32, (quarter, HEAD), 1)
    stats = jnp.zeros((quarter, HEAD), F32)
    for j in range(GROUP):
        cols = slice(j * HEAD, (j + 1) * HEAD)
        start = (j % 2) * half
        inside = QUARTER_OF[j] * quarter - start
        mine = slice(start, start + half)
        other = slice(half - start, 2 * half - start)
        summed, _, total = softmax_parts(
            q_ref[other, cols], k_ref[:, cols], v_ref[:, cols], bias_ref[0:1, :]
        )
        mixed_ref[other, cols] = ratio(summed, total)
        one = softmax_parts(q_ref[mine, cols], k_ref[:, cols], v_ref[:, cols], bias_ref[0:1, :])
        keys = jnp.concatenate([k_ref[mine, cols], pair_k[:, cols]], axis=0)
        values = jnp.concatenate([v_ref[mine, cols], pair_v[:, cols]], axis=0)
        two = softmax_parts(q_ref[mine, cols], keys, values, bias_ref[1 + j % 2 : 2 + j % 2, :])
        above, top, below = merge([one, two])
        done = quarter - inside
        mixed_ref[start + done : start + done + quarter, cols] = ratio(
            above[done : done + quarter], below[done : done + quarter]
        )
        begin = start + inside
        fourth = slice(begin, begin + quarter)
        within = slice(inside, inside + quarter)
        keys = jnp.concatenate([k_ref[fourth, cols], pair_k[within, cols]], axis=0)
        values = jnp.concatenate([v_ref[fourth, cols], pair_v[within, cols]], axis=0)
        four = softmax_parts(q_ref[fourth, cols], keys, values, bias_ref[3 + j : 4 + j, :half])
        above, top, below = merge([(above[within], top[within], below[within]), four])
        summed_ref[:, cols] = above
        stats = jnp.where(lanes == 2 * j, top, jnp.where(lanes == 2 * j + 1, below, stats))
        query_ref[:, cols] = q_ref[fourth, cols]
        mixed_ref[fourth, cols] = jnp.zeros((quarter, HEAD), BF16)
    stats_ref[...] = stats


def halves(array, steps):
    rows = array.shape[0]
    return [
        pl.BlockSpec((rows, WIDE), lambda i: (0, i)),
        pl.BlockSpec((rows, WIDE), lambda i: (0, i + steps)),
    ]


def near_attention(query, pairs, bias, pair):
    slots, width = query.shape
    quarter = slots // 4
    steps = width // WIDE
    return pl.pallas_call(
        near_attention_kernel,
        grid=(steps,),
        in_specs=[
            pl.BlockSpec((slots, WIDE), lambda i: (0, i)),
            *halves(pairs, steps),
            pl.BlockSpec(bias.shape, lambda i: (0, 0)),
            *halves(pair, steps),
        ],
        out_specs=[
            pl.BlockSpec((slots, WIDE), lambda i: (0, i)),
            pl.BlockSpec((quarter, WIDE), lambda i: (0, i)),
            pl.BlockSpec((quarter, HEAD), lambda i: (0, i)),
            pl.BlockSpec((quarter, WIDE), lambda i: (0, i)),
        ],
        out_shape=(
            jax.ShapeDtypeStruct((slots, width), BF16),
            jax.ShapeDtypeStruct((quarter, width), F32),
            jax.ShapeDtypeStruct((quarter, steps * HEAD), F32),
            jax.ShapeDtypeStruct((quarter, width), BF16),
        ),
        compiler_params=params(SMALL_LIMIT),
        cost_estimate=pl.CostEstimate(
            flops=12 * slots * slots * width,
            bytes_accessed=14_000_000,
            transcendentals=6 * slots * slots * HEADS,
        ),
        name="near_attention",
    )(query, pairs, pairs, bias, pair, pair)


def far_attention_kernel(
    q_ref, bias_ref, one_k, one_v, two_k, two_v, summed_ref, stats_ref, mixed_ref
):
    half = bias_ref.shape[1] // 2
    for j in range(GROUP):
        cols = slice(j * HEAD, (j + 1) * HEAD)
        keys = jnp.concatenate([one_k[:, cols], two_k[:, cols]], axis=0)
        values = jnp.concatenate([one_v[:, cols], two_v[:, cols]], axis=0)
        four = softmax_parts(q_ref[:, cols], keys, values, bias_ref[3 + j : 4 + j, half:])
        before = (
            summed_ref[:, cols],
            stats_ref[:, 2 * j : 2 * j + 1],
            stats_ref[:, 2 * j + 1 : 2 * j + 2],
        )
        above, _, below = merge([before, four])
        mixed_ref[:, cols] = ratio(above, below)


def far_attention(query, bias, one, two, summed, stats):
    quarter, width = query.shape
    steps = width // WIDE
    block = pl.BlockSpec((quarter, WIDE), lambda i: (0, i))
    return pl.pallas_call(
        far_attention_kernel,
        grid=(steps,),
        in_specs=[
            block,
            pl.BlockSpec(bias.shape, lambda i: (0, 0)),
            *halves(one, steps),
            *halves(two, steps),
            block,
            pl.BlockSpec((quarter, HEAD), lambda i: (0, i)),
        ],
        out_specs=block,
        out_shape=jax.ShapeDtypeStruct((quarter, width), BF16),
        compiler_params=params(SMALL_LIMIT),
        name="far_attention",
    )(query, bias, one, one, two, two, summed, stats)


def finish_kernel(mixed_ref, last_ref, tiles_ref, weight_ref, finding_ref, mask_ref, layer_ref, keys_ref, stats_ref, plain_ref):
    slots, width = tiles_ref.shape
    quarter = slots // 4
    position = lax.broadcasted_iota(jnp.int32, (slots, slots), 0)
    index = lax.broadcasted_iota(jnp.int32, (slots, slots), 1)
    order = (original_of(index, quarter) == position).astype(F32).astype(BF16)
    for start in range(0, width, WIDE):
        heads = []
        for j in range(GROUP):
            cols = slice(start + j * HEAD, start + (j + 1) * HEAD)
            begin = QUARTER_OF[j] * quarter
            pieces = [last_ref[:, cols]]
            if begin > 0:
                pieces.insert(0, mixed_ref[:begin, cols])
            if begin + quarter < slots:
                pieces.append(mixed_ref[begin + quarter :, cols])
            heads.append(jnp.concatenate(pieces, axis=0))
        plain_ref[:, start : start + WIDE] = jnp.dot(
            order, jnp.concatenate(heads, axis=1), preferred_element_type=F32
        ).astype(BF16)
    square = jnp.zeros((slots, 1), F32)
    for start in range(0, width, WIDE):
        cols = slice(start, start + WIDE)
        added = jnp.dot(plain_ref[...], weight_ref[:, cols], preferred_element_type=F32)
        out = (tiles_ref[:, cols].astype(F32) + added).astype(BF16)
        layer_ref[:, cols] = out
        wide = out.astype(F32)
        square = square + jnp.sum(wide * wide, axis=1, keepdims=True)
    inverse = lax.rsqrt(square * (1.0 / width) + EPSILON)
    mask = mask_ref[...]
    for h in range(HEADS):
        cols = slice(h * HEAD, (h + 1) * HEAD)
        keys = (layer_ref[:, cols].astype(F32) * inverse).astype(BF16)
        keys_ref[:, cols] = keys
        scores = lax.dot_general(
            keys, finding_ref[:, cols], (((1,), (1,)), ((), ())), preferred_element_type=F32
        )
        scores = scores * FACTOR + mask
        peak = jnp.max(scores, axis=0, keepdims=True)
        stats_ref[h : h + 1, :] = peak
        stats_ref[HEADS + h : HEADS + h + 1, :] = jnp.sum(
            jnp.exp2(scores - peak), axis=0, keepdims=True
        )


def finish(mixed, last, tiles, weight, finding, mask):
    slots, width = tiles.shape
    return pl.pallas_call(
        finish_kernel,
        out_shape=(
            jax.ShapeDtypeStruct((slots, width), BF16),
            jax.ShapeDtypeStruct((slots, width), BF16),
            jax.ShapeDtypeStruct((2 * HEADS, finding.shape[0]), F32),
        ),
        scratch_shapes=[pltpu.VMEM((slots, width), BF16)],
        compiler_params=params(SMALL_LIMIT),
        name="finish",
    )(mixed, last, tiles, weight, finding, mask)


def heat_kernel(count, scale, stats_ref, keys_ref, finding_ref, mask_ref, heat_ref, held, kept, send_sem, recv_sem):
    slide = lax.axis_index("slide")
    me = lax.axis_index("seq")
    barrier = pltpu.get_barrier_semaphore()
    for hop in range(1, count):
        peer = lax.rem(me + hop, count)
        pl.semaphore_signal(
            barrier, inc=1, device_id=(slide, peer), device_id_type=pl.DeviceIdType.MESH
        )
    pl.semaphore_wait(barrier, count - 1)
    copies = []
    for hop in range(1, count):
        peer = lax.rem(me + hop, count)
        copy = pltpu.make_async_remote_copy(
            src_ref=stats_ref,
            dst_ref=held.at[hop],
            send_sem=send_sem.at[hop],
            recv_sem=recv_sem.at[hop],
            device_id=(slide, peer),
            device_id_type=pl.DeviceIdType.MESH,
        )
        copy.start()
        copies.append(copy)
    mask = mask_ref[...]
    for h in range(HEADS):
        cols = slice(h * HEAD, (h + 1) * HEAD)
        scores = lax.dot_general(
            keys_ref[:, cols], finding_ref[:, cols], (((1,), (1,)), ((), ())),
            preferred_element_type=F32,
        )
        kept[h] = jnp.exp2(scores * FACTOR + mask - stats_ref[h : h + 1, :])
    for copy in copies:
        copy.wait()
    everything = [stats_ref[...]] + [held[hop] for hop in range(1, count)]
    peaks = everything[0][:HEADS]
    for part in everything[1:]:
        peaks = jnp.maximum(peaks, part[:HEADS])
    totals = jnp.zeros_like(peaks)
    for part in everything:
        totals = totals + part[HEADS:] * jnp.exp2(part[:HEADS] - peaks)
    factors = jnp.exp2(everything[0][:HEADS] - peaks) * (scale / totals)
    slots = keys_ref.shape[0]
    chunk = 64
    for start in range(0, slots, chunk):
        rows = slice(start, start + chunk)
        total = kept[0, rows, :] * factors[0:1]
        for h in range(1, HEADS):
            total = total + kept[h, rows, :] * factors[h : h + 1]
        heat_ref[rows, :] = total


def heat_map(count, stats, keys, finding, mask):
    slots = keys.shape[0]
    finds = finding.shape[0]
    return pl.pallas_call(
        functools.partial(heat_kernel, count, count * slots / HEADS),
        in_specs=[pl.BlockSpec(memory_space=pltpu.VMEM)] * 4,
        out_specs=pl.BlockSpec(memory_space=pltpu.VMEM),
        out_shape=jax.ShapeDtypeStruct((slots, finds), F32),
        scratch_shapes=[
            pltpu.VMEM((count, 2 * HEADS, finds), F32),
            pltpu.VMEM((HEADS, slots, finds), F32),
            pltpu.SemaphoreType.DMA((count,)),
            pltpu.SemaphoreType.DMA((count,)),
        ],
        compiler_params=params(SMALL_LIMIT, collective_id=0, has_side_effects=True),
        name="heat_map",
    )(stats, keys, finding, mask)


def exchange(value, mask):
    pairs = [(source, source ^ mask) for source in range(lax.axis_size("seq"))]
    return lax.ppermute(value, "seq", pairs)


def shards(embeds, destination, norm_gain, qkv_weight, out_weight, finding_queries):
    devices = lax.axis_size(("slide", "seq"))
    seq_count = lax.axis_size("seq")
    slots = embeds.shape[0] * 2
    capacity = slots // devices
    padded = -(-capacity // 8) * 8
    width = embeds.shape[1]
    buffer, counts = dispatch(destination, embeds, devices, padded)
    received, counts = route(
        buffer.reshape(devices, padded, width), counts[None], devices, seq_count
    )
    tiles = received[:, :capacity].reshape(slots, width)
    pairs, near, far, normed, bias, mask = project(
        tiles, norm_gain, counts[:, 0], qkv_weight, capacity, seq_count
    )
    one = exchange(far, 2)
    pair = exchange(near, 1)
    query = project_query(normed, qkv_weight)
    mixed, summed, stats, quarter_query = near_attention(query, pairs, bias, pair)
    one, mixed = lax.optimization_barrier((one, mixed))
    two = exchange(one, 1)
    last = far_attention(quarter_query, bias, one, two, summed, stats)
    layer_out, keys, stats = finish(mixed, last, tiles, out_weight, finding_queries, mask)
    heat = heat_map(seq_count, stats, keys, finding_queries, mask)
    return (layer_out, heat)


LOG2_3 = math.log2(3.0)


def split(index, size):
    block = ((index.astype(F32) + 0.5) * (1.0 / size)).astype(jnp.int32)
    return block, index - block * size


def chunk_position(index, quarter):
    block, inner = split(index, quarter)
    phase = 2 * jnp.where((block == 1) | (block == 3), 1, 0) + (block >= 2).astype(jnp.int32)
    return 4 * inner + phase


def write_biases(capacity, slides, seq_count, counts, bias_ref, mask_ref):
    devices, lanes = counts.shape
    slots = mask_ref.shape[0]
    chunk = slots // slides
    half, quarter = chunk // 2, chunk // 4
    slide = lax.axis_index("slide")
    seq = lax.axis_index("seq")
    core = lax.rem(seq, 2)
    chip = lax.rem(seq // 2, 2)
    base = slide * seq_count + seq - core - 2 * chip
    members = [
        base + core + 2 * chip,
        base + (1 - core) + 2 * chip,
        base + core + 2 * (1 - chip),
        base + (1 - core) + 2 * (1 - chip),
    ]
    counts = counts.astype(F32)
    lane = lax.broadcasted_iota(jnp.int32, (devices, lanes), 1)
    columns = [
        jnp.sum(jnp.where(lane == member, counts, 0.0), axis=1, keepdims=True)
        for member in members
    ]
    sender = lax.broadcasted_iota(jnp.int32, (devices, slots), 0) * capacity
    index = lax.broadcasted_iota(jnp.int32, (1, slots), 1)

    def start_of(part):
        column = slide - part
        return chunk * jnp.where(column < 0, column + slides, column)

    def row(position, reached):
        place = (position - sender).astype(F32)
        inside = jnp.logical_and(place >= 0.0, place < reached)
        return (jnp.sum(inside.astype(F32), axis=0, keepdims=True) - 1.0) * (-MASKED)

    part, inner = split(index, chunk)
    block, _ = split(inner, quarter)
    own = row(start_of(part) + chunk_position(inner, quarter), columns[0])
    bias_ref[0:1, :] = own
    member, within = split(index, slots // 2)
    part, inner = split(within, half)
    sub, inner = split(inner, quarter)
    pair_rows = []
    for parity in range(2):
        in_half = jnp.where((block >= 2) == (parity == 1), 1.0, 0.0)
        bias_ref[1 + parity : 2 + parity, :] = own + in_half
        pair = row(start_of(part) + 4 * inner + parity + 2 * sub, columns[1])
        bias_ref[7 + parity : 8 + parity, :] = pair
        pair_rows.append(pair)
    member4, within4 = split(index, slots // 4)
    part4, inner4 = split(within4, quarter)
    reached = jnp.where(member4 >= 3, columns[3], columns[2])
    for phase in range(4):
        parity = phase % 2
        in_half = jnp.where((block >= 2) == (parity == 1), 1.0, 0.0)
        mine = jnp.where(block == QUARTER_OF[phase], LOG2_3, in_half)
        bias_ref[3 + phase : 4 + phase, :] = own + mine
        in_sub = jnp.where(sub == QUARTER_OF[phase] - 2 * parity, 1.0, 0.0)
        far = row(start_of(part4) + 4 * inner4 + phase, reached)
        bias_ref[9 + phase : 10 + phase, :] = jnp.where(
            member == 0, pair_rows[parity] + in_sub, far
        )
    bias_ref[13:16, :] = jnp.zeros((3, slots), F32)
    own = (lax.broadcasted_iota(jnp.int32, (8, lanes), 1) == members[0]).astype(F32)
    reached = lax.dot_general(
        own, counts, (((1,), (1,)), ((), ())), preferred_element_type=F32
    )[0:1, :]
    place = (
        lax.broadcasted_iota(jnp.int32, (slots, devices), 0)
        - lax.broadcasted_iota(jnp.int32, (slots, devices), 1) * capacity
    ).astype(F32)
    inside = jnp.logical_and(place >= 0.0, place < reached)
    mask_ref[...] = (jnp.sum(inside.astype(F32), axis=1, keepdims=True) - 1.0) * (-MASKED)


def pick(ref, parts, start, size, cols):
    step = ref.shape[0] // parts
    return jnp.concatenate(
        [ref[c * step + start : c * step + start + size, cols] for c in range(parts)], axis=0
    )


def put(ref, parts, start, cols, value):
    step, size = ref.shape[0] // parts, value.shape[0] // parts
    for c in range(parts):
        ref[c * step + start : c * step + start + size, cols] = value[c * size : (c + 1) * size]


def attend(query, pieces):
    scores = [
        lax.dot_general(query, keys, (((1,), (1,)), ((), ())), preferred_element_type=F32) * FACTOR
        + bias
        for keys, _, bias in pieces
    ]
    peak = functools.reduce(
        jnp.maximum, [jnp.max(score, axis=1, keepdims=True) for score in scores]
    )
    summed = None
    for score, (_, values, _) in zip(scores, pieces):
        wide = jnp.concatenate([values, jnp.ones(values.shape, BF16)], axis=1)
        part = jnp.dot(jnp.exp2(score - peak).astype(BF16), wide, preferred_element_type=F32)
        summed = part if summed is None else summed + part
    return ratio(summed[:, :HEAD], summed[:, HEAD:])


def layer_kernel(
    capacity, slides, seq_count,
    row_ref, embeds_ref, gain_ref, weight_ref, out_weight_ref, finding_ref,
    layer_ref, heat_ref,
    sending, received, counts_ref, all_ref, weight, tiles, query, keys, near, far, normed_ref,
    pair, one, two, plain, kept, bias_ref, mask_ref, stats_ref, held,
    send, recv, count_send, count_recv, own_sem, weight_sem, near_send, near_recv,
    far_send, far_recv, pass_send, pass_recv, stat_send, stat_recv, out_sem,
):
    rows, width = embeds_ref.shape
    devices = slides * seq_count
    chunk = seq_count * capacity
    slots = slides * chunk
    half, quarter = chunk // 2, chunk // 4
    lanes = counts_ref.shape[1]
    groups = width // WIDE
    slide = lax.axis_index("slide")
    seq = lax.axis_index("seq")
    me = slide * seq_count + seq
    core_peer = seq + 1 - 2 * lax.rem(seq, 2)
    chip_peer = seq + 2 - 4 * lax.rem(seq // 2, 2)
    barrier = pltpu.get_barrier_semaphore()

    def place_of(hop):
        return (lax.rem(slide + hop // seq_count, slides), lax.rem(seq + lax.rem(hop, seq_count), seq_count))

    def remote(src, dst, send_sem, recv_sem, where):
        return pltpu.make_async_remote_copy(
            src_ref=src,
            dst_ref=dst,
            send_sem=send_sem,
            recv_sem=recv_sem,
            device_id=where,
            device_id_type=pl.DeviceIdType.MESH,
        )

    def greet(hop, carry):
        pl.semaphore_signal(
            barrier, inc=1, device_id=place_of(hop), device_id_type=pl.DeviceIdType.MESH
        )
        return carry

    lax.fori_loop(1, devices, greet, 0)
    load = pltpu.make_async_copy(weight_ref, weight, weight_sem.at[0])
    load.start()

    row = row_ref[...]
    col = jnp.transpose(jnp.broadcast_to(row.astype(F32), (128, rows)))[:, 0:1].astype(jnp.int32)
    first = lax.broadcasted_iota(jnp.int32, (rows, rows), 0)
    second = lax.broadcasted_iota(jnp.int32, (rows, rows), 1)
    same = jnp.logical_and(col == row, first < second)
    rank = jnp.sum(same.astype(F32), axis=0, keepdims=True).astype(jnp.int32)
    place = row * capacity + rank
    lane = lax.broadcasted_iota(jnp.int32, (rows, lanes), 1)
    tally = jnp.sum((col == lane).astype(F32), axis=0, keepdims=True).astype(jnp.int32)
    counts_ref[...] = jnp.broadcast_to(tally, counts_ref.shape)

    def count_copy(hop):
        return remote(
            counts_ref, all_ref.at[me], count_send.at[hop], count_recv.at[hop], place_of(hop)
        )

    def row_copy(hop):
        where = place_of(hop)
        return remote(
            sending.at[where[0] * seq_count + where[1]],
            received.at[me],
            send.at[hop],
            recv.at[hop],
            where,
        )

    def each(make, method, low, high):
        def step(hop, carry):
            getattr(make(hop), method)()
            return carry

        lax.fori_loop(low, high, step, 0)

    def fill(k):
        column = lax.rem(slide + k, slides)
        wanted = lax.broadcasted_iota(jnp.int32, (chunk, rows), 0) + column * chunk
        chosen = (wanted == place).astype(F32).astype(BF16)
        for start in range(0, width, WIDE):
            part = jnp.dot(
                chosen, embeds_ref[:, start : start + WIDE], preferred_element_type=F32
            )
            sending[pl.ds(column * seq_count, seq_count), :, start : start + WIDE] = part.reshape(
                seq_count, capacity, WIDE
            ).astype(BF16)

    fill(0)
    pl.semaphore_wait(barrier, devices - 1)
    each(count_copy, "start", 1, devices)
    each(row_copy, "start", 1, seq_count)
    own = pltpu.make_async_copy(sending.at[me], received.at[me], own_sem)
    own.start()
    all_ref[pl.ds(me, 1)] = counts_ref[...][None]

    def fill_next(k, carry):
        fill(k)
        each(row_copy, "start", k * seq_count, (k + 1) * seq_count)
        return carry

    lax.fori_loop(1, slides, fill_next, 0)
    each(count_copy, "wait", 1, devices)
    write_biases(
        capacity, slides, seq_count, jnp.max(all_ref[...], axis=1), bias_ref, mask_ref
    )

    def near_copy(k):
        part = pl.ds(pl.multiple_of(k * half, half), half)
        return remote(
            near.at[part], pair.at[part], near_send.at[k], near_recv.at[k], (slide, core_peer)
        )

    def far_copy(k):
        part = pl.ds(pl.multiple_of(k * quarter, quarter), quarter)
        return remote(
            far.at[part], one.at[part], far_send.at[k], far_recv.at[k], (slide, chip_peer)
        )

    def pass_copy(k):
        part = pl.ds(pl.multiple_of(k * quarter, quarter), quarter)
        return remote(
            one.at[part], two.at[part], pass_send.at[k], pass_recv.at[k], (slide, core_peer)
        )

    index = lax.broadcasted_iota(jnp.int32, (chunk, 1), 0)
    position = lax.broadcasted_iota(jnp.int32, (chunk, chunk), 1)
    order = (chunk_position(index, quarter) == position).astype(F32).astype(BF16)

    def work(k):
        c = lax.rem(slide - k + slides, slides)
        place = pl.ds(pl.multiple_of(c * chunk, chunk), chunk)
        part = pl.ds(pl.multiple_of(k * chunk, chunk), chunk)
        group = pl.ds(c * seq_count, seq_count)
        square = jnp.zeros((chunk, 1), F32)
        for start in range(0, width, WIDE):
            tile = received[group, :, start : start + WIDE].astype(F32).reshape(chunk, WIDE)
            tiles[place, start : start + WIDE] = tile.astype(BF16)
            square = square + jnp.sum(tile * tile, axis=1, keepdims=True)
        inverse = lax.rsqrt(square * (1.0 / width) + EPSILON)
        for start in range(0, width, WIDE):
            tile = received[group, :, start : start + WIDE].astype(F32).reshape(chunk, WIDE)
            normed = (tile * inverse * gain_ref[:, start : start + WIDE]).astype(BF16)
            normed_ref[:, start : start + WIDE] = jnp.dot(
                order, normed, preferred_element_type=F32
            ).astype(BF16)

        def pairs(g, carry):
            at = pl.multiple_of(g * WIDE, WIDE)
            value = jnp.dot(
                normed_ref[...], weight[:, pl.ds(at + width, WIDE)], preferred_element_type=F32
            ).astype(BF16)
            keys[part, pl.ds(at, WIDE)] = value
            for j in range(GROUP):
                cols = pl.ds(at + j * HEAD, HEAD)
                begin = (j % 2) * half
                near[pl.ds(pl.multiple_of(k * half, half), half), cols] = value[
                    begin : begin + half, j * HEAD : (j + 1) * HEAD
                ]
                begin = QUARTER_OF[j] * quarter
                far[pl.ds(pl.multiple_of(k * quarter, quarter), quarter), cols] = value[
                    begin : begin + quarter, j * HEAD : (j + 1) * HEAD
                ]
            return carry

        def single(g, carry):
            at = pl.multiple_of(g * WIDE, WIDE)
            query[part, pl.ds(at, WIDE)] = jnp.dot(
                normed_ref[...], weight[:, pl.ds(at, WIDE)], preferred_element_type=F32
            ).astype(BF16)
            return carry

        lax.fori_loop(0, 2 * groups, pairs, 0)
        far_copy(k).start()
        near_copy(k).start()
        lax.fori_loop(0, groups, single, 0)

    own.wait()
    load.wait()

    def step(k, carry):
        each(row_copy, "wait_recv", jnp.maximum(k * seq_count, 1), (k + 1) * seq_count)
        work(k)
        return carry

    lax.fori_loop(0, slides, step, 0)
    again = pltpu.make_async_copy(
        out_weight_ref, weight.at[:, pl.ds(0, width)], weight_sem.at[1]
    )
    again.start()

    def forward(k, carry):
        far_copy(k).wait_recv()
        pass_copy(k).start()
        return carry

    each(near_copy, "wait_recv", 0, slides)

    def head_cols(g, j):
        at = pl.multiple_of(g * WIDE + j * HEAD, HEAD)
        return pl.ds(at, HEAD), pl.ds(pl.multiple_of(at + width, HEAD), HEAD)

    def near_pass(g, carry):
        for j in range(GROUP):
            cols, value_cols = head_cols(g, j)
            start = (j % 2) * half
            done = start + quarter - (QUARTER_OF[j] * quarter - start)
            put(query, slides, half - start, cols, attend(
                pick(query, slides, half - start, half, cols),
                [(keys[:, cols], keys[:, value_cols], bias_ref[0:1, :])],
            ))
            put(query, slides, done, cols, attend(
                pick(query, slides, done, quarter, cols),
                [
                    (keys[:, cols], keys[:, value_cols], bias_ref[1 + j % 2 : 2 + j % 2, :]),
                    (pair[:, cols], pair[:, value_cols], bias_ref[7 + j % 2 : 8 + j % 2, : slots // 2]),
                ],
            ))
        return carry

    def far_pass(g, carry):
        count = slots // 4
        for j in range(GROUP):
            cols, value_cols = head_cols(g, j)
            line = slice(9 + j, 10 + j)
            put(query, slides, QUARTER_OF[j] * quarter, cols, attend(
                pick(query, slides, QUARTER_OF[j] * quarter, quarter, cols),
                [
                    (keys[:, cols], keys[:, value_cols], bias_ref[3 + j : 4 + j, :]),
                    (pair[:, cols], pair[:, value_cols], bias_ref[line, : 2 * count]),
                    (one[:, cols], one[:, value_cols], bias_ref[line, 2 * count : 3 * count]),
                    (two[:, cols], two[:, value_cols], bias_ref[line, 3 * count :]),
                ],
            ))
        return carry

    lax.fori_loop(0, groups - 1, near_pass, 0)
    lax.fori_loop(0, slides, forward, 0)
    lax.fori_loop(groups - 1, groups, near_pass, 0)
    each(pass_copy, "wait_recv", 0, slides)
    lax.fori_loop(0, groups, far_pass, 0)

    def restore(k, carry):
        c = lax.rem(slide - k + slides, slides)
        place = pl.ds(pl.multiple_of(c * chunk, chunk), chunk)
        part = pl.ds(pl.multiple_of(k * chunk, chunk), chunk)
        for start in range(0, width, WIDE):
            plain[place, start : start + WIDE] = lax.dot_general(
                order, query[part, start : start + WIDE], (((0,), (0,)), ((), ())),
                preferred_element_type=F32,
            ).astype(BF16)
        return carry

    lax.fori_loop(0, slides, restore, 0)
    again.wait()
    square = jnp.zeros((slots, 1), F32)
    for start in range(0, width, WIDE):
        cols = slice(start, start + WIDE)
        added = jnp.dot(plain[...], weight[:, cols], preferred_element_type=F32)
        out = (tiles[:, cols].astype(F32) + added).astype(BF16)
        tiles[:, cols] = out
        wide = out.astype(F32)
        square = square + jnp.sum(wide * wide, axis=1, keepdims=True)
    store = pltpu.make_async_copy(tiles, layer_ref, out_sem)
    store.start()
    inverse = lax.rsqrt(square * (1.0 / width) + EPSILON)
    mask = mask_ref[...]
    for h in range(HEADS):
        cols = slice(h * HEAD, (h + 1) * HEAD)
        found = (tiles[:, cols].astype(F32) * inverse).astype(BF16)
        scores = lax.dot_general(
            found, finding_ref[:, cols], (((1,), (1,)), ((), ())), preferred_element_type=F32
        )
        scores = scores * FACTOR + mask
        peak = jnp.max(scores, axis=0, keepdims=True)
        raised = jnp.exp2(scores - peak)
        kept[h] = raised
        stats_ref[h : h + 1, :] = peak
        stats_ref[HEADS + h : HEADS + h + 1, :] = jnp.sum(raised, axis=0, keepdims=True)

    def stat_copy(hop):
        return remote(
            stats_ref, held.at[hop], stat_send.at[hop], stat_recv.at[hop],
            (slide, lax.rem(seq + hop, seq_count)),
        )

    each(stat_copy, "start", 1, seq_count)
    each(stat_copy, "wait_recv", 1, seq_count)
    everything = [stats_ref[...]] + [held[hop] for hop in range(1, seq_count)]
    peaks = everything[0][:HEADS]
    for part in everything[1:]:
        peaks = jnp.maximum(peaks, part[:HEADS])
    totals = jnp.zeros_like(peaks)
    for part in everything:
        totals = totals + part[HEADS:] * jnp.exp2(part[:HEADS] - peaks)
    factors = jnp.exp2(everything[0][:HEADS] - peaks) * (seq_count * slots / HEADS / totals)
    small = 64
    for start in range(0, slots, small):
        part = slice(start, start + small)
        total = kept[0, part, :] * factors[0:1]
        for h in range(1, HEADS):
            total = total + kept[h, part, :] * factors[h : h + 1]
        heat_ref[part, :] = total
    each(row_copy, "wait_send", 1, devices)
    each(near_copy, "wait_send", 0, slides)
    each(far_copy, "wait_send", 0, slides)
    each(pass_copy, "wait_send", 0, slides)
    each(stat_copy, "wait_send", 1, seq_count)
    store.wait()


def layer(destination, embeds, gain, weight, out_weight, finding, capacity, slides, seq_count):
    rows, width = embeds.shape
    finds = finding.shape[0]
    devices = slides * seq_count
    slots = devices * capacity
    chunk = seq_count * capacity
    lanes = max(128, devices)
    vmem = pl.BlockSpec(memory_space=pltpu.VMEM)
    anywhere = pl.BlockSpec(memory_space=pl.ANY)
    dma = pltpu.SemaphoreType.DMA
    return pl.pallas_call(
        functools.partial(layer_kernel, capacity, slides, seq_count),
        in_specs=[vmem, vmem, vmem, anywhere, anywhere, vmem],
        out_specs=[anywhere, vmem],
        out_shape=(
            jax.ShapeDtypeStruct((slots, width), BF16),
            jax.ShapeDtypeStruct((slots, finds), F32),
        ),
        scratch_shapes=[
            pltpu.VMEM((devices, capacity, width), BF16),
            pltpu.VMEM((devices, capacity, width), BF16),
            pltpu.VMEM((8, lanes), jnp.int32),
            pltpu.VMEM((devices, 8, lanes), jnp.int32),
            pltpu.VMEM(weight.shape, BF16),
            pltpu.VMEM((slots, width), BF16),
            pltpu.VMEM((slots, width), BF16),
            pltpu.VMEM((slots, 2 * width), BF16),
            pltpu.VMEM((slots // 2, 2 * width), BF16),
            pltpu.VMEM((slots // 4, 2 * width), BF16),
            pltpu.VMEM((chunk, width), BF16),
            pltpu.VMEM((slots // 2, 2 * width), BF16),
            pltpu.VMEM((slots // 4, 2 * width), BF16),
            pltpu.VMEM((slots // 4, 2 * width), BF16),
            pltpu.VMEM((slots, width), BF16),
            pltpu.VMEM((HEADS, slots, finds), F32),
            pltpu.VMEM((16, slots), F32),
            pltpu.VMEM((slots, 1), F32),
            pltpu.VMEM((2 * HEADS, finds), F32),
            pltpu.VMEM((seq_count, 2 * HEADS, finds), F32),
            dma((devices,)),
            dma((devices,)),
            dma((devices,)),
            dma((devices,)),
            dma,
            dma((2,)),
            dma((slides,)),
            dma((slides,)),
            dma((slides,)),
            dma((slides,)),
            dma((slides,)),
            dma((slides,)),
            dma((seq_count,)),
            dma((seq_count,)),
            dma,
        ],
        compiler_params=params(LAYER_LIMIT, collective_id=2, has_side_effects=True),
        cost_estimate=pl.CostEstimate(
            flops=8 * slots * width * width + 8 * slots * slots * width,
            bytes_accessed=30_000_000,
            transcendentals=20_000_000,
        ),
        name="layer",
    )(destination.reshape(1, rows), embeds, gain.reshape(1, width), weight, out_weight, finding)


LAYER_LIMIT = 60 * 1024 * 1024


def layer_shards(embeds, destination, norm_gain, qkv_weight, out_weight, finding_queries):
    slides = lax.axis_size("slide")
    seq_count = lax.axis_size("seq")
    slots = embeds.shape[0] * 2
    capacity = slots // (slides * seq_count)
    return layer(
        destination, embeds, norm_gain, qkv_weight, out_weight, finding_queries,
        capacity, slides, seq_count,
    )


def solution(mesh):
    in_specs = (P(("slide", "seq"), None), P(("slide", "seq"), None), P(), P(), P(), P())
    out_specs = (P(("slide", "seq"), None), P(("slide", "seq"), None))

    def program(embeds, *rest):
        devices = mesh.shape["slide"] * mesh.shape["seq"]
        capacity = embeds.shape[0] * 2 // devices // devices
        chunk = capacity * mesh.shape["seq"]
        body = layer_shards if capacity % 8 == 0 and chunk % 64 == 0 else shards
        return jax.shard_map(
            body, mesh=mesh, in_specs=in_specs, out_specs=out_specs, check_vma=False
        )(embeds, *rest)

    return program
```

```python
import functools
import math

import jax
import jax.numpy as jnp
from jax import lax
from jax.experimental import pallas as pl
from jax.experimental.pallas import tpu as pltpu
from jax.sharding import PartitionSpec as P

HEADS = 12
HEAD = 128
GROUP = 4
WIDE = GROUP * HEAD
MASKED = -1e30
EPSILON = 1e-06
FACTOR = math.log2(math.e) / math.sqrt(HEAD)
F32 = jnp.float32
BF16 = jnp.bfloat16
QUARTER_OF = (0, 2, 1, 3)
VMEM_LIMIT = 56 * 1024 * 1024
SMALL_LIMIT = 34 * 1024 * 1024


def params(limit=VMEM_LIMIT, **more):
    return pltpu.CompilerParams(vmem_limit_bytes=limit, **more)


def dispatch_kernel(capacity, row_ref, embeds_ref, buffer_ref, counts_ref):
    rows = embeds_ref.shape[0]
    slots = buffer_ref.shape[0]
    row = row_ref[...]
    col = jnp.transpose(jnp.broadcast_to(row.astype(F32), (128, rows)))[:, 0:1].astype(jnp.int32)
    first = lax.broadcasted_iota(jnp.int32, (rows, rows), 0)
    second = lax.broadcasted_iota(jnp.int32, (rows, rows), 1)
    same = jnp.logical_and(col == row, first < second)
    rank = jnp.sum(same.astype(F32), axis=0, keepdims=True).astype(jnp.int32)
    place = row * capacity + rank
    lanes = lax.broadcasted_iota(jnp.int32, (rows, counts_ref.shape[1]), 1)
    counts_ref[...] = jnp.sum((col == lanes).astype(F32), axis=0, keepdims=True).astype(jnp.int32)
    chosen = (lax.broadcasted_iota(jnp.int32, (slots, rows), 0) == place).astype(F32).astype(BF16)
    for start in range(0, embeds_ref.shape[1], WIDE):
        part = embeds_ref[:, start : start + WIDE]
        buffer_ref[:, start : start + WIDE] = jnp.dot(
            chosen, part, preferred_element_type=F32
        ).astype(BF16)


def dispatch(destination, embeds, devices, capacity):
    rows, width = embeds.shape
    slots = devices * capacity
    return pl.pallas_call(
        functools.partial(dispatch_kernel, capacity),
        out_shape=(
            jax.ShapeDtypeStruct((slots, width), BF16),
            jax.ShapeDtypeStruct((1, max(128, devices)), jnp.int32),
        ),
        compiler_params=params(),
        name="dispatch",
    )(destination.reshape(1, rows), embeds)


def original_of(index, quarter):
    block = (
        (index >= quarter).astype(jnp.int32)
        + (index >= 2 * quarter).astype(jnp.int32)
        + (index >= 3 * quarter).astype(jnp.int32)
    )
    phase = 2 * jnp.where((block == 1) | (block == 3), 1, 0) + (block >= 2).astype(jnp.int32)
    return 4 * (index - quarter * block) + phase


def route_kernel(devices, seq_count, buffer_ref, counts_ref, tiles_ref, all_ref, send, recv, count_send, count_recv, own_sem):
    me = lax.axis_index("slide") * seq_count + lax.axis_index("seq")
    barrier = pltpu.get_barrier_semaphore()

    def place_of(hop):
        peer = lax.rem(me + hop, devices)
        return peer, (peer // seq_count, lax.rem(peer, seq_count))

    def greet(hop, carry):
        pl.semaphore_signal(
            barrier, inc=1, device_id=place_of(hop)[1], device_id_type=pl.DeviceIdType.MESH
        )
        return carry

    lax.fori_loop(1, devices, greet, 0)
    pl.semaphore_wait(barrier, devices - 1)

    def copies(hop):
        peer, where = place_of(hop)
        rows = pltpu.make_async_remote_copy(
            src_ref=buffer_ref.at[peer],
            dst_ref=tiles_ref.at[me],
            send_sem=send.at[hop],
            recv_sem=recv.at[hop],
            device_id=where,
            device_id_type=pl.DeviceIdType.MESH,
        )
        count = pltpu.make_async_remote_copy(
            src_ref=counts_ref.at[0],
            dst_ref=all_ref.at[me],
            send_sem=count_send.at[hop],
            recv_sem=count_recv.at[hop],
            device_id=where,
            device_id_type=pl.DeviceIdType.MESH,
        )
        return rows, count

    def begin(hop, carry):
        for copy in copies(hop):
            copy.start()
        return carry

    def end(hop, carry):
        for copy in copies(hop):
            copy.wait()
        return carry

    own_rows = pltpu.make_async_copy(buffer_ref.at[me], tiles_ref.at[me], own_sem.at[0])
    own_count = pltpu.make_async_copy(counts_ref.at[0], all_ref.at[me], own_sem.at[1])
    lax.fori_loop(1, devices, begin, 0)
    own_rows.start()
    own_count.start()
    own_rows.wait()
    own_count.wait()
    lax.fori_loop(1, devices, end, 0)


def route(buffer, counts, devices, seq_count):
    capacity, width = buffer.shape[1:]
    lanes = counts.shape[2]
    return pl.pallas_call(
        functools.partial(route_kernel, devices, seq_count),
        in_specs=[pl.BlockSpec(memory_space=pl.ANY)] * 2,
        out_specs=[pl.BlockSpec(memory_space=pl.ANY)] * 2,
        out_shape=(
            jax.ShapeDtypeStruct((devices, capacity, width), BF16),
            jax.ShapeDtypeStruct((devices, 1, lanes), jnp.int32),
        ),
        scratch_shapes=[pltpu.SemaphoreType.DMA((devices,))] * 4
        + [pltpu.SemaphoreType.DMA((2,))],
        compiler_params=pltpu.CompilerParams(collective_id=1, has_side_effects=True),
        name="route",
    )(buffer, counts)


def write_masks(capacity, seq_count, counts_ref, bias_ref, mask_ref):
    devices, lanes = counts_ref.shape
    slots = mask_ref.shape[0]
    half, quarter = slots // 2, slots // 4
    slide = lax.axis_index("slide")
    seq = lax.axis_index("seq")
    core = lax.rem(seq, 2)
    chip = lax.rem(seq // 2, 2)
    base = slide * seq_count + seq - core - 2 * chip
    members = [
        base + core + 2 * chip,
        base + (1 - core) + 2 * chip,
        base + core + 2 * (1 - chip),
        base + (1 - core) + 2 * (1 - chip),
    ]
    counts = counts_ref[...].astype(F32)
    lane = lax.broadcasted_iota(jnp.int32, (devices, lanes), 1)
    columns = [
        jnp.sum(jnp.where(lane == member, counts, 0.0), axis=1, keepdims=True)
        for member in members
    ]
    sender = lax.broadcasted_iota(jnp.int32, (devices, slots), 0) * capacity
    index = lax.broadcasted_iota(jnp.int32, (devices, slots), 1)

    def row(position, reached):
        place = (position - sender).astype(F32)
        inside = jnp.logical_and(place >= 0.0, place < reached)
        return (jnp.sum(inside.astype(F32), axis=0, keepdims=True) - 1.0) * (-MASKED)

    bias_ref[0:1, :] = row(original_of(index, quarter), columns[0])
    within = jnp.where(index >= half, index - half, index)
    for parity in range(2):
        reached = jnp.where(index >= half, columns[1], columns[0])
        bias_ref[1 + parity : 2 + parity, :] = row(
            original_of(within + parity * half, quarter), reached
        )
    for phase in range(4):
        block = (
            (index >= quarter).astype(jnp.int32)
            + (index >= 2 * quarter).astype(jnp.int32)
            + (index >= 3 * quarter).astype(jnp.int32)
        )
        reached = jnp.where(
            index >= half,
            jnp.where(index >= 3 * quarter, columns[3], columns[2]),
            jnp.where(index >= quarter, columns[1], columns[0]),
        )
        bias_ref[3 + phase : 4 + phase, :] = row(4 * (index - quarter * block) + phase, reached)
    bias_ref[7:8, :] = jnp.zeros((1, slots), F32)
    own = (lax.broadcasted_iota(jnp.int32, (8, lanes), 1) == members[0]).astype(F32)
    reached = lax.dot_general(
        own, counts, (((1,), (1,)), ((), ())), preferred_element_type=F32
    )[0:1, :]
    place = (
        lax.broadcasted_iota(jnp.int32, (slots, devices), 0)
        - lax.broadcasted_iota(jnp.int32, (slots, devices), 1) * capacity
    ).astype(F32)
    inside = jnp.logical_and(place >= 0.0, place < reached)
    mask_ref[...] = (jnp.sum(inside.astype(F32), axis=1, keepdims=True) - 1.0) * (-MASKED)


def project_kernel(capacity, seq_count, tiles_ref, gain_ref, counts_ref, weight_ref, out_ref, near_ref, far_ref, normed_ref, bias_ref, mask_ref):
    step = pl.program_id(0)
    slots, width = tiles_ref.shape
    quarter = slots // 4
    half = slots // 2

    @pl.when(step == 0)
    def _():
        tile = tiles_ref[...].astype(F32)
        mean = jnp.mean(tile * tile, axis=1, keepdims=True)
        normed = (tile * lax.rsqrt(mean + EPSILON) * gain_ref[...]).astype(BF16)
        index = lax.broadcasted_iota(jnp.int32, (slots, slots), 0)
        position = lax.broadcasted_iota(jnp.int32, (slots, slots), 1)
        order = (original_of(index, quarter) == position).astype(F32).astype(BF16)
        for start in range(0, width, WIDE):
            normed_ref[:, start : start + WIDE] = jnp.dot(
                order, normed[:, start : start + WIDE], preferred_element_type=F32
            ).astype(BF16)
        write_masks(capacity, seq_count, counts_ref, bias_ref, mask_ref)

    value = jnp.dot(normed_ref[...], weight_ref[...], preferred_element_type=F32).astype(BF16)
    out_ref[...] = value
    for j in range(GROUP):
        cols = slice(j * HEAD, (j + 1) * HEAD)
        near_ref[:, cols] = value[(j % 2) * half : (j % 2 + 1) * half, cols]
        begin = QUARTER_OF[j] * quarter
        far_ref[:, cols] = value[begin : begin + quarter, cols]


def project(tiles, gain, counts, weight, capacity, seq_count):
    slots, width = tiles.shape
    steps = width // WIDE
    whole = lambda i: (0, 0)
    return pl.pallas_call(
        functools.partial(project_kernel, capacity, seq_count),
        grid=(2 * steps,),
        in_specs=[
            pl.BlockSpec((slots, width), whole),
            pl.BlockSpec((1, width), whole),
            pl.BlockSpec(counts.shape, whole),
            pl.BlockSpec((width, WIDE), lambda i: (0, i + steps)),
        ],
        out_specs=[
            pl.BlockSpec((slots, WIDE), lambda i: (0, i)),
            pl.BlockSpec((slots // 2, WIDE), lambda i: (0, i)),
            pl.BlockSpec((slots // 4, WIDE), lambda i: (0, i)),
            pl.BlockSpec((slots, width), whole),
            pl.BlockSpec((8, slots), whole),
            pl.BlockSpec((slots, 1), whole),
        ],
        out_shape=(
            jax.ShapeDtypeStruct((slots, 2 * width), BF16),
            jax.ShapeDtypeStruct((slots // 2, 2 * width), BF16),
            jax.ShapeDtypeStruct((slots // 4, 2 * width), BF16),
            jax.ShapeDtypeStruct((slots, width), BF16),
            jax.ShapeDtypeStruct((8, slots), F32),
            jax.ShapeDtypeStruct((slots, 1), F32),
        ),
        compiler_params=params(),
        name="project",
    )(tiles, gain.reshape(1, width), counts, weight)


def query_kernel(normed_ref, weight_ref, out_ref):
    out_ref[...] = jnp.dot(
        normed_ref[...], weight_ref[...], preferred_element_type=F32
    ).astype(BF16)


def project_query(normed, weight):
    slots, width = normed.shape
    return pl.pallas_call(
        query_kernel,
        grid=(width // WIDE,),
        in_specs=[
            pl.BlockSpec((slots, width), lambda i: (0, 0)),
            pl.BlockSpec((width, WIDE), lambda i: (0, i)),
        ],
        out_specs=pl.BlockSpec((slots, WIDE), lambda i: (0, i)),
        out_shape=jax.ShapeDtypeStruct((slots, width), BF16),
        compiler_params=params(),
        cost_estimate=pl.CostEstimate(
            flops=2 * slots * width * width, bytes_accessed=10_000_000, transcendentals=0
        ),
        name="project_query",
    )(normed, weight)


def softmax_parts(query, keys, values, bias):
    scores = lax.dot_general(
        query, keys, (((1,), (1,)), ((), ())), preferred_element_type=F32
    )
    scores = scores * FACTOR + bias
    peak = jnp.max(scores, axis=1, keepdims=True)
    weights = jnp.exp2(scores - peak)
    total = jnp.sum(weights, axis=1, keepdims=True)
    summed = jnp.dot(weights.astype(BF16), values, preferred_element_type=F32)
    return summed, peak, total


def merge(parts):
    top = parts[0][1]
    for _, peak, _ in parts[1:]:
        top = jnp.maximum(top, peak)
    above, below = 0.0, 0.0
    for summed, peak, total in parts:
        factor = jnp.exp2(peak - top)
        above = above + factor * summed
        below = below + factor * total
    return above, top, below


def ratio(above, below):
    return (above * (1.0 / jnp.maximum(below, 1.0))).astype(BF16)


def near_attention_kernel(
    q_ref, k_ref, v_ref, bias_ref, pair_k, pair_v, mixed_ref, summed_ref, stats_ref, query_ref
):
    slots = q_ref.shape[0]
    half, quarter = slots // 2, slots // 4
    lanes = lax.broadcasted_iota(jnp.int32, (quarter, HEAD), 1)
    stats = jnp.zeros((quarter, HEAD), F32)
    for j in range(GROUP):
        cols = slice(j * HEAD, (j + 1) * HEAD)
        start = (j % 2) * half
        inside = QUARTER_OF[j] * quarter - start
        mine = slice(start, start + half)
        other = slice(half - start, 2 * half - start)
        summed, _, total = softmax_parts(
            q_ref[other, cols], k_ref[:, cols], v_ref[:, cols], bias_ref[0:1, :]
        )
        mixed_ref[other, cols] = ratio(summed, total)
        one = softmax_parts(q_ref[mine, cols], k_ref[:, cols], v_ref[:, cols], bias_ref[0:1, :])
        keys = jnp.concatenate([k_ref[mine, cols], pair_k[:, cols]], axis=0)
        values = jnp.concatenate([v_ref[mine, cols], pair_v[:, cols]], axis=0)
        two = softmax_parts(q_ref[mine, cols], keys, values, bias_ref[1 + j % 2 : 2 + j % 2, :])
        above, top, below = merge([one, two])
        done = quarter - inside
        mixed_ref[start + done : start + done + quarter, cols] = ratio(
            above[done : done + quarter], below[done : done + quarter]
        )
        begin = start + inside
        fourth = slice(begin, begin + quarter)
        within = slice(inside, inside + quarter)
        keys = jnp.concatenate([k_ref[fourth, cols], pair_k[within, cols]], axis=0)
        values = jnp.concatenate([v_ref[fourth, cols], pair_v[within, cols]], axis=0)
        four = softmax_parts(q_ref[fourth, cols], keys, values, bias_ref[3 + j : 4 + j, :half])
        above, top, below = merge([(above[within], top[within], below[within]), four])
        summed_ref[:, cols] = above
        stats = jnp.where(lanes == 2 * j, top, jnp.where(lanes == 2 * j + 1, below, stats))
        query_ref[:, cols] = q_ref[fourth, cols]
        mixed_ref[fourth, cols] = jnp.zeros((quarter, HEAD), BF16)
    stats_ref[...] = stats


def halves(array, steps):
    rows = array.shape[0]
    return [
        pl.BlockSpec((rows, WIDE), lambda i: (0, i)),
        pl.BlockSpec((rows, WIDE), lambda i: (0, i + steps)),
    ]


def near_attention(query, pairs, bias, pair):
    slots, width = query.shape
    quarter = slots // 4
    steps = width // WIDE
    return pl.pallas_call(
        near_attention_kernel,
        grid=(steps,),
        in_specs=[
            pl.BlockSpec((slots, WIDE), lambda i: (0, i)),
            *halves(pairs, steps),
            pl.BlockSpec(bias.shape, lambda i: (0, 0)),
            *halves(pair, steps),
        ],
        out_specs=[
            pl.BlockSpec((slots, WIDE), lambda i: (0, i)),
            pl.BlockSpec((quarter, WIDE), lambda i: (0, i)),
            pl.BlockSpec((quarter, HEAD), lambda i: (0, i)),
            pl.BlockSpec((quarter, WIDE), lambda i: (0, i)),
        ],
        out_shape=(
            jax.ShapeDtypeStruct((slots, width), BF16),
            jax.ShapeDtypeStruct((quarter, width), F32),
            jax.ShapeDtypeStruct((quarter, steps * HEAD), F32),
            jax.ShapeDtypeStruct((quarter, width), BF16),
        ),
        compiler_params=params(SMALL_LIMIT),
        cost_estimate=pl.CostEstimate(
            flops=12 * slots * slots * width,
            bytes_accessed=14_000_000,
            transcendentals=6 * slots * slots * HEADS,
        ),
        name="near_attention",
    )(query, pairs, pairs, bias, pair, pair)


def far_attention_kernel(
    q_ref, bias_ref, one_k, one_v, two_k, two_v, summed_ref, stats_ref, mixed_ref
):
    half = bias_ref.shape[1] // 2
    for j in range(GROUP):
        cols = slice(j * HEAD, (j + 1) * HEAD)
        keys = jnp.concatenate([one_k[:, cols], two_k[:, cols]], axis=0)
        values = jnp.concatenate([one_v[:, cols], two_v[:, cols]], axis=0)
        four = softmax_parts(q_ref[:, cols], keys, values, bias_ref[3 + j : 4 + j, half:])
        before = (
            summed_ref[:, cols],
            stats_ref[:, 2 * j : 2 * j + 1],
            stats_ref[:, 2 * j + 1 : 2 * j + 2],
        )
        above, _, below = merge([before, four])
        mixed_ref[:, cols] = ratio(above, below)


def far_attention(query, bias, one, two, summed, stats):
    quarter, width = query.shape
    steps = width // WIDE
    block = pl.BlockSpec((quarter, WIDE), lambda i: (0, i))
    return pl.pallas_call(
        far_attention_kernel,
        grid=(steps,),
        in_specs=[
            block,
            pl.BlockSpec(bias.shape, lambda i: (0, 0)),
            *halves(one, steps),
            *halves(two, steps),
            block,
            pl.BlockSpec((quarter, HEAD), lambda i: (0, i)),
        ],
        out_specs=block,
        out_shape=jax.ShapeDtypeStruct((quarter, width), BF16),
        compiler_params=params(SMALL_LIMIT),
        name="far_attention",
    )(query, bias, one, one, two, two, summed, stats)


def finish_kernel(mixed_ref, last_ref, tiles_ref, weight_ref, finding_ref, mask_ref, layer_ref, keys_ref, stats_ref, plain_ref):
    slots, width = tiles_ref.shape
    quarter = slots // 4
    position = lax.broadcasted_iota(jnp.int32, (slots, slots), 0)
    index = lax.broadcasted_iota(jnp.int32, (slots, slots), 1)
    order = (original_of(index, quarter) == position).astype(F32).astype(BF16)
    for start in range(0, width, WIDE):
        heads = []
        for j in range(GROUP):
            cols = slice(start + j * HEAD, start + (j + 1) * HEAD)
            begin = QUARTER_OF[j] * quarter
            pieces = [last_ref[:, cols]]
            if begin > 0:
                pieces.insert(0, mixed_ref[:begin, cols])
            if begin + quarter < slots:
                pieces.append(mixed_ref[begin + quarter :, cols])
            heads.append(jnp.concatenate(pieces, axis=0))
        plain_ref[:, start : start + WIDE] = jnp.dot(
            order, jnp.concatenate(heads, axis=1), preferred_element_type=F32
        ).astype(BF16)
    square = jnp.zeros((slots, 1), F32)
    for start in range(0, width, WIDE):
        cols = slice(start, start + WIDE)
        added = jnp.dot(plain_ref[...], weight_ref[:, cols], preferred_element_type=F32)
        out = (tiles_ref[:, cols].astype(F32) + added).astype(BF16)
        layer_ref[:, cols] = out
        wide = out.astype(F32)
        square = square + jnp.sum(wide * wide, axis=1, keepdims=True)
    inverse = lax.rsqrt(square * (1.0 / width) + EPSILON)
    mask = mask_ref[...]
    for h in range(HEADS):
        cols = slice(h * HEAD, (h + 1) * HEAD)
        keys = (layer_ref[:, cols].astype(F32) * inverse).astype(BF16)
        keys_ref[:, cols] = keys
        scores = lax.dot_general(
            keys, finding_ref[:, cols], (((1,), (1,)), ((), ())), preferred_element_type=F32
        )
        scores = scores * FACTOR + mask
        peak = jnp.max(scores, axis=0, keepdims=True)
        stats_ref[h : h + 1, :] = peak
        stats_ref[HEADS + h : HEADS + h + 1, :] = jnp.sum(
            jnp.exp2(scores - peak), axis=0, keepdims=True
        )


def finish(mixed, last, tiles, weight, finding, mask):
    slots, width = tiles.shape
    return pl.pallas_call(
        finish_kernel,
        out_shape=(
            jax.ShapeDtypeStruct((slots, width), BF16),
            jax.ShapeDtypeStruct((slots, width), BF16),
            jax.ShapeDtypeStruct((2 * HEADS, finding.shape[0]), F32),
        ),
        scratch_shapes=[pltpu.VMEM((slots, width), BF16)],
        compiler_params=params(SMALL_LIMIT),
        name="finish",
    )(mixed, last, tiles, weight, finding, mask)


def heat_kernel(count, scale, stats_ref, keys_ref, finding_ref, mask_ref, heat_ref, held, kept, send_sem, recv_sem):
    slide = lax.axis_index("slide")
    me = lax.axis_index("seq")
    barrier = pltpu.get_barrier_semaphore()
    for hop in range(1, count):
        peer = lax.rem(me + hop, count)
        pl.semaphore_signal(
            barrier, inc=1, device_id=(slide, peer), device_id_type=pl.DeviceIdType.MESH
        )
    pl.semaphore_wait(barrier, count - 1)
    copies = []
    for hop in range(1, count):
        peer = lax.rem(me + hop, count)
        copy = pltpu.make_async_remote_copy(
            src_ref=stats_ref,
            dst_ref=held.at[hop],
            send_sem=send_sem.at[hop],
            recv_sem=recv_sem.at[hop],
            device_id=(slide, peer),
            device_id_type=pl.DeviceIdType.MESH,
        )
        copy.start()
        copies.append(copy)
    mask = mask_ref[...]
    for h in range(HEADS):
        cols = slice(h * HEAD, (h + 1) * HEAD)
        scores = lax.dot_general(
            keys_ref[:, cols], finding_ref[:, cols], (((1,), (1,)), ((), ())),
            preferred_element_type=F32,
        )
        kept[h] = jnp.exp2(scores * FACTOR + mask - stats_ref[h : h + 1, :])
    for copy in copies:
        copy.wait()
    everything = [stats_ref[...]] + [held[hop] for hop in range(1, count)]
    peaks = everything[0][:HEADS]
    for part in everything[1:]:
        peaks = jnp.maximum(peaks, part[:HEADS])
    totals = jnp.zeros_like(peaks)
    for part in everything:
        totals = totals + part[HEADS:] * jnp.exp2(part[:HEADS] - peaks)
    factors = jnp.exp2(everything[0][:HEADS] - peaks) * (scale / totals)
    slots = keys_ref.shape[0]
    chunk = 64
    for start in range(0, slots, chunk):
        rows = slice(start, start + chunk)
        total = kept[0, rows, :] * factors[0:1]
        for h in range(1, HEADS):
            total = total + kept[h, rows, :] * factors[h : h + 1]
        heat_ref[rows, :] = total


def heat_map(count, stats, keys, finding, mask):
    slots = keys.shape[0]
    finds = finding.shape[0]
    return pl.pallas_call(
        functools.partial(heat_kernel, count, count * slots / HEADS),
        in_specs=[pl.BlockSpec(memory_space=pltpu.VMEM)] * 4,
        out_specs=pl.BlockSpec(memory_space=pltpu.VMEM),
        out_shape=jax.ShapeDtypeStruct((slots, finds), F32),
        scratch_shapes=[
            pltpu.VMEM((count, 2 * HEADS, finds), F32),
            pltpu.VMEM((HEADS, slots, finds), F32),
            pltpu.SemaphoreType.DMA((count,)),
            pltpu.SemaphoreType.DMA((count,)),
        ],
        compiler_params=params(SMALL_LIMIT, collective_id=0, has_side_effects=True),
        name="heat_map",
    )(stats, keys, finding, mask)


def exchange(value, mask):
    pairs = [(source, source ^ mask) for source in range(lax.axis_size("seq"))]
    return lax.ppermute(value, "seq", pairs)


def shards(embeds, destination, norm_gain, qkv_weight, out_weight, finding_queries):
    devices = lax.axis_size(("slide", "seq"))
    seq_count = lax.axis_size("seq")
    slots = embeds.shape[0] * 2
    capacity = slots // devices
    padded = -(-capacity // 8) * 8
    width = embeds.shape[1]
    buffer, counts = dispatch(destination, embeds, devices, padded)
    received, counts = route(
        buffer.reshape(devices, padded, width), counts[None], devices, seq_count
    )
    tiles = received[:, :capacity].reshape(slots, width)
    pairs, near, far, normed, bias, mask = project(
        tiles, norm_gain, counts[:, 0], qkv_weight, capacity, seq_count
    )
    one = exchange(far, 2)
    pair = exchange(near, 1)
    query = project_query(normed, qkv_weight)
    mixed, summed, stats, quarter_query = near_attention(query, pairs, bias, pair)
    one, mixed = lax.optimization_barrier((one, mixed))
    two = exchange(one, 1)
    last = far_attention(quarter_query, bias, one, two, summed, stats)
    layer_out, keys, stats = finish(mixed, last, tiles, out_weight, finding_queries, mask)
    heat = heat_map(seq_count, stats, keys, finding_queries, mask)
    return (layer_out, heat)


LOG2_3 = math.log2(3.0)


def split(index, size):
    block = ((index.astype(F32) + 0.5) * (1.0 / size)).astype(jnp.int32)
    return block, index - block * size


def chunk_position(index, quarter):
    block, inner = split(index, quarter)
    phase = 2 * jnp.where((block == 1) | (block == 3), 1, 0) + (block >= 2).astype(jnp.int32)
    return 4 * inner + phase


def write_biases(capacity, slides, seq_count, counts, bias_ref, mask_ref):
    devices, lanes = counts.shape
    slots = mask_ref.shape[0]
    chunk = slots // slides
    half, quarter = chunk // 2, chunk // 4
    slide = lax.axis_index("slide")
    seq = lax.axis_index("seq")
    core = lax.rem(seq, 2)
    chip = lax.rem(seq // 2, 2)
    base = slide * seq_count + seq - core - 2 * chip
    members = [
        base + core + 2 * chip,
        base + (1 - core) + 2 * chip,
        base + core + 2 * (1 - chip),
        base + (1 - core) + 2 * (1 - chip),
    ]
    counts = counts.astype(F32)
    lane = lax.broadcasted_iota(jnp.int32, (devices, lanes), 1)
    columns = [
        jnp.sum(jnp.where(lane == member, counts, 0.0), axis=1, keepdims=True)
        for member in members
    ]
    sender = lax.broadcasted_iota(jnp.int32, (devices, slots), 0) * capacity
    index = lax.broadcasted_iota(jnp.int32, (1, slots), 1)

    def start_of(part):
        column = slide - part
        return chunk * jnp.where(column < 0, column + slides, column)

    def row(position, reached):
        place = (position - sender).astype(F32)
        inside = jnp.logical_and(place >= 0.0, place < reached)
        return (jnp.sum(inside.astype(F32), axis=0, keepdims=True) - 1.0) * (-MASKED)

    part, inner = split(index, chunk)
    block, _ = split(inner, quarter)
    own = row(start_of(part) + chunk_position(inner, quarter), columns[0])
    bias_ref[0:1, :] = own
    member, within = split(index, slots // 2)
    part, inner = split(within, half)
    sub, inner = split(inner, quarter)
    pair_rows = []
    for parity in range(2):
        in_half = jnp.where((block >= 2) == (parity == 1), 1.0, 0.0)
        bias_ref[1 + parity : 2 + parity, :] = own + in_half
        pair = row(start_of(part) + 4 * inner + parity + 2 * sub, columns[1])
        bias_ref[7 + parity : 8 + parity, :] = pair
        pair_rows.append(pair)
    member4, within4 = split(index, slots // 4)
    part4, inner4 = split(within4, quarter)
    reached = jnp.where(member4 >= 3, columns[3], columns[2])
    for phase in range(4):
        parity = phase % 2
        in_half = jnp.where((block >= 2) == (parity == 1), 1.0, 0.0)
        mine = jnp.where(block == QUARTER_OF[phase], LOG2_3, in_half)
        bias_ref[3 + phase : 4 + phase, :] = own + mine
        in_sub = jnp.where(sub == QUARTER_OF[phase] - 2 * parity, 1.0, 0.0)
        far = row(start_of(part4) + 4 * inner4 + phase, reached)
        bias_ref[9 + phase : 10 + phase, :] = jnp.where(
            member == 0, pair_rows[parity] + in_sub, far
        )
    bias_ref[13:16, :] = jnp.zeros((3, slots), F32)
    own = (lax.broadcasted_iota(jnp.int32, (8, lanes), 1) == members[0]).astype(F32)
    reached = lax.dot_general(
        own, counts, (((1,), (1,)), ((), ())), preferred_element_type=F32
    )[0:1, :]
    place = (
        lax.broadcasted_iota(jnp.int32, (slots, devices), 0)
        - lax.broadcasted_iota(jnp.int32, (slots, devices), 1) * capacity
    ).astype(F32)
    inside = jnp.logical_and(place >= 0.0, place < reached)
    mask_ref[...] = (jnp.sum(inside.astype(F32), axis=1, keepdims=True) - 1.0) * (-MASKED)


def pick(ref, parts, start, size, cols):
    step = ref.shape[0] // parts
    return jnp.concatenate(
        [ref[c * step + start : c * step + start + size, cols] for c in range(parts)], axis=0
    )


def put(ref, parts, start, cols, value):
    step, size = ref.shape[0] // parts, value.shape[0] // parts
    for c in range(parts):
        ref[c * step + start : c * step + start + size, cols] = value[c * size : (c + 1) * size]


def scores_of(query, parts, task):
    start, size, cols, pieces = task
    keys = jnp.concatenate([ref[:, cols] for ref, _, _ in pieces], axis=0)
    bias = jnp.concatenate([line for _, _, line in pieces], axis=1)
    scores = lax.dot_general(
        pick(query, parts, start, size, cols), keys, (((1,), (1,)), ((), ())),
        preferred_element_type=F32,
    )
    return scores * FACTOR + bias


def attend(query, mixed, parts, tasks):
    scores = scores_of(query, parts, tasks[0])
    for i, (start, _, cols, pieces) in enumerate(tasks):
        later = scores_of(query, parts, tasks[i + 1]) if i + 1 < len(tasks) else None
        values = jnp.concatenate([ref[:, at] for ref, at, _ in pieces], axis=0)
        weights = jnp.exp2(scores - jnp.max(scores, axis=1, keepdims=True))
        total = jnp.sum(weights, axis=1, keepdims=True)
        summed = jnp.dot(weights.astype(BF16), values, preferred_element_type=F32)
        put(mixed, parts, start, cols, ratio(summed, total))
        scores = later


def layer_kernel(
    capacity, slides, seq_count,
    row_ref, embeds_ref, gain_ref, weight_ref, out_weight_ref, finding_ref,
    layer_ref, heat_ref,
    sending, received, counts_ref, all_ref, weight, query, keys, near, far, normed_ref,
    pair, one, two, mixed, bias_ref, mask_ref, stats_ref, held,
    send, recv, count_send, count_recv, own_sem, weight_sem, near_send, near_recv,
    far_send, far_recv, pass_send, pass_recv, stat_send, stat_recv, out_sem,
):
    rows, width = embeds_ref.shape
    devices = slides * seq_count
    chunk = seq_count * capacity
    slots = slides * chunk
    half, quarter = chunk // 2, chunk // 4
    lanes = counts_ref.shape[1]
    groups = width // WIDE
    slide = lax.axis_index("slide")
    seq = lax.axis_index("seq")
    me = slide * seq_count + seq
    core_peer = seq + 1 - 2 * lax.rem(seq, 2)
    chip_peer = seq + 2 - 4 * lax.rem(seq // 2, 2)
    barrier = pltpu.get_barrier_semaphore()

    def place_of(hop):
        return (lax.rem(slide + hop // seq_count, slides), lax.rem(seq + lax.rem(hop, seq_count), seq_count))

    def remote(src, dst, send_sem, recv_sem, where):
        return pltpu.make_async_remote_copy(
            src_ref=src,
            dst_ref=dst,
            send_sem=send_sem,
            recv_sem=recv_sem,
            device_id=where,
            device_id_type=pl.DeviceIdType.MESH,
        )

    def greet(hop, carry):
        pl.semaphore_signal(
            barrier, inc=1, device_id=place_of(hop), device_id_type=pl.DeviceIdType.MESH
        )
        return carry

    lax.fori_loop(1, devices, greet, 0)
    load = pltpu.make_async_copy(weight_ref, weight, weight_sem.at[0])
    load.start()

    row = row_ref[...]
    col = jnp.transpose(jnp.broadcast_to(row.astype(F32), (128, rows)))[:, 0:1].astype(jnp.int32)
    first = lax.broadcasted_iota(jnp.int32, (rows, rows), 0)
    second = lax.broadcasted_iota(jnp.int32, (rows, rows), 1)
    same = jnp.logical_and(col == row, first < second)
    rank = jnp.sum(same.astype(F32), axis=0, keepdims=True).astype(jnp.int32)
    place = row * capacity + rank
    lane = lax.broadcasted_iota(jnp.int32, (rows, lanes), 1)
    tally = jnp.sum((col == lane).astype(F32), axis=0, keepdims=True).astype(jnp.int32)
    counts_ref[...] = jnp.broadcast_to(tally, counts_ref.shape)

    def count_copy(hop):
        return remote(
            counts_ref, all_ref.at[me], count_send.at[hop], count_recv.at[hop], place_of(hop)
        )

    def row_copy(hop):
        where = place_of(hop)
        return remote(
            sending.at[where[0] * seq_count + where[1]],
            received.at[me],
            send.at[hop],
            recv.at[hop],
            where,
        )

    def each(make, method, low, high):
        def step(hop, carry):
            getattr(make(hop), method)()
            return carry

        lax.fori_loop(low, high, step, 0)

    def fill(k):
        column = lax.rem(slide + k, slides)
        wanted = lax.broadcasted_iota(jnp.int32, (chunk, rows), 0) + column * chunk
        chosen = (wanted == place).astype(F32).astype(BF16)
        for start in range(0, width, WIDE):
            part = jnp.dot(
                chosen, embeds_ref[:, start : start + WIDE], preferred_element_type=F32
            )
            sending[pl.ds(column * seq_count, seq_count), :, start : start + WIDE] = part.reshape(
                seq_count, capacity, WIDE
            ).astype(BF16)

    fill(0)
    pl.semaphore_wait(barrier, devices - 1)
    each(row_copy, "start", 1, seq_count)
    own = pltpu.make_async_copy(sending.at[me], received.at[me], own_sem)
    own.start()
    all_ref[pl.ds(me, 1)] = counts_ref[...][None]

    def fill_next(k, carry):
        fill(k)
        each(row_copy, "start", k * seq_count, (k + 1) * seq_count)
        return carry

    lax.fori_loop(1, slides, fill_next, 0)
    each(count_copy, "start", 1, devices)

    def near_copy(k):
        part = pl.ds(pl.multiple_of(k * half, half), half)
        return remote(
            near.at[part], pair.at[part], near_send.at[k], near_recv.at[k], (slide, core_peer)
        )

    def far_copy(k):
        part = pl.ds(pl.multiple_of(k * quarter, quarter), quarter)
        return remote(
            far.at[part], one.at[part], far_send.at[k], far_recv.at[k], (slide, chip_peer)
        )

    def pass_copy(k):
        part = pl.ds(pl.multiple_of(k * quarter, quarter), quarter)
        return remote(
            one.at[part], two.at[part], pass_send.at[k], pass_recv.at[k], (slide, core_peer)
        )

    index = lax.broadcasted_iota(jnp.int32, (chunk, 1), 0)
    position = lax.broadcasted_iota(jnp.int32, (chunk, chunk), 1)
    order = (chunk_position(index, quarter) == position).astype(F32).astype(BF16)

    def work(k):
        c = lax.rem(slide - k + slides, slides)
        part = pl.ds(pl.multiple_of(k * chunk, chunk), chunk)
        group = pl.ds(c * seq_count, seq_count)
        square = jnp.zeros((chunk, 1), F32)
        for start in range(0, width, WIDE):
            tile = received[group, :, start : start + WIDE].astype(F32).reshape(chunk, WIDE)
            square = square + jnp.sum(tile * tile, axis=1, keepdims=True)
        inverse = lax.rsqrt(square * (1.0 / width) + EPSILON)
        for start in range(0, width, WIDE):
            tile = received[group, :, start : start + WIDE].astype(F32).reshape(chunk, WIDE)
            gain = jnp.concatenate(
                [gain_ref[i : i + 1, :] for i in range(start // HEAD, (start + WIDE) // HEAD)], axis=1
            )
            normed = (tile * inverse * gain).astype(BF16)
            normed_ref[:, start : start + WIDE] = jnp.dot(
                order, normed, preferred_element_type=F32
            ).astype(BF16)

        def pairs(g, carry):
            at = pl.multiple_of(g * WIDE, WIDE)
            value = jnp.dot(
                normed_ref[...], weight[:, pl.ds(at + width, WIDE)], preferred_element_type=F32
            ).astype(BF16)
            keys[part, pl.ds(at, WIDE)] = value
            for j in range(GROUP):
                cols = pl.ds(at + j * HEAD, HEAD)
                begin = (j % 2) * half
                near[pl.ds(pl.multiple_of(k * half, half), half), cols] = value[
                    begin : begin + half, j * HEAD : (j + 1) * HEAD
                ]
                begin = QUARTER_OF[j] * quarter
                far[pl.ds(pl.multiple_of(k * quarter, quarter), quarter), cols] = value[
                    begin : begin + quarter, j * HEAD : (j + 1) * HEAD
                ]
            return carry

        def single(g, carry):
            at = pl.multiple_of(g * WIDE, WIDE)
            query[part, pl.ds(at, WIDE)] = jnp.dot(
                normed_ref[...], weight[:, pl.ds(at, WIDE)], preferred_element_type=F32
            ).astype(BF16)
            return carry

        lax.fori_loop(0, 2 * groups, pairs, 0)
        far_copy(k).start()
        near_copy(k).start()
        lax.fori_loop(0, groups, single, 0)

    own.wait()
    load.wait()

    def step(k, carry):
        @pl.when(k == slides - 1)
        def _():
            each(count_copy, "wait", 1, devices)
            write_biases(
                capacity, slides, seq_count, jnp.max(all_ref[...], axis=1), bias_ref, mask_ref
            )

        each(row_copy, "wait_recv", jnp.maximum(k * seq_count, 1), (k + 1) * seq_count)
        work(k)
        return carry

    lax.fori_loop(0, slides, step, 0)
    again = pltpu.make_async_copy(
        out_weight_ref, weight.at[:, pl.ds(0, width)], weight_sem.at[1]
    )
    again.start()

    def forward(k, carry):
        far_copy(k).wait_recv()
        pass_copy(k).start()
        return carry

    each(near_copy, "wait_recv", 0, slides)

    def head_cols(g, j):
        at = pl.multiple_of(g * WIDE + j * HEAD, HEAD)
        return pl.ds(at, HEAD), pl.ds(pl.multiple_of(at + width, HEAD), HEAD)

    def near_pass(g, carry):
        tasks = []
        for j in range(GROUP):
            cols, at = head_cols(g, j)
            start = (j % 2) * half
            done = start + quarter - (QUARTER_OF[j] * quarter - start)
            tasks.append((half - start, half, cols, [(keys, at, bias_ref[0:1, :])]))
            tasks.append((done, quarter, cols, [
                (keys, at, bias_ref[1 + j % 2 : 2 + j % 2, :]),
                (pair, at, bias_ref[7 + j % 2 : 8 + j % 2, : slots // 2]),
            ]))
        attend(query, mixed, slides, tasks)
        return carry

    def far_pass(g, carry):
        count = slots // 4
        tasks = []
        for j in range(GROUP):
            cols, at = head_cols(g, j)
            line = slice(9 + j, 10 + j)
            tasks.append((QUARTER_OF[j] * quarter, quarter, cols, [
                (keys, at, bias_ref[3 + j : 4 + j, :]),
                (pair, at, bias_ref[line, : 2 * count]),
                (one, at, bias_ref[line, 2 * count : 3 * count]),
                (two, at, bias_ref[line, 3 * count :]),
            ]))
        attend(query, mixed, slides, tasks)
        return carry

    lax.fori_loop(0, groups - 1, near_pass, 0)
    lax.fori_loop(0, slides, forward, 0)
    lax.fori_loop(groups - 1, groups, near_pass, 0)
    each(pass_copy, "wait_recv", 0, slides)
    lax.fori_loop(0, groups, far_pass, 0)

    def restore(k, carry):
        c = lax.rem(slide - k + slides, slides)
        place = pl.ds(pl.multiple_of(c * chunk, chunk), chunk)
        part = pl.ds(pl.multiple_of(k * chunk, chunk), chunk)
        for start in range(0, width, WIDE):
            query[place, start : start + WIDE] = lax.dot_general(
                order, mixed[part, start : start + WIDE], (((0,), (0,)), ((), ())),
                preferred_element_type=F32,
            ).astype(BF16)
        return carry

    lax.fori_loop(0, slides, restore, 0)
    again.wait()
    def output(g, square):
        cols = pl.ds(pl.multiple_of(g * WIDE, WIDE), WIDE)
        added = jnp.dot(query[...], weight[:, cols], preferred_element_type=F32)
        tile = received[:, :, cols].astype(F32).reshape(slots, WIDE)
        out = (tile + added).astype(BF16)
        keys[:, cols] = out
        wide = out.astype(F32)
        return square + jnp.sum(wide * wide, axis=1, keepdims=True)

    square = lax.fori_loop(0, groups, output, jnp.zeros((slots, 1), F32))
    store = pltpu.make_async_copy(keys.at[:, pl.ds(0, width)], layer_ref, out_sem)
    store.start()
    inverse = lax.rsqrt(square * (1.0 / width) + EPSILON)
    mask = mask_ref[...]

    def stat_copy(hop):
        half = hop // seq_count
        hop_in = lax.rem(hop, seq_count)
        return remote(
            stats_ref.at[half], held.at[hop], stat_send.at[hop], stat_recv.at[hop],
            (slide, lax.rem(seq + hop_in, seq_count)),
        )

    def find(kept):
        per = HEADS // 2
        local = []
        for part in range(2):
            for i in range(per):
                h = part * per + i
                cols = slice(h * HEAD, (h + 1) * HEAD)
                found = (keys[:, cols].astype(F32) * inverse).astype(BF16)
                scores = lax.dot_general(
                    found, finding_ref[:, cols], (((1,), (1,)), ((), ())), preferred_element_type=F32
                )
                scores = scores * FACTOR + mask
                peak = jnp.max(scores, axis=0, keepdims=True)
                raised = jnp.exp2(scores - peak)
                kept[h] = raised
                local.append(peak)
                stats_ref[part, i : i + 1, :] = peak + jnp.log2(
                    jnp.sum(raised, axis=0, keepdims=True)
                )
            stats_ref[part, per:, :] = jnp.zeros((8 - per, finding_ref.shape[0]), F32)
            each(stat_copy, "start", part * seq_count + 1, (part + 1) * seq_count)
        factors = []
        for part in range(2):
            each(stat_copy, "wait_recv", part * seq_count + 1, (part + 1) * seq_count)
            logs = [stats_ref[part]] + [held[part * seq_count + hop] for hop in range(1, seq_count)]
            top = functools.reduce(jnp.maximum, logs)
            total = functools.reduce(jnp.add, [jnp.exp2(log - top) for log in logs])
            shares = (seq_count * slots / HEADS) / total
            for i in range(per):
                factors.append(
                    shares[i : i + 1] * jnp.exp2(local[part * per + i] - top[i : i + 1])
                )
        small = 64
        for start in range(0, slots, small):
            part = slice(start, start + small)
            total = kept[0, part, :] * factors[0]
            for h in range(1, HEADS):
                total = total + kept[h, part, :] * factors[h]
            heat_ref[part, :] = total

    pl.run_scoped(find, pltpu.VMEM((HEADS, slots, finding_ref.shape[0]), F32))
    each(row_copy, "wait_send", 1, devices)
    each(near_copy, "wait_send", 0, slides)
    each(far_copy, "wait_send", 0, slides)
    each(pass_copy, "wait_send", 0, slides)
    each(stat_copy, "wait_send", 1, seq_count)
    each(stat_copy, "wait_send", seq_count + 1, 2 * seq_count)
    store.wait()


def layer(destination, embeds, gain, weight, out_weight, finding, capacity, slides, seq_count):
    rows, width = embeds.shape
    finds = finding.shape[0]
    devices = slides * seq_count
    slots = devices * capacity
    chunk = seq_count * capacity
    lanes = max(128, devices)
    vmem = pl.BlockSpec(memory_space=pltpu.VMEM)
    anywhere = pl.BlockSpec(memory_space=pl.ANY)
    dma = pltpu.SemaphoreType.DMA
    return pl.pallas_call(
        functools.partial(layer_kernel, capacity, slides, seq_count),
        in_specs=[vmem, vmem, vmem, anywhere, anywhere, vmem],
        out_specs=[anywhere, vmem],
        out_shape=(
            jax.ShapeDtypeStruct((slots, width), BF16),
            jax.ShapeDtypeStruct((slots, finds), F32),
        ),
        scratch_shapes=[
            pltpu.VMEM((devices, capacity, width), BF16),
            pltpu.VMEM((devices, capacity, width), BF16),
            pltpu.VMEM((8, lanes), jnp.int32),
            pltpu.VMEM((devices, 8, lanes), jnp.int32),
            pltpu.VMEM(weight.shape, BF16),
            pltpu.VMEM((slots, width), BF16),
            pltpu.VMEM((slots, 2 * width), BF16),
            pltpu.VMEM((slots // 2, 2 * width), BF16),
            pltpu.VMEM((slots // 4, 2 * width), BF16),
            pltpu.VMEM((chunk, width), BF16),
            pltpu.VMEM((slots // 2, 2 * width), BF16),
            pltpu.VMEM((slots // 4, 2 * width), BF16),
            pltpu.VMEM((slots // 4, 2 * width), BF16),
            pltpu.VMEM((slots, width), BF16),
            pltpu.VMEM((16, slots), F32),
            pltpu.VMEM((slots, 1), F32),
            pltpu.VMEM((2, 8, finds), F32),
            pltpu.VMEM((2 * seq_count, 8, finds), F32),
            dma((devices,)),
            dma((devices,)),
            dma((devices,)),
            dma((devices,)),
            dma,
            dma((2,)),
            dma((slides,)),
            dma((slides,)),
            dma((slides,)),
            dma((slides,)),
            dma((slides,)),
            dma((slides,)),
            dma((2 * seq_count,)),
            dma((2 * seq_count,)),
            dma,
        ],
        compiler_params=params(LAYER_LIMIT, collective_id=2, has_side_effects=True),
        cost_estimate=pl.CostEstimate(
            flops=8 * slots * width * width + 8 * slots * slots * width,
            bytes_accessed=30_000_000,
            transcendentals=20_000_000,
        ),
        name="layer",
    )(destination.reshape(1, rows), embeds, gain.reshape(width // HEAD, HEAD), weight, out_weight, finding)


LAYER_LIMIT = 60 * 1024 * 1024


def layer_shards(embeds, destination, norm_gain, qkv_weight, out_weight, finding_queries):
    slides = lax.axis_size("slide")
    seq_count = lax.axis_size("seq")
    slots = embeds.shape[0] * 2
    capacity = slots // (slides * seq_count)
    return layer(
        destination, embeds, norm_gain, qkv_weight, out_weight, finding_queries,
        capacity, slides, seq_count,
    )


def solution(mesh):
    in_specs = (P(("slide", "seq"), None), P(("slide", "seq"), None), P(), P(), P(), P())
    out_specs = (P(("slide", "seq"), None), P(("slide", "seq"), None))

    def program(embeds, *rest):
        devices = mesh.shape["slide"] * mesh.shape["seq"]
        capacity = embeds.shape[0] * 2 // devices // devices
        chunk = capacity * mesh.shape["seq"]
        body = layer_shards if capacity % 8 == 0 and chunk % 64 == 0 else shards
        return jax.shard_map(
            body, mesh=mesh, in_specs=in_specs, out_specs=out_specs, check_vma=False
        )(embeds, *rest)

    return program
```

```python
import functools
import math

import jax
import jax.numpy as jnp
from jax import lax
from jax.experimental import pallas as pl
from jax.experimental.pallas import tpu as pltpu
from jax.sharding import PartitionSpec as P

HEADS = 12
HEAD = 128
GROUP = 4
WIDE = GROUP * HEAD
MASKED = -1e30
EPSILON = 1e-06
FACTOR = math.log2(math.e) / math.sqrt(HEAD)
F32 = jnp.float32
BF16 = jnp.bfloat16
QUARTER_OF = (0, 2, 1, 3)
VMEM_LIMIT = 56 * 1024 * 1024
SMALL_LIMIT = 34 * 1024 * 1024


def params(limit=VMEM_LIMIT, **more):
    return pltpu.CompilerParams(vmem_limit_bytes=limit, **more)


def dispatch_kernel(capacity, row_ref, embeds_ref, buffer_ref, counts_ref):
    rows = embeds_ref.shape[0]
    slots = buffer_ref.shape[0]
    row = row_ref[...]
    col = jnp.transpose(jnp.broadcast_to(row.astype(F32), (128, rows)))[:, 0:1].astype(jnp.int32)
    first = lax.broadcasted_iota(jnp.int32, (rows, rows), 0)
    second = lax.broadcasted_iota(jnp.int32, (rows, rows), 1)
    same = jnp.logical_and(col == row, first < second)
    rank = jnp.sum(same.astype(F32), axis=0, keepdims=True).astype(jnp.int32)
    place = row * capacity + rank
    lanes = lax.broadcasted_iota(jnp.int32, (rows, counts_ref.shape[1]), 1)
    counts_ref[...] = jnp.sum((col == lanes).astype(F32), axis=0, keepdims=True).astype(jnp.int32)
    chosen = (lax.broadcasted_iota(jnp.int32, (slots, rows), 0) == place).astype(F32).astype(BF16)
    for start in range(0, embeds_ref.shape[1], WIDE):
        part = embeds_ref[:, start : start + WIDE]
        buffer_ref[:, start : start + WIDE] = jnp.dot(
            chosen, part, preferred_element_type=F32
        ).astype(BF16)


def dispatch(destination, embeds, devices, capacity):
    rows, width = embeds.shape
    slots = devices * capacity
    return pl.pallas_call(
        functools.partial(dispatch_kernel, capacity),
        out_shape=(
            jax.ShapeDtypeStruct((slots, width), BF16),
            jax.ShapeDtypeStruct((1, max(128, devices)), jnp.int32),
        ),
        compiler_params=params(),
        name="dispatch",
    )(destination.reshape(1, rows), embeds)


def original_of(index, quarter):
    block = (
        (index >= quarter).astype(jnp.int32)
        + (index >= 2 * quarter).astype(jnp.int32)
        + (index >= 3 * quarter).astype(jnp.int32)
    )
    phase = 2 * jnp.where((block == 1) | (block == 3), 1, 0) + (block >= 2).astype(jnp.int32)
    return 4 * (index - quarter * block) + phase


def route_kernel(devices, seq_count, buffer_ref, counts_ref, tiles_ref, all_ref, send, recv, count_send, count_recv, own_sem):
    me = lax.axis_index("slide") * seq_count + lax.axis_index("seq")
    barrier = pltpu.get_barrier_semaphore()

    def place_of(hop):
        peer = lax.rem(me + hop, devices)
        return peer, (peer // seq_count, lax.rem(peer, seq_count))

    def greet(hop, carry):
        pl.semaphore_signal(
            barrier, inc=1, device_id=place_of(hop)[1], device_id_type=pl.DeviceIdType.MESH
        )
        return carry

    lax.fori_loop(1, devices, greet, 0)
    pl.semaphore_wait(barrier, devices - 1)

    def copies(hop):
        peer, where = place_of(hop)
        rows = pltpu.make_async_remote_copy(
            src_ref=buffer_ref.at[peer],
            dst_ref=tiles_ref.at[me],
            send_sem=send.at[hop],
            recv_sem=recv.at[hop],
            device_id=where,
            device_id_type=pl.DeviceIdType.MESH,
        )
        count = pltpu.make_async_remote_copy(
            src_ref=counts_ref.at[0],
            dst_ref=all_ref.at[me],
            send_sem=count_send.at[hop],
            recv_sem=count_recv.at[hop],
            device_id=where,
            device_id_type=pl.DeviceIdType.MESH,
        )
        return rows, count

    def begin(hop, carry):
        for copy in copies(hop):
            copy.start()
        return carry

    def end(hop, carry):
        for copy in copies(hop):
            copy.wait()
        return carry

    own_rows = pltpu.make_async_copy(buffer_ref.at[me], tiles_ref.at[me], own_sem.at[0])
    own_count = pltpu.make_async_copy(counts_ref.at[0], all_ref.at[me], own_sem.at[1])
    lax.fori_loop(1, devices, begin, 0)
    own_rows.start()
    own_count.start()
    own_rows.wait()
    own_count.wait()
    lax.fori_loop(1, devices, end, 0)


def route(buffer, counts, devices, seq_count):
    capacity, width = buffer.shape[1:]
    lanes = counts.shape[2]
    return pl.pallas_call(
        functools.partial(route_kernel, devices, seq_count),
        in_specs=[pl.BlockSpec(memory_space=pl.ANY)] * 2,
        out_specs=[pl.BlockSpec(memory_space=pl.ANY)] * 2,
        out_shape=(
            jax.ShapeDtypeStruct((devices, capacity, width), BF16),
            jax.ShapeDtypeStruct((devices, 1, lanes), jnp.int32),
        ),
        scratch_shapes=[pltpu.SemaphoreType.DMA((devices,))] * 4
        + [pltpu.SemaphoreType.DMA((2,))],
        compiler_params=pltpu.CompilerParams(collective_id=1, has_side_effects=True),
        name="route",
    )(buffer, counts)


def write_masks(capacity, seq_count, counts_ref, bias_ref, mask_ref):
    devices, lanes = counts_ref.shape
    slots = mask_ref.shape[0]
    half, quarter = slots // 2, slots // 4
    slide = lax.axis_index("slide")
    seq = lax.axis_index("seq")
    core = lax.rem(seq, 2)
    chip = lax.rem(seq // 2, 2)
    base = slide * seq_count + seq - core - 2 * chip
    members = [
        base + core + 2 * chip,
        base + (1 - core) + 2 * chip,
        base + core + 2 * (1 - chip),
        base + (1 - core) + 2 * (1 - chip),
    ]
    counts = counts_ref[...].astype(F32)
    lane = lax.broadcasted_iota(jnp.int32, (devices, lanes), 1)
    columns = [
        jnp.sum(jnp.where(lane == member, counts, 0.0), axis=1, keepdims=True)
        for member in members
    ]
    sender = lax.broadcasted_iota(jnp.int32, (devices, slots), 0) * capacity
    index = lax.broadcasted_iota(jnp.int32, (devices, slots), 1)

    def row(position, reached):
        place = (position - sender).astype(F32)
        inside = jnp.logical_and(place >= 0.0, place < reached)
        return (jnp.sum(inside.astype(F32), axis=0, keepdims=True) - 1.0) * (-MASKED)

    bias_ref[0:1, :] = row(original_of(index, quarter), columns[0])
    within = jnp.where(index >= half, index - half, index)
    for parity in range(2):
        reached = jnp.where(index >= half, columns[1], columns[0])
        bias_ref[1 + parity : 2 + parity, :] = row(
            original_of(within + parity * half, quarter), reached
        )
    for phase in range(4):
        block = (
            (index >= quarter).astype(jnp.int32)
            + (index >= 2 * quarter).astype(jnp.int32)
            + (index >= 3 * quarter).astype(jnp.int32)
        )
        reached = jnp.where(
            index >= half,
            jnp.where(index >= 3 * quarter, columns[3], columns[2]),
            jnp.where(index >= quarter, columns[1], columns[0]),
        )
        bias_ref[3 + phase : 4 + phase, :] = row(4 * (index - quarter * block) + phase, reached)
    bias_ref[7:8, :] = jnp.zeros((1, slots), F32)
    own = (lax.broadcasted_iota(jnp.int32, (8, lanes), 1) == members[0]).astype(F32)
    reached = lax.dot_general(
        own, counts, (((1,), (1,)), ((), ())), preferred_element_type=F32
    )[0:1, :]
    place = (
        lax.broadcasted_iota(jnp.int32, (slots, devices), 0)
        - lax.broadcasted_iota(jnp.int32, (slots, devices), 1) * capacity
    ).astype(F32)
    inside = jnp.logical_and(place >= 0.0, place < reached)
    mask_ref[...] = (jnp.sum(inside.astype(F32), axis=1, keepdims=True) - 1.0) * (-MASKED)


def project_kernel(capacity, seq_count, tiles_ref, gain_ref, counts_ref, weight_ref, out_ref, near_ref, far_ref, normed_ref, bias_ref, mask_ref):
    step = pl.program_id(0)
    slots, width = tiles_ref.shape
    quarter = slots // 4
    half = slots // 2

    @pl.when(step == 0)
    def _():
        tile = tiles_ref[...].astype(F32)
        mean = jnp.mean(tile * tile, axis=1, keepdims=True)
        normed = (tile * lax.rsqrt(mean + EPSILON) * gain_ref[...]).astype(BF16)
        index = lax.broadcasted_iota(jnp.int32, (slots, slots), 0)
        position = lax.broadcasted_iota(jnp.int32, (slots, slots), 1)
        order = (original_of(index, quarter) == position).astype(F32).astype(BF16)
        for start in range(0, width, WIDE):
            normed_ref[:, start : start + WIDE] = jnp.dot(
                order, normed[:, start : start + WIDE], preferred_element_type=F32
            ).astype(BF16)
        write_masks(capacity, seq_count, counts_ref, bias_ref, mask_ref)

    value = jnp.dot(normed_ref[...], weight_ref[...], preferred_element_type=F32).astype(BF16)
    out_ref[...] = value
    for j in range(GROUP):
        cols = slice(j * HEAD, (j + 1) * HEAD)
        near_ref[:, cols] = value[(j % 2) * half : (j % 2 + 1) * half, cols]
        begin = QUARTER_OF[j] * quarter
        far_ref[:, cols] = value[begin : begin + quarter, cols]


def project(tiles, gain, counts, weight, capacity, seq_count):
    slots, width = tiles.shape
    steps = width // WIDE
    whole = lambda i: (0, 0)
    return pl.pallas_call(
        functools.partial(project_kernel, capacity, seq_count),
        grid=(2 * steps,),
        in_specs=[
            pl.BlockSpec((slots, width), whole),
            pl.BlockSpec((1, width), whole),
            pl.BlockSpec(counts.shape, whole),
            pl.BlockSpec((width, WIDE), lambda i: (0, i + steps)),
        ],
        out_specs=[
            pl.BlockSpec((slots, WIDE), lambda i: (0, i)),
            pl.BlockSpec((slots // 2, WIDE), lambda i: (0, i)),
            pl.BlockSpec((slots // 4, WIDE), lambda i: (0, i)),
            pl.BlockSpec((slots, width), whole),
            pl.BlockSpec((8, slots), whole),
            pl.BlockSpec((slots, 1), whole),
        ],
        out_shape=(
            jax.ShapeDtypeStruct((slots, 2 * width), BF16),
            jax.ShapeDtypeStruct((slots // 2, 2 * width), BF16),
            jax.ShapeDtypeStruct((slots // 4, 2 * width), BF16),
            jax.ShapeDtypeStruct((slots, width), BF16),
            jax.ShapeDtypeStruct((8, slots), F32),
            jax.ShapeDtypeStruct((slots, 1), F32),
        ),
        compiler_params=params(),
        name="project",
    )(tiles, gain.reshape(1, width), counts, weight)


def query_kernel(normed_ref, weight_ref, out_ref):
    out_ref[...] = jnp.dot(
        normed_ref[...], weight_ref[...], preferred_element_type=F32
    ).astype(BF16)


def project_query(normed, weight):
    slots, width = normed.shape
    return pl.pallas_call(
        query_kernel,
        grid=(width // WIDE,),
        in_specs=[
            pl.BlockSpec((slots, width), lambda i: (0, 0)),
            pl.BlockSpec((width, WIDE), lambda i: (0, i)),
        ],
        out_specs=pl.BlockSpec((slots, WIDE), lambda i: (0, i)),
        out_shape=jax.ShapeDtypeStruct((slots, width), BF16),
        compiler_params=params(),
        cost_estimate=pl.CostEstimate(
            flops=2 * slots * width * width, bytes_accessed=10_000_000, transcendentals=0
        ),
        name="project_query",
    )(normed, weight)


def softmax_parts(query, keys, values, bias):
    scores = lax.dot_general(
        query, keys, (((1,), (1,)), ((), ())), preferred_element_type=F32
    )
    scores = scores * FACTOR + bias
    peak = jnp.max(scores, axis=1, keepdims=True)
    weights = jnp.exp2(scores - peak)
    total = jnp.sum(weights, axis=1, keepdims=True)
    summed = jnp.dot(weights.astype(BF16), values, preferred_element_type=F32)
    return summed, peak, total


def merge(parts):
    top = parts[0][1]
    for _, peak, _ in parts[1:]:
        top = jnp.maximum(top, peak)
    above, below = 0.0, 0.0
    for summed, peak, total in parts:
        factor = jnp.exp2(peak - top)
        above = above + factor * summed
        below = below + factor * total
    return above, top, below


def ratio(above, below):
    return (above * (1.0 / jnp.maximum(below, 1.0))).astype(BF16)


def near_attention_kernel(
    q_ref, k_ref, v_ref, bias_ref, pair_k, pair_v, mixed_ref, summed_ref, stats_ref, query_ref
):
    slots = q_ref.shape[0]
    half, quarter = slots // 2, slots // 4
    lanes = lax.broadcasted_iota(jnp.int32, (quarter, HEAD), 1)
    stats = jnp.zeros((quarter, HEAD), F32)
    for j in range(GROUP):
        cols = slice(j * HEAD, (j + 1) * HEAD)
        start = (j % 2) * half
        inside = QUARTER_OF[j] * quarter - start
        mine = slice(start, start + half)
        other = slice(half - start, 2 * half - start)
        summed, _, total = softmax_parts(
            q_ref[other, cols], k_ref[:, cols], v_ref[:, cols], bias_ref[0:1, :]
        )
        mixed_ref[other, cols] = ratio(summed, total)
        one = softmax_parts(q_ref[mine, cols], k_ref[:, cols], v_ref[:, cols], bias_ref[0:1, :])
        keys = jnp.concatenate([k_ref[mine, cols], pair_k[:, cols]], axis=0)
        values = jnp.concatenate([v_ref[mine, cols], pair_v[:, cols]], axis=0)
        two = softmax_parts(q_ref[mine, cols], keys, values, bias_ref[1 + j % 2 : 2 + j % 2, :])
        above, top, below = merge([one, two])
        done = quarter - inside
        mixed_ref[start + done : start + done + quarter, cols] = ratio(
            above[done : done + quarter], below[done : done + quarter]
        )
        begin = start + inside
        fourth = slice(begin, begin + quarter)
        within = slice(inside, inside + quarter)
        keys = jnp.concatenate([k_ref[fourth, cols], pair_k[within, cols]], axis=0)
        values = jnp.concatenate([v_ref[fourth, cols], pair_v[within, cols]], axis=0)
        four = softmax_parts(q_ref[fourth, cols], keys, values, bias_ref[3 + j : 4 + j, :half])
        above, top, below = merge([(above[within], top[within], below[within]), four])
        summed_ref[:, cols] = above
        stats = jnp.where(lanes == 2 * j, top, jnp.where(lanes == 2 * j + 1, below, stats))
        query_ref[:, cols] = q_ref[fourth, cols]
        mixed_ref[fourth, cols] = jnp.zeros((quarter, HEAD), BF16)
    stats_ref[...] = stats


def halves(array, steps):
    rows = array.shape[0]
    return [
        pl.BlockSpec((rows, WIDE), lambda i: (0, i)),
        pl.BlockSpec((rows, WIDE), lambda i: (0, i + steps)),
    ]


def near_attention(query, pairs, bias, pair):
    slots, width = query.shape
    quarter = slots // 4
    steps = width // WIDE
    return pl.pallas_call(
        near_attention_kernel,
        grid=(steps,),
        in_specs=[
            pl.BlockSpec((slots, WIDE), lambda i: (0, i)),
            *halves(pairs, steps),
            pl.BlockSpec(bias.shape, lambda i: (0, 0)),
            *halves(pair, steps),
        ],
        out_specs=[
            pl.BlockSpec((slots, WIDE), lambda i: (0, i)),
            pl.BlockSpec((quarter, WIDE), lambda i: (0, i)),
            pl.BlockSpec((quarter, HEAD), lambda i: (0, i)),
            pl.BlockSpec((quarter, WIDE), lambda i: (0, i)),
        ],
        out_shape=(
            jax.ShapeDtypeStruct((slots, width), BF16),
            jax.ShapeDtypeStruct((quarter, width), F32),
            jax.ShapeDtypeStruct((quarter, steps * HEAD), F32),
            jax.ShapeDtypeStruct((quarter, width), BF16),
        ),
        compiler_params=params(SMALL_LIMIT),
        cost_estimate=pl.CostEstimate(
            flops=12 * slots * slots * width,
            bytes_accessed=14_000_000,
            transcendentals=6 * slots * slots * HEADS,
        ),
        name="near_attention",
    )(query, pairs, pairs, bias, pair, pair)


def far_attention_kernel(
    q_ref, bias_ref, one_k, one_v, two_k, two_v, summed_ref, stats_ref, mixed_ref
):
    half = bias_ref.shape[1] // 2
    for j in range(GROUP):
        cols = slice(j * HEAD, (j + 1) * HEAD)
        keys = jnp.concatenate([one_k[:, cols], two_k[:, cols]], axis=0)
        values = jnp.concatenate([one_v[:, cols], two_v[:, cols]], axis=0)
        four = softmax_parts(q_ref[:, cols], keys, values, bias_ref[3 + j : 4 + j, half:])
        before = (
            summed_ref[:, cols],
            stats_ref[:, 2 * j : 2 * j + 1],
            stats_ref[:, 2 * j + 1 : 2 * j + 2],
        )
        above, _, below = merge([before, four])
        mixed_ref[:, cols] = ratio(above, below)


def far_attention(query, bias, one, two, summed, stats):
    quarter, width = query.shape
    steps = width // WIDE
    block = pl.BlockSpec((quarter, WIDE), lambda i: (0, i))
    return pl.pallas_call(
        far_attention_kernel,
        grid=(steps,),
        in_specs=[
            block,
            pl.BlockSpec(bias.shape, lambda i: (0, 0)),
            *halves(one, steps),
            *halves(two, steps),
            block,
            pl.BlockSpec((quarter, HEAD), lambda i: (0, i)),
        ],
        out_specs=block,
        out_shape=jax.ShapeDtypeStruct((quarter, width), BF16),
        compiler_params=params(SMALL_LIMIT),
        name="far_attention",
    )(query, bias, one, one, two, two, summed, stats)


def finish_kernel(mixed_ref, last_ref, tiles_ref, weight_ref, finding_ref, mask_ref, layer_ref, keys_ref, stats_ref, plain_ref):
    slots, width = tiles_ref.shape
    quarter = slots // 4
    position = lax.broadcasted_iota(jnp.int32, (slots, slots), 0)
    index = lax.broadcasted_iota(jnp.int32, (slots, slots), 1)
    order = (original_of(index, quarter) == position).astype(F32).astype(BF16)
    for start in range(0, width, WIDE):
        heads = []
        for j in range(GROUP):
            cols = slice(start + j * HEAD, start + (j + 1) * HEAD)
            begin = QUARTER_OF[j] * quarter
            pieces = [last_ref[:, cols]]
            if begin > 0:
                pieces.insert(0, mixed_ref[:begin, cols])
            if begin + quarter < slots:
                pieces.append(mixed_ref[begin + quarter :, cols])
            heads.append(jnp.concatenate(pieces, axis=0))
        plain_ref[:, start : start + WIDE] = jnp.dot(
            order, jnp.concatenate(heads, axis=1), preferred_element_type=F32
        ).astype(BF16)
    square = jnp.zeros((slots, 1), F32)
    for start in range(0, width, WIDE):
        cols = slice(start, start + WIDE)
        added = jnp.dot(plain_ref[...], weight_ref[:, cols], preferred_element_type=F32)
        out = (tiles_ref[:, cols].astype(F32) + added).astype(BF16)
        layer_ref[:, cols] = out
        wide = out.astype(F32)
        square = square + jnp.sum(wide * wide, axis=1, keepdims=True)
    inverse = lax.rsqrt(square * (1.0 / width) + EPSILON)
    mask = mask_ref[...]
    for h in range(HEADS):
        cols = slice(h * HEAD, (h + 1) * HEAD)
        keys = (layer_ref[:, cols].astype(F32) * inverse).astype(BF16)
        keys_ref[:, cols] = keys
        scores = lax.dot_general(
            keys, finding_ref[:, cols], (((1,), (1,)), ((), ())), preferred_element_type=F32
        )
        scores = scores * FACTOR + mask
        peak = jnp.max(scores, axis=0, keepdims=True)
        stats_ref[h : h + 1, :] = peak
        stats_ref[HEADS + h : HEADS + h + 1, :] = jnp.sum(
            jnp.exp2(scores - peak), axis=0, keepdims=True
        )


def finish(mixed, last, tiles, weight, finding, mask):
    slots, width = tiles.shape
    return pl.pallas_call(
        finish_kernel,
        out_shape=(
            jax.ShapeDtypeStruct((slots, width), BF16),
            jax.ShapeDtypeStruct((slots, width), BF16),
            jax.ShapeDtypeStruct((2 * HEADS, finding.shape[0]), F32),
        ),
        scratch_shapes=[pltpu.VMEM((slots, width), BF16)],
        compiler_params=params(SMALL_LIMIT),
        name="finish",
    )(mixed, last, tiles, weight, finding, mask)


def heat_kernel(count, scale, stats_ref, keys_ref, finding_ref, mask_ref, heat_ref, held, kept, send_sem, recv_sem):
    slide = lax.axis_index("slide")
    me = lax.axis_index("seq")
    barrier = pltpu.get_barrier_semaphore()
    for hop in range(1, count):
        peer = lax.rem(me + hop, count)
        pl.semaphore_signal(
            barrier, inc=1, device_id=(slide, peer), device_id_type=pl.DeviceIdType.MESH
        )
    pl.semaphore_wait(barrier, count - 1)
    copies = []
    for hop in range(1, count):
        peer = lax.rem(me + hop, count)
        copy = pltpu.make_async_remote_copy(
            src_ref=stats_ref,
            dst_ref=held.at[hop],
            send_sem=send_sem.at[hop],
            recv_sem=recv_sem.at[hop],
            device_id=(slide, peer),
            device_id_type=pl.DeviceIdType.MESH,
        )
        copy.start()
        copies.append(copy)
    mask = mask_ref[...]
    for h in range(HEADS):
        cols = slice(h * HEAD, (h + 1) * HEAD)
        scores = lax.dot_general(
            keys_ref[:, cols], finding_ref[:, cols], (((1,), (1,)), ((), ())),
            preferred_element_type=F32,
        )
        kept[h] = jnp.exp2(scores * FACTOR + mask - stats_ref[h : h + 1, :])
    for copy in copies:
        copy.wait()
    everything = [stats_ref[...]] + [held[hop] for hop in range(1, count)]
    peaks = everything[0][:HEADS]
    for part in everything[1:]:
        peaks = jnp.maximum(peaks, part[:HEADS])
    totals = jnp.zeros_like(peaks)
    for part in everything:
        totals = totals + part[HEADS:] * jnp.exp2(part[:HEADS] - peaks)
    factors = jnp.exp2(everything[0][:HEADS] - peaks) * (scale / totals)
    slots = keys_ref.shape[0]
    chunk = 64
    for start in range(0, slots, chunk):
        rows = slice(start, start + chunk)
        total = kept[0, rows, :] * factors[0:1]
        for h in range(1, HEADS):
            total = total + kept[h, rows, :] * factors[h : h + 1]
        heat_ref[rows, :] = total


def heat_map(count, stats, keys, finding, mask):
    slots = keys.shape[0]
    finds = finding.shape[0]
    return pl.pallas_call(
        functools.partial(heat_kernel, count, count * slots / HEADS),
        in_specs=[pl.BlockSpec(memory_space=pltpu.VMEM)] * 4,
        out_specs=pl.BlockSpec(memory_space=pltpu.VMEM),
        out_shape=jax.ShapeDtypeStruct((slots, finds), F32),
        scratch_shapes=[
            pltpu.VMEM((count, 2 * HEADS, finds), F32),
            pltpu.VMEM((HEADS, slots, finds), F32),
            pltpu.SemaphoreType.DMA((count,)),
            pltpu.SemaphoreType.DMA((count,)),
        ],
        compiler_params=params(SMALL_LIMIT, collective_id=0, has_side_effects=True),
        name="heat_map",
    )(stats, keys, finding, mask)


def exchange(value, mask):
    pairs = [(source, source ^ mask) for source in range(lax.axis_size("seq"))]
    return lax.ppermute(value, "seq", pairs)


def shards(embeds, destination, norm_gain, qkv_weight, out_weight, finding_queries):
    devices = lax.axis_size(("slide", "seq"))
    seq_count = lax.axis_size("seq")
    slots = embeds.shape[0] * 2
    capacity = slots // devices
    padded = -(-capacity // 8) * 8
    width = embeds.shape[1]
    buffer, counts = dispatch(destination, embeds, devices, padded)
    received, counts = route(
        buffer.reshape(devices, padded, width), counts[None], devices, seq_count
    )
    tiles = received[:, :capacity].reshape(slots, width)
    pairs, near, far, normed, bias, mask = project(
        tiles, norm_gain, counts[:, 0], qkv_weight, capacity, seq_count
    )
    one = exchange(far, 2)
    pair = exchange(near, 1)
    query = project_query(normed, qkv_weight)
    mixed, summed, stats, quarter_query = near_attention(query, pairs, bias, pair)
    one, mixed = lax.optimization_barrier((one, mixed))
    two = exchange(one, 1)
    last = far_attention(quarter_query, bias, one, two, summed, stats)
    layer_out, keys, stats = finish(mixed, last, tiles, out_weight, finding_queries, mask)
    heat = heat_map(seq_count, stats, keys, finding_queries, mask)
    return (layer_out, heat)


LOG2_3 = math.log2(3.0)


def split(index, size):
    block = ((index.astype(F32) + 0.5) * (1.0 / size)).astype(jnp.int32)
    return block, index - block * size


def chunk_position(index, quarter):
    block, inner = split(index, quarter)
    phase = 2 * jnp.where((block == 1) | (block == 3), 1, 0) + (block >= 2).astype(jnp.int32)
    return 4 * inner + phase


def write_biases(capacity, slides, seq_count, counts, bias_ref, mask_ref):
    devices, lanes = counts.shape
    slots = mask_ref.shape[0]
    chunk = slots // slides
    half, quarter = chunk // 2, chunk // 4
    slide = lax.axis_index("slide")
    seq = lax.axis_index("seq")
    core = lax.rem(seq, 2)
    chip = lax.rem(seq // 2, 2)
    base = slide * seq_count + seq - core - 2 * chip
    members = [
        base + core + 2 * chip,
        base + (1 - core) + 2 * chip,
        base + core + 2 * (1 - chip),
        base + (1 - core) + 2 * (1 - chip),
    ]
    counts = counts.astype(F32)
    lane = lax.broadcasted_iota(jnp.int32, (devices, lanes), 1)
    columns = [
        jnp.sum(jnp.where(lane == member, counts, 0.0), axis=1, keepdims=True)
        for member in members
    ]
    sender = lax.broadcasted_iota(jnp.int32, (devices, slots), 0) * capacity
    index = lax.broadcasted_iota(jnp.int32, (1, slots), 1)

    def start_of(part):
        column = slide - part
        return chunk * jnp.where(column < 0, column + slides, column)

    def row(position, reached):
        place = (position - sender).astype(F32)
        inside = jnp.logical_and(place >= 0.0, place < reached)
        return (jnp.sum(inside.astype(F32), axis=0, keepdims=True) - 1.0) * (-MASKED)

    part, inner = split(index, chunk)
    block, _ = split(inner, quarter)
    own = row(start_of(part) + chunk_position(inner, quarter), columns[0])
    bias_ref[0:1, :] = own
    member, within = split(index, slots // 2)
    part, inner = split(within, half)
    sub, inner = split(inner, quarter)
    pair_rows = []
    for parity in range(2):
        in_half = jnp.where((block >= 2) == (parity == 1), 1.0, 0.0)
        bias_ref[1 + parity : 2 + parity, :] = own + in_half
        pair = row(start_of(part) + 4 * inner + parity + 2 * sub, columns[1])
        bias_ref[7 + parity : 8 + parity, :] = pair
        pair_rows.append(pair)
    member4, within4 = split(index, slots // 4)
    part4, inner4 = split(within4, quarter)
    reached = jnp.where(member4 >= 3, columns[3], columns[2])
    for phase in range(4):
        parity = phase % 2
        in_half = jnp.where((block >= 2) == (parity == 1), 1.0, 0.0)
        mine = jnp.where(block == QUARTER_OF[phase], LOG2_3, in_half)
        bias_ref[3 + phase : 4 + phase, :] = own + mine
        in_sub = jnp.where(sub == QUARTER_OF[phase] - 2 * parity, 1.0, 0.0)
        far = row(start_of(part4) + 4 * inner4 + phase, reached)
        bias_ref[9 + phase : 10 + phase, :] = jnp.where(
            member == 0, pair_rows[parity] + in_sub, far
        )
    bias_ref[13:16, :] = jnp.zeros((3, slots), F32)
    own = (lax.broadcasted_iota(jnp.int32, (8, lanes), 1) == members[0]).astype(F32)
    reached = lax.dot_general(
        own, counts, (((1,), (1,)), ((), ())), preferred_element_type=F32
    )[0:1, :]
    place = (
        lax.broadcasted_iota(jnp.int32, (slots, devices), 0)
        - lax.broadcasted_iota(jnp.int32, (slots, devices), 1) * capacity
    ).astype(F32)
    inside = jnp.logical_and(place >= 0.0, place < reached)
    mask_ref[...] = (jnp.sum(inside.astype(F32), axis=1, keepdims=True) - 1.0) * (-MASKED)


def pick(ref, parts, start, size, cols):
    step = ref.shape[0] // parts
    return jnp.concatenate(
        [ref[c * step + start : c * step + start + size, cols] for c in range(parts)], axis=0
    )


def put(ref, parts, start, cols, value):
    step, size = ref.shape[0] // parts, value.shape[0] // parts
    for c in range(parts):
        ref[c * step + start : c * step + start + size, cols] = value[c * size : (c + 1) * size]


def scores_of(query, parts, task):
    start, size, cols, pieces = task
    keys = jnp.concatenate([ref[:, cols] for ref, _, _ in pieces], axis=0)
    bias = jnp.concatenate([line for _, _, line in pieces], axis=1)
    scores = lax.dot_general(
        pick(query, parts, start, size, cols), keys, (((1,), (1,)), ((), ())),
        preferred_element_type=F32,
    )
    return scores * FACTOR + bias


def attend(query, mixed, parts, tasks):
    scores = scores_of(query, parts, tasks[0])
    for i, (start, _, cols, pieces) in enumerate(tasks):
        later = scores_of(query, parts, tasks[i + 1]) if i + 1 < len(tasks) else None
        values = jnp.concatenate([ref[:, at] for ref, at, _ in pieces], axis=0)
        weights = jnp.exp2(scores - jnp.max(scores, axis=1, keepdims=True))
        total = jnp.sum(weights, axis=1, keepdims=True)
        summed = jnp.dot(weights.astype(BF16), values, preferred_element_type=F32)
        put(mixed, parts, start, cols, ratio(summed, total))
        scores = later


def layer_kernel(
    capacity, slides, seq_count,
    row_ref, embeds_in, gain_ref, weight_ref, out_weight_ref, finding_in,
    layer_ref, heat_ref,
    sending, received, counts_ref, all_ref, embeds_ref, finding_ref, weight, query, keys, near, far, normed_ref,
    pair, one, two, mixed, bias_ref, mask_ref, stats_ref, held,
    send, recv, count_send, count_recv, own_sem, weight_sem, near_send, near_recv,
    far_send, far_recv, pass_send, pass_recv, stat_send, stat_recv, out_sem,
):
    rows, width = embeds_ref.shape
    devices = slides * seq_count
    chunk = seq_count * capacity
    slots = slides * chunk
    half, quarter = chunk // 2, chunk // 4
    lanes = counts_ref.shape[1]
    groups = width // WIDE
    slide = lax.axis_index("slide")
    seq = lax.axis_index("seq")
    me = slide * seq_count + seq
    core_peer = seq + 1 - 2 * lax.rem(seq, 2)
    chip_peer = seq + 2 - 4 * lax.rem(seq // 2, 2)
    barrier = pltpu.get_barrier_semaphore()

    def place_of(hop):
        return (lax.rem(slide + hop // seq_count, slides), lax.rem(seq + lax.rem(hop, seq_count), seq_count))

    def remote(src, dst, send_sem, recv_sem, where):
        return pltpu.make_async_remote_copy(
            src_ref=src,
            dst_ref=dst,
            send_sem=send_sem,
            recv_sem=recv_sem,
            device_id=where,
            device_id_type=pl.DeviceIdType.MESH,
        )

    def greet(hop, carry):
        pl.semaphore_signal(
            barrier, inc=1, device_id=place_of(hop), device_id_type=pl.DeviceIdType.MESH
        )
        return carry

    lax.fori_loop(1, devices, greet, 0)
    fetch = pltpu.make_async_copy(embeds_in, embeds_ref, weight_sem.at[2])
    fetch.start()
    load = pltpu.make_async_copy(weight_ref, weight, weight_sem.at[0])
    load.start()
    look = pltpu.make_async_copy(finding_in, finding_ref, weight_sem.at[3])
    look.start()

    row = row_ref[...]
    col = jnp.transpose(jnp.broadcast_to(row.astype(F32), (128, rows)))[:, 0:1].astype(jnp.int32)
    first = lax.broadcasted_iota(jnp.int32, (rows, rows), 0)
    second = lax.broadcasted_iota(jnp.int32, (rows, rows), 1)
    same = jnp.logical_and(col == row, first < second)
    rank = jnp.sum(same.astype(F32), axis=0, keepdims=True).astype(jnp.int32)
    place = row * capacity + rank
    lane = lax.broadcasted_iota(jnp.int32, (rows, lanes), 1)
    tally = jnp.sum((col == lane).astype(F32), axis=0, keepdims=True).astype(jnp.int32)
    counts_ref[...] = jnp.broadcast_to(tally, counts_ref.shape)

    def count_copy(hop):
        return remote(
            counts_ref, all_ref.at[me], count_send.at[hop], count_recv.at[hop], place_of(hop)
        )

    def row_copy(hop):
        where = place_of(hop)
        return remote(
            sending.at[where[0] * seq_count + where[1]],
            received.at[me],
            send.at[hop],
            recv.at[hop],
            where,
        )

    def each(make, method, low, high):
        def step(hop, carry):
            getattr(make(hop), method)()
            return carry

        lax.fori_loop(low, high, step, 0)

    def fill(k):
        column = lax.rem(slide + k, slides)
        wanted = lax.broadcasted_iota(jnp.int32, (chunk, rows), 0) + column * chunk
        chosen = (wanted == place).astype(F32).astype(BF16)
        for start in range(0, width, WIDE):
            part = jnp.dot(
                chosen, embeds_ref[:, start : start + WIDE], preferred_element_type=F32
            )
            sending[pl.ds(column * seq_count, seq_count), :, start : start + WIDE] = part.reshape(
                seq_count, capacity, WIDE
            ).astype(BF16)

    fetch.wait()
    fill(0)
    pl.semaphore_wait(barrier, devices - 1)
    each(row_copy, "start", 1, seq_count)
    own = pltpu.make_async_copy(sending.at[me], received.at[me], own_sem)
    own.start()
    all_ref[pl.ds(me, 1)] = counts_ref[...][None]

    def fill_next(k, carry):
        fill(k)
        each(row_copy, "start", k * seq_count, (k + 1) * seq_count)
        return carry

    each(count_copy, "start", 1, devices)
    lax.fori_loop(1, slides, fill_next, 0)

    def near_copy(k):
        part = pl.ds(pl.multiple_of(k * half, half), half)
        return remote(
            near.at[part], pair.at[part], near_send.at[k], near_recv.at[k], (slide, core_peer)
        )

    def far_copy(k):
        part = pl.ds(pl.multiple_of(k * quarter, quarter), quarter)
        return remote(
            far.at[part], one.at[part], far_send.at[k], far_recv.at[k], (slide, chip_peer)
        )

    def pass_copy(k):
        part = pl.ds(pl.multiple_of(k * quarter, quarter), quarter)
        return remote(
            one.at[part], two.at[part], pass_send.at[k], pass_recv.at[k], (slide, core_peer)
        )

    index = lax.broadcasted_iota(jnp.int32, (chunk, 1), 0)
    position = lax.broadcasted_iota(jnp.int32, (chunk, chunk), 1)
    order = (chunk_position(index, quarter) == position).astype(F32).astype(BF16)
    index = lax.broadcasted_iota(jnp.int32, (1, chunk), 1)
    position = lax.broadcasted_iota(jnp.int32, (chunk, chunk), 0)
    back = (chunk_position(index, quarter) == position).astype(F32).astype(BF16)

    def work(k):
        c = lax.rem(slide - k + slides, slides)
        part = pl.ds(pl.multiple_of(k * chunk, chunk), chunk)
        group = pl.ds(c * seq_count, seq_count)
        square = jnp.zeros((chunk, 1), F32)
        for start in range(0, width, WIDE):
            tile = received[group, :, start : start + WIDE].astype(F32).reshape(chunk, WIDE)
            square = square + jnp.sum(tile * tile, axis=1, keepdims=True)
        inverse = lax.rsqrt(square * (1.0 / width) + EPSILON)
        for start in range(0, width, WIDE):
            tile = received[group, :, start : start + WIDE].astype(F32).reshape(chunk, WIDE)
            gain = jnp.concatenate(
                [gain_ref[i : i + 1, :] for i in range(start // HEAD, (start + WIDE) // HEAD)], axis=1
            )
            normed = (tile * inverse * gain).astype(BF16)
            normed_ref[:, start : start + WIDE] = jnp.dot(
                order, normed, preferred_element_type=F32
            ).astype(BF16)

        def pairs(g, carry):
            at = pl.multiple_of(g * WIDE, WIDE)
            value = jnp.dot(
                normed_ref[...], weight[:, pl.ds(at + width, WIDE)], preferred_element_type=F32
            ).astype(BF16)
            keys[part, pl.ds(at, WIDE)] = value
            for j in range(GROUP):
                cols = pl.ds(at + j * HEAD, HEAD)
                begin = (j % 2) * half
                near[pl.ds(pl.multiple_of(k * half, half), half), cols] = value[
                    begin : begin + half, j * HEAD : (j + 1) * HEAD
                ]
                begin = QUARTER_OF[j] * quarter
                far[pl.ds(pl.multiple_of(k * quarter, quarter), quarter), cols] = value[
                    begin : begin + quarter, j * HEAD : (j + 1) * HEAD
                ]
            return carry

        def single(g, carry):
            at = pl.multiple_of(g * WIDE, WIDE)
            query[part, pl.ds(at, WIDE)] = jnp.dot(
                normed_ref[...], weight[:, pl.ds(at, WIDE)], preferred_element_type=F32
            ).astype(BF16)
            return carry

        lax.fori_loop(0, 2 * groups, pairs, 0, unroll=True)
        far_copy(k).start()
        near_copy(k).start()
        lax.fori_loop(0, groups, single, 0, unroll=True)

    own.wait()
    load.wait()
    look.wait()

    def step(k, carry):
        @pl.when(k == 1)
        def _():
            each(count_copy, "wait", 1, devices)
            write_biases(
                capacity, slides, seq_count, jnp.max(all_ref[...], axis=1), bias_ref, mask_ref
            )

        each(row_copy, "wait_recv", jnp.maximum(k * seq_count, 1), (k + 1) * seq_count)
        work(k)
        return carry

    lax.fori_loop(0, slides, step, 0)
    again = pltpu.make_async_copy(
        out_weight_ref, weight.at[:, pl.ds(0, width)], weight_sem.at[1]
    )
    again.start()

    def forward(k, carry):
        far_copy(k).wait_recv()
        pass_copy(k).start()
        return carry

    each(near_copy, "wait_recv", 0, slides)

    def head_cols(g, j):
        at = pl.multiple_of(g * WIDE + j * HEAD, HEAD)
        return pl.ds(at, HEAD), pl.ds(pl.multiple_of(at + width, HEAD), HEAD)

    def near_pass(g, carry):
        tasks = []
        for j in range(GROUP):
            cols, at = head_cols(g, j)
            start = (j % 2) * half
            done = start + quarter - (QUARTER_OF[j] * quarter - start)
            tasks.append((half - start, half, cols, [(keys, at, bias_ref[0:1, :])]))
            tasks.append((done, quarter, cols, [
                (keys, at, bias_ref[1 + j % 2 : 2 + j % 2, :]),
                (pair, at, bias_ref[7 + j % 2 : 8 + j % 2, : slots // 2]),
            ]))
        attend(query, mixed, slides, tasks)
        return carry

    def far_pass(g, carry):
        count = slots // 4
        tasks = []
        for j in range(GROUP):
            cols, at = head_cols(g, j)
            line = slice(9 + j, 10 + j)
            tasks.append((QUARTER_OF[j] * quarter, quarter, cols, [
                (keys, at, bias_ref[3 + j : 4 + j, :]),
                (pair, at, bias_ref[line, : 2 * count]),
                (one, at, bias_ref[line, 2 * count : 3 * count]),
                (two, at, bias_ref[line, 3 * count :]),
            ]))
        attend(query, mixed, slides, tasks)
        return carry

    lax.fori_loop(0, groups - 1, near_pass, 0)
    lax.fori_loop(0, slides, forward, 0)
    lax.fori_loop(groups - 1, groups, near_pass, 0)
    each(pass_copy, "wait_recv", 0, slides)
    lax.fori_loop(0, groups, far_pass, 0, unroll=True)

    def restore(k, carry):
        c = lax.rem(slide - k + slides, slides)
        place = pl.ds(pl.multiple_of(c * chunk, chunk), chunk)
        part = pl.ds(pl.multiple_of(k * chunk, chunk), chunk)
        for start in range(0, width, WIDE):
            query[place, start : start + WIDE] = jnp.dot(
                back, mixed[part, start : start + WIDE], preferred_element_type=F32
            ).astype(BF16)
        return carry

    lax.fori_loop(0, slides, restore, 0, unroll=True)
    again.wait()
    def output(g, square):
        cols = pl.ds(pl.multiple_of(g * WIDE, WIDE), WIDE)
        added = jnp.dot(query[...], weight[:, cols], preferred_element_type=F32)
        tile = received[:, :, cols].astype(F32).reshape(slots, WIDE)
        out = (tile + added).astype(BF16)
        keys[:, cols] = out
        wide = out.astype(F32)
        return square + jnp.sum(wide * wide, axis=1, keepdims=True)

    square = lax.fori_loop(0, groups, output, jnp.zeros((slots, 1), F32))
    store = pltpu.make_async_copy(keys.at[:, pl.ds(0, width)], layer_ref, out_sem)
    store.start()
    inverse = lax.rsqrt(square * (1.0 / width) + EPSILON)
    mask = mask_ref[...]

    def stat_copy(hop):
        half = hop // seq_count
        hop_in = lax.rem(hop, seq_count)
        return remote(
            stats_ref.at[half], held.at[hop], stat_send.at[hop], stat_recv.at[hop],
            (slide, lax.rem(seq + hop_in, seq_count)),
        )

    def find(kept):
        per = HEADS // 2
        local = []
        for part in range(2):
            for i in range(per):
                h = part * per + i
                cols = slice(h * HEAD, (h + 1) * HEAD)
                found = (keys[:, cols].astype(F32) * inverse).astype(BF16)
                scores = lax.dot_general(
                    found, finding_ref[:, cols], (((1,), (1,)), ((), ())), preferred_element_type=F32
                )
                scores = scores * FACTOR + mask
                peak = jnp.max(scores, axis=0, keepdims=True)
                raised = jnp.exp2(scores - peak)
                kept[h] = raised
                local.append(peak)
                stats_ref[part, i : i + 1, :] = peak + jnp.log2(
                    jnp.sum(raised, axis=0, keepdims=True)
                )
            stats_ref[part, per:, :] = jnp.zeros((8 - per, finding_ref.shape[0]), F32)
            each(stat_copy, "start", part * seq_count + 1, (part + 1) * seq_count)
        factors = []
        for part in range(2):
            each(stat_copy, "wait_recv", part * seq_count + 1, (part + 1) * seq_count)
            logs = [stats_ref[part]] + [held[part * seq_count + hop] for hop in range(1, seq_count)]
            top = functools.reduce(jnp.maximum, logs)
            total = functools.reduce(jnp.add, [jnp.exp2(log - top) for log in logs])
            shares = (seq_count * slots / HEADS) / total
            for i in range(per):
                factors.append(
                    shares[i : i + 1] * jnp.exp2(local[part * per + i] - top[i : i + 1])
                )
        small = 64
        for start in range(0, slots, small):
            part = slice(start, start + small)
            total = kept[0, part, :] * factors[0]
            for h in range(1, HEADS):
                total = total + kept[h, part, :] * factors[h]
            heat_ref[part, :] = total

    pl.run_scoped(find, pltpu.VMEM((HEADS, slots, finding_ref.shape[0]), F32))
    each(row_copy, "wait_send", 1, devices)
    each(near_copy, "wait_send", 0, slides)
    each(far_copy, "wait_send", 0, slides)
    each(pass_copy, "wait_send", 0, slides)
    each(stat_copy, "wait_send", 1, seq_count)
    each(stat_copy, "wait_send", seq_count + 1, 2 * seq_count)
    store.wait()


def layer(destination, embeds, gain, weight, out_weight, finding, capacity, slides, seq_count):
    rows, width = embeds.shape
    finds = finding.shape[0]
    devices = slides * seq_count
    slots = devices * capacity
    chunk = seq_count * capacity
    lanes = max(128, devices)
    vmem = pl.BlockSpec(memory_space=pltpu.VMEM)
    anywhere = pl.BlockSpec(memory_space=pl.ANY)
    dma = pltpu.SemaphoreType.DMA
    return pl.pallas_call(
        functools.partial(layer_kernel, capacity, slides, seq_count),
        in_specs=[vmem, anywhere, vmem, anywhere, anywhere, anywhere],
        out_specs=[anywhere, vmem],
        out_shape=(
            jax.ShapeDtypeStruct((slots, width), BF16),
            jax.ShapeDtypeStruct((slots, finds), F32),
        ),
        scratch_shapes=[
            pltpu.VMEM((devices, capacity, width), BF16),
            pltpu.VMEM((devices, capacity, width), BF16),
            pltpu.VMEM((8, lanes), jnp.int32),
            pltpu.VMEM((devices, 8, lanes), jnp.int32),
            pltpu.VMEM(embeds.shape, BF16),
            pltpu.VMEM(finding.shape, BF16),
            pltpu.VMEM(weight.shape, BF16),
            pltpu.VMEM((slots, width), BF16),
            pltpu.VMEM((slots, 2 * width), BF16),
            pltpu.VMEM((slots // 2, 2 * width), BF16),
            pltpu.VMEM((slots // 4, 2 * width), BF16),
            pltpu.VMEM((chunk, width), BF16),
            pltpu.VMEM((slots // 2, 2 * width), BF16),
            pltpu.VMEM((slots // 4, 2 * width), BF16),
            pltpu.VMEM((slots // 4, 2 * width), BF16),
            pltpu.VMEM((slots, width), BF16),
            pltpu.VMEM((16, slots), F32),
            pltpu.VMEM((slots, 1), F32),
            pltpu.VMEM((2, 8, finds), F32),
            pltpu.VMEM((2 * seq_count, 8, finds), F32),
            dma((devices,)),
            dma((devices,)),
            dma((devices,)),
            dma((devices,)),
            dma,
            dma((4,)),
            dma((slides,)),
            dma((slides,)),
            dma((slides,)),
            dma((slides,)),
            dma((slides,)),
            dma((slides,)),
            dma((2 * seq_count,)),
            dma((2 * seq_count,)),
            dma,
        ],
        compiler_params=params(LAYER_LIMIT, collective_id=2, has_side_effects=True),
        cost_estimate=pl.CostEstimate(
            flops=8 * slots * width * width + 8 * slots * slots * width,
            bytes_accessed=30_000_000,
            transcendentals=20_000_000,
        ),
        name="layer",
    )(destination.reshape(1, rows), embeds, gain.reshape(width // HEAD, HEAD), weight, out_weight, finding)


LAYER_LIMIT = 63 * 1024 * 1024


def layer_shards(embeds, destination, norm_gain, qkv_weight, out_weight, finding_queries):
    slides = lax.axis_size("slide")
    seq_count = lax.axis_size("seq")
    slots = embeds.shape[0] * 2
    capacity = slots // (slides * seq_count)
    return layer(
        destination, embeds, norm_gain, qkv_weight, out_weight, finding_queries,
        capacity, slides, seq_count,
    )


def solution(mesh):
    in_specs = (P(("slide", "seq"), None), P(("slide", "seq"), None), P(), P(), P(), P())
    out_specs = (P(("slide", "seq"), None), P(("slide", "seq"), None))

    def program(embeds, *rest):
        devices = mesh.shape["slide"] * mesh.shape["seq"]
        capacity = embeds.shape[0] * 2 // devices // devices
        chunk = capacity * mesh.shape["seq"]
        body = layer_shards if capacity % 8 == 0 and chunk % 64 == 0 else shards
        return jax.shard_map(
            body, mesh=mesh, in_specs=in_specs, out_specs=out_specs, check_vma=False
        )(embeds, *rest)

    return program
```

```python
import functools
import math

import jax
import jax.numpy as jnp
from jax import lax
from jax.experimental import pallas as pl
from jax.experimental.pallas import tpu as pltpu
from jax.sharding import PartitionSpec as P

HEADS = 12
HEAD = 128
GROUP = 4
WIDE = GROUP * HEAD
MASKED = -1e30
EPSILON = 1e-06
FACTOR = math.log2(math.e) / math.sqrt(HEAD)
F32 = jnp.float32
BF16 = jnp.bfloat16
QUARTER_OF = (0, 2, 1, 3)
VMEM_LIMIT = 56 * 1024 * 1024
SMALL_LIMIT = 34 * 1024 * 1024


def params(limit=VMEM_LIMIT, **more):
    return pltpu.CompilerParams(vmem_limit_bytes=limit, **more)


def dispatch_kernel(capacity, row_ref, embeds_ref, buffer_ref, counts_ref):
    rows = embeds_ref.shape[0]
    slots = buffer_ref.shape[0]
    row = row_ref[...]
    col = jnp.transpose(jnp.broadcast_to(row.astype(F32), (128, rows)))[:, 0:1].astype(jnp.int32)
    first = lax.broadcasted_iota(jnp.int32, (rows, rows), 0)
    second = lax.broadcasted_iota(jnp.int32, (rows, rows), 1)
    same = jnp.logical_and(col == row, first < second)
    rank = jnp.sum(same.astype(F32), axis=0, keepdims=True).astype(jnp.int32)
    place = row * capacity + rank
    lanes = lax.broadcasted_iota(jnp.int32, (rows, counts_ref.shape[1]), 1)
    counts_ref[...] = jnp.sum((col == lanes).astype(F32), axis=0, keepdims=True).astype(jnp.int32)
    chosen = (lax.broadcasted_iota(jnp.int32, (slots, rows), 0) == place).astype(F32).astype(BF16)
    for start in range(0, embeds_ref.shape[1], WIDE):
        part = embeds_ref[:, start : start + WIDE]
        buffer_ref[:, start : start + WIDE] = jnp.dot(
            chosen, part, preferred_element_type=F32
        ).astype(BF16)


def dispatch(destination, embeds, devices, capacity):
    rows, width = embeds.shape
    slots = devices * capacity
    return pl.pallas_call(
        functools.partial(dispatch_kernel, capacity),
        out_shape=(
            jax.ShapeDtypeStruct((slots, width), BF16),
            jax.ShapeDtypeStruct((1, max(128, devices)), jnp.int32),
        ),
        compiler_params=params(),
        name="dispatch",
    )(destination.reshape(1, rows), embeds)


def original_of(index, quarter):
    block = (
        (index >= quarter).astype(jnp.int32)
        + (index >= 2 * quarter).astype(jnp.int32)
        + (index >= 3 * quarter).astype(jnp.int32)
    )
    phase = 2 * jnp.where((block == 1) | (block == 3), 1, 0) + (block >= 2).astype(jnp.int32)
    return 4 * (index - quarter * block) + phase


def route_kernel(devices, seq_count, buffer_ref, counts_ref, tiles_ref, all_ref, send, recv, count_send, count_recv, own_sem):
    me = lax.axis_index("slide") * seq_count + lax.axis_index("seq")
    barrier = pltpu.get_barrier_semaphore()

    def place_of(hop):
        peer = lax.rem(me + hop, devices)
        return peer, (peer // seq_count, lax.rem(peer, seq_count))

    def greet(hop, carry):
        pl.semaphore_signal(
            barrier, inc=1, device_id=place_of(hop)[1], device_id_type=pl.DeviceIdType.MESH
        )
        return carry

    lax.fori_loop(1, devices, greet, 0)
    pl.semaphore_wait(barrier, devices - 1)

    def copies(hop):
        peer, where = place_of(hop)
        rows = pltpu.make_async_remote_copy(
            src_ref=buffer_ref.at[peer],
            dst_ref=tiles_ref.at[me],
            send_sem=send.at[hop],
            recv_sem=recv.at[hop],
            device_id=where,
            device_id_type=pl.DeviceIdType.MESH,
        )
        count = pltpu.make_async_remote_copy(
            src_ref=counts_ref.at[0],
            dst_ref=all_ref.at[me],
            send_sem=count_send.at[hop],
            recv_sem=count_recv.at[hop],
            device_id=where,
            device_id_type=pl.DeviceIdType.MESH,
        )
        return rows, count

    def begin(hop, carry):
        for copy in copies(hop):
            copy.start()
        return carry

    def end(hop, carry):
        for copy in copies(hop):
            copy.wait()
        return carry

    own_rows = pltpu.make_async_copy(buffer_ref.at[me], tiles_ref.at[me], own_sem.at[0])
    own_count = pltpu.make_async_copy(counts_ref.at[0], all_ref.at[me], own_sem.at[1])
    lax.fori_loop(1, devices, begin, 0)
    own_rows.start()
    own_count.start()
    own_rows.wait()
    own_count.wait()
    lax.fori_loop(1, devices, end, 0)


def route(buffer, counts, devices, seq_count):
    capacity, width = buffer.shape[1:]
    lanes = counts.shape[2]
    return pl.pallas_call(
        functools.partial(route_kernel, devices, seq_count),
        in_specs=[pl.BlockSpec(memory_space=pl.ANY)] * 2,
        out_specs=[pl.BlockSpec(memory_space=pl.ANY)] * 2,
        out_shape=(
            jax.ShapeDtypeStruct((devices, capacity, width), BF16),
            jax.ShapeDtypeStruct((devices, 1, lanes), jnp.int32),
        ),
        scratch_shapes=[pltpu.SemaphoreType.DMA((devices,))] * 4
        + [pltpu.SemaphoreType.DMA((2,))],
        compiler_params=pltpu.CompilerParams(collective_id=1, has_side_effects=True),
        name="route",
    )(buffer, counts)


def write_masks(capacity, seq_count, counts_ref, bias_ref, mask_ref):
    devices, lanes = counts_ref.shape
    slots = mask_ref.shape[0]
    half, quarter = slots // 2, slots // 4
    slide = lax.axis_index("slide")
    seq = lax.axis_index("seq")
    core = lax.rem(seq, 2)
    chip = lax.rem(seq // 2, 2)
    base = slide * seq_count + seq - core - 2 * chip
    members = [
        base + core + 2 * chip,
        base + (1 - core) + 2 * chip,
        base + core + 2 * (1 - chip),
        base + (1 - core) + 2 * (1 - chip),
    ]
    counts = counts_ref[...].astype(F32)
    lane = lax.broadcasted_iota(jnp.int32, (devices, lanes), 1)
    columns = [
        jnp.sum(jnp.where(lane == member, counts, 0.0), axis=1, keepdims=True)
        for member in members
    ]
    sender = lax.broadcasted_iota(jnp.int32, (devices, slots), 0) * capacity
    index = lax.broadcasted_iota(jnp.int32, (devices, slots), 1)

    def row(position, reached):
        place = (position - sender).astype(F32)
        inside = jnp.logical_and(place >= 0.0, place < reached)
        return (jnp.sum(inside.astype(F32), axis=0, keepdims=True) - 1.0) * (-MASKED)

    bias_ref[0:1, :] = row(original_of(index, quarter), columns[0])
    within = jnp.where(index >= half, index - half, index)
    for parity in range(2):
        reached = jnp.where(index >= half, columns[1], columns[0])
        bias_ref[1 + parity : 2 + parity, :] = row(
            original_of(within + parity * half, quarter), reached
        )
    for phase in range(4):
        block = (
            (index >= quarter).astype(jnp.int32)
            + (index >= 2 * quarter).astype(jnp.int32)
            + (index >= 3 * quarter).astype(jnp.int32)
        )
        reached = jnp.where(
            index >= half,
            jnp.where(index >= 3 * quarter, columns[3], columns[2]),
            jnp.where(index >= quarter, columns[1], columns[0]),
        )
        bias_ref[3 + phase : 4 + phase, :] = row(4 * (index - quarter * block) + phase, reached)
    bias_ref[7:8, :] = jnp.zeros((1, slots), F32)
    own = (lax.broadcasted_iota(jnp.int32, (8, lanes), 1) == members[0]).astype(F32)
    reached = lax.dot_general(
        own, counts, (((1,), (1,)), ((), ())), preferred_element_type=F32
    )[0:1, :]
    place = (
        lax.broadcasted_iota(jnp.int32, (slots, devices), 0)
        - lax.broadcasted_iota(jnp.int32, (slots, devices), 1) * capacity
    ).astype(F32)
    inside = jnp.logical_and(place >= 0.0, place < reached)
    mask_ref[...] = (jnp.sum(inside.astype(F32), axis=1, keepdims=True) - 1.0) * (-MASKED)


def project_kernel(capacity, seq_count, tiles_ref, gain_ref, counts_ref, weight_ref, out_ref, near_ref, far_ref, normed_ref, bias_ref, mask_ref):
    step = pl.program_id(0)
    slots, width = tiles_ref.shape
    quarter = slots // 4
    half = slots // 2

    @pl.when(step == 0)
    def _():
        tile = tiles_ref[...].astype(F32)
        mean = jnp.mean(tile * tile, axis=1, keepdims=True)
        normed = (tile * lax.rsqrt(mean + EPSILON) * gain_ref[...]).astype(BF16)
        index = lax.broadcasted_iota(jnp.int32, (slots, slots), 0)
        position = lax.broadcasted_iota(jnp.int32, (slots, slots), 1)
        order = (original_of(index, quarter) == position).astype(F32).astype(BF16)
        for start in range(0, width, WIDE):
            normed_ref[:, start : start + WIDE] = jnp.dot(
                order, normed[:, start : start + WIDE], preferred_element_type=F32
            ).astype(BF16)
        write_masks(capacity, seq_count, counts_ref, bias_ref, mask_ref)

    value = jnp.dot(normed_ref[...], weight_ref[...], preferred_element_type=F32).astype(BF16)
    out_ref[...] = value
    for j in range(GROUP):
        cols = slice(j * HEAD, (j + 1) * HEAD)
        near_ref[:, cols] = value[(j % 2) * half : (j % 2 + 1) * half, cols]
        begin = QUARTER_OF[j] * quarter
        far_ref[:, cols] = value[begin : begin + quarter, cols]


def project(tiles, gain, counts, weight, capacity, seq_count):
    slots, width = tiles.shape
    steps = width // WIDE
    whole = lambda i: (0, 0)
    return pl.pallas_call(
        functools.partial(project_kernel, capacity, seq_count),
        grid=(2 * steps,),
        in_specs=[
            pl.BlockSpec((slots, width), whole),
            pl.BlockSpec((1, width), whole),
            pl.BlockSpec(counts.shape, whole),
            pl.BlockSpec((width, WIDE), lambda i: (0, i + steps)),
        ],
        out_specs=[
            pl.BlockSpec((slots, WIDE), lambda i: (0, i)),
            pl.BlockSpec((slots // 2, WIDE), lambda i: (0, i)),
            pl.BlockSpec((slots // 4, WIDE), lambda i: (0, i)),
            pl.BlockSpec((slots, width), whole),
            pl.BlockSpec((8, slots), whole),
            pl.BlockSpec((slots, 1), whole),
        ],
        out_shape=(
            jax.ShapeDtypeStruct((slots, 2 * width), BF16),
            jax.ShapeDtypeStruct((slots // 2, 2 * width), BF16),
            jax.ShapeDtypeStruct((slots // 4, 2 * width), BF16),
            jax.ShapeDtypeStruct((slots, width), BF16),
            jax.ShapeDtypeStruct((8, slots), F32),
            jax.ShapeDtypeStruct((slots, 1), F32),
        ),
        compiler_params=params(),
        name="project",
    )(tiles, gain.reshape(1, width), counts, weight)


def query_kernel(normed_ref, weight_ref, out_ref):
    out_ref[...] = jnp.dot(
        normed_ref[...], weight_ref[...], preferred_element_type=F32
    ).astype(BF16)


def project_query(normed, weight):
    slots, width = normed.shape
    return pl.pallas_call(
        query_kernel,
        grid=(width // WIDE,),
        in_specs=[
            pl.BlockSpec((slots, width), lambda i: (0, 0)),
            pl.BlockSpec((width, WIDE), lambda i: (0, i)),
        ],
        out_specs=pl.BlockSpec((slots, WIDE), lambda i: (0, i)),
        out_shape=jax.ShapeDtypeStruct((slots, width), BF16),
        compiler_params=params(),
        cost_estimate=pl.CostEstimate(
            flops=2 * slots * width * width, bytes_accessed=10_000_000, transcendentals=0
        ),
        name="project_query",
    )(normed, weight)


def softmax_parts(query, keys, values, bias):
    scores = lax.dot_general(
        query, keys, (((1,), (1,)), ((), ())), preferred_element_type=F32
    )
    scores = scores * FACTOR + bias
    peak = jnp.max(scores, axis=1, keepdims=True)
    weights = jnp.exp2(scores - peak)
    total = jnp.sum(weights, axis=1, keepdims=True)
    summed = jnp.dot(weights.astype(BF16), values, preferred_element_type=F32)
    return summed, peak, total


def merge(parts):
    top = parts[0][1]
    for _, peak, _ in parts[1:]:
        top = jnp.maximum(top, peak)
    above, below = 0.0, 0.0
    for summed, peak, total in parts:
        factor = jnp.exp2(peak - top)
        above = above + factor * summed
        below = below + factor * total
    return above, top, below


def ratio(above, below):
    return (above * (1.0 / jnp.maximum(below, 1.0))).astype(BF16)


def near_attention_kernel(
    q_ref, k_ref, v_ref, bias_ref, pair_k, pair_v, mixed_ref, summed_ref, stats_ref, query_ref
):
    slots = q_ref.shape[0]
    half, quarter = slots // 2, slots // 4
    lanes = lax.broadcasted_iota(jnp.int32, (quarter, HEAD), 1)
    stats = jnp.zeros((quarter, HEAD), F32)
    for j in range(GROUP):
        cols = slice(j * HEAD, (j + 1) * HEAD)
        start = (j % 2) * half
        inside = QUARTER_OF[j] * quarter - start
        mine = slice(start, start + half)
        other = slice(half - start, 2 * half - start)
        summed, _, total = softmax_parts(
            q_ref[other, cols], k_ref[:, cols], v_ref[:, cols], bias_ref[0:1, :]
        )
        mixed_ref[other, cols] = ratio(summed, total)
        one = softmax_parts(q_ref[mine, cols], k_ref[:, cols], v_ref[:, cols], bias_ref[0:1, :])
        keys = jnp.concatenate([k_ref[mine, cols], pair_k[:, cols]], axis=0)
        values = jnp.concatenate([v_ref[mine, cols], pair_v[:, cols]], axis=0)
        two = softmax_parts(q_ref[mine, cols], keys, values, bias_ref[1 + j % 2 : 2 + j % 2, :])
        above, top, below = merge([one, two])
        done = quarter - inside
        mixed_ref[start + done : start + done + quarter, cols] = ratio(
            above[done : done + quarter], below[done : done + quarter]
        )
        begin = start + inside
        fourth = slice(begin, begin + quarter)
        within = slice(inside, inside + quarter)
        keys = jnp.concatenate([k_ref[fourth, cols], pair_k[within, cols]], axis=0)
        values = jnp.concatenate([v_ref[fourth, cols], pair_v[within, cols]], axis=0)
        four = softmax_parts(q_ref[fourth, cols], keys, values, bias_ref[3 + j : 4 + j, :half])
        above, top, below = merge([(above[within], top[within], below[within]), four])
        summed_ref[:, cols] = above
        stats = jnp.where(lanes == 2 * j, top, jnp.where(lanes == 2 * j + 1, below, stats))
        query_ref[:, cols] = q_ref[fourth, cols]
        mixed_ref[fourth, cols] = jnp.zeros((quarter, HEAD), BF16)
    stats_ref[...] = stats


def halves(array, steps):
    rows = array.shape[0]
    return [
        pl.BlockSpec((rows, WIDE), lambda i: (0, i)),
        pl.BlockSpec((rows, WIDE), lambda i: (0, i + steps)),
    ]


def near_attention(query, pairs, bias, pair):
    slots, width = query.shape
    quarter = slots // 4
    steps = width // WIDE
    return pl.pallas_call(
        near_attention_kernel,
        grid=(steps,),
        in_specs=[
            pl.BlockSpec((slots, WIDE), lambda i: (0, i)),
            *halves(pairs, steps),
            pl.BlockSpec(bias.shape, lambda i: (0, 0)),
            *halves(pair, steps),
        ],
        out_specs=[
            pl.BlockSpec((slots, WIDE), lambda i: (0, i)),
            pl.BlockSpec((quarter, WIDE), lambda i: (0, i)),
            pl.BlockSpec((quarter, HEAD), lambda i: (0, i)),
            pl.BlockSpec((quarter, WIDE), lambda i: (0, i)),
        ],
        out_shape=(
            jax.ShapeDtypeStruct((slots, width), BF16),
            jax.ShapeDtypeStruct((quarter, width), F32),
            jax.ShapeDtypeStruct((quarter, steps * HEAD), F32),
            jax.ShapeDtypeStruct((quarter, width), BF16),
        ),
        compiler_params=params(SMALL_LIMIT),
        cost_estimate=pl.CostEstimate(
            flops=12 * slots * slots * width,
            bytes_accessed=14_000_000,
            transcendentals=6 * slots * slots * HEADS,
        ),
        name="near_attention",
    )(query, pairs, pairs, bias, pair, pair)


def far_attention_kernel(
    q_ref, bias_ref, one_k, one_v, two_k, two_v, summed_ref, stats_ref, mixed_ref
):
    half = bias_ref.shape[1] // 2
    for j in range(GROUP):
        cols = slice(j * HEAD, (j + 1) * HEAD)
        keys = jnp.concatenate([one_k[:, cols], two_k[:, cols]], axis=0)
        values = jnp.concatenate([one_v[:, cols], two_v[:, cols]], axis=0)
        four = softmax_parts(q_ref[:, cols], keys, values, bias_ref[3 + j : 4 + j, half:])
        before = (
            summed_ref[:, cols],
            stats_ref[:, 2 * j : 2 * j + 1],
            stats_ref[:, 2 * j + 1 : 2 * j + 2],
        )
        above, _, below = merge([before, four])
        mixed_ref[:, cols] = ratio(above, below)


def far_attention(query, bias, one, two, summed, stats):
    quarter, width = query.shape
    steps = width // WIDE
    block = pl.BlockSpec((quarter, WIDE), lambda i: (0, i))
    return pl.pallas_call(
        far_attention_kernel,
        grid=(steps,),
        in_specs=[
            block,
            pl.BlockSpec(bias.shape, lambda i: (0, 0)),
            *halves(one, steps),
            *halves(two, steps),
            block,
            pl.BlockSpec((quarter, HEAD), lambda i: (0, i)),
        ],
        out_specs=block,
        out_shape=jax.ShapeDtypeStruct((quarter, width), BF16),
        compiler_params=params(SMALL_LIMIT),
        name="far_attention",
    )(query, bias, one, one, two, two, summed, stats)


def finish_kernel(mixed_ref, last_ref, tiles_ref, weight_ref, finding_ref, mask_ref, layer_ref, keys_ref, stats_ref, plain_ref):
    slots, width = tiles_ref.shape
    quarter = slots // 4
    position = lax.broadcasted_iota(jnp.int32, (slots, slots), 0)
    index = lax.broadcasted_iota(jnp.int32, (slots, slots), 1)
    order = (original_of(index, quarter) == position).astype(F32).astype(BF16)
    for start in range(0, width, WIDE):
        heads = []
        for j in range(GROUP):
            cols = slice(start + j * HEAD, start + (j + 1) * HEAD)
            begin = QUARTER_OF[j] * quarter
            pieces = [last_ref[:, cols]]
            if begin > 0:
                pieces.insert(0, mixed_ref[:begin, cols])
            if begin + quarter < slots:
                pieces.append(mixed_ref[begin + quarter :, cols])
            heads.append(jnp.concatenate(pieces, axis=0))
        plain_ref[:, start : start + WIDE] = jnp.dot(
            order, jnp.concatenate(heads, axis=1), preferred_element_type=F32
        ).astype(BF16)
    square = jnp.zeros((slots, 1), F32)
    for start in range(0, width, WIDE):
        cols = slice(start, start + WIDE)
        added = jnp.dot(plain_ref[...], weight_ref[:, cols], preferred_element_type=F32)
        out = (tiles_ref[:, cols].astype(F32) + added).astype(BF16)
        layer_ref[:, cols] = out
        wide = out.astype(F32)
        square = square + jnp.sum(wide * wide, axis=1, keepdims=True)
    inverse = lax.rsqrt(square * (1.0 / width) + EPSILON)
    mask = mask_ref[...]
    for h in range(HEADS):
        cols = slice(h * HEAD, (h + 1) * HEAD)
        keys = (layer_ref[:, cols].astype(F32) * inverse).astype(BF16)
        keys_ref[:, cols] = keys
        scores = lax.dot_general(
            keys, finding_ref[:, cols], (((1,), (1,)), ((), ())), preferred_element_type=F32
        )
        scores = scores * FACTOR + mask
        peak = jnp.max(scores, axis=0, keepdims=True)
        stats_ref[h : h + 1, :] = peak
        stats_ref[HEADS + h : HEADS + h + 1, :] = jnp.sum(
            jnp.exp2(scores - peak), axis=0, keepdims=True
        )


def finish(mixed, last, tiles, weight, finding, mask):
    slots, width = tiles.shape
    return pl.pallas_call(
        finish_kernel,
        out_shape=(
            jax.ShapeDtypeStruct((slots, width), BF16),
            jax.ShapeDtypeStruct((slots, width), BF16),
            jax.ShapeDtypeStruct((2 * HEADS, finding.shape[0]), F32),
        ),
        scratch_shapes=[pltpu.VMEM((slots, width), BF16)],
        compiler_params=params(SMALL_LIMIT),
        name="finish",
    )(mixed, last, tiles, weight, finding, mask)


def heat_kernel(count, scale, stats_ref, keys_ref, finding_ref, mask_ref, heat_ref, held, kept, send_sem, recv_sem):
    slide = lax.axis_index("slide")
    me = lax.axis_index("seq")
    barrier = pltpu.get_barrier_semaphore()
    for hop in range(1, count):
        peer = lax.rem(me + hop, count)
        pl.semaphore_signal(
            barrier, inc=1, device_id=(slide, peer), device_id_type=pl.DeviceIdType.MESH
        )
    pl.semaphore_wait(barrier, count - 1)
    copies = []
    for hop in range(1, count):
        peer = lax.rem(me + hop, count)
        copy = pltpu.make_async_remote_copy(
            src_ref=stats_ref,
            dst_ref=held.at[hop],
            send_sem=send_sem.at[hop],
            recv_sem=recv_sem.at[hop],
            device_id=(slide, peer),
            device_id_type=pl.DeviceIdType.MESH,
        )
        copy.start()
        copies.append(copy)
    mask = mask_ref[...]
    for h in range(HEADS):
        cols = slice(h * HEAD, (h + 1) * HEAD)
        scores = lax.dot_general(
            keys_ref[:, cols], finding_ref[:, cols], (((1,), (1,)), ((), ())),
            preferred_element_type=F32,
        )
        kept[h] = jnp.exp2(scores * FACTOR + mask - stats_ref[h : h + 1, :])
    for copy in copies:
        copy.wait()
    everything = [stats_ref[...]] + [held[hop] for hop in range(1, count)]
    peaks = everything[0][:HEADS]
    for part in everything[1:]:
        peaks = jnp.maximum(peaks, part[:HEADS])
    totals = jnp.zeros_like(peaks)
    for part in everything:
        totals = totals + part[HEADS:] * jnp.exp2(part[:HEADS] - peaks)
    factors = jnp.exp2(everything[0][:HEADS] - peaks) * (scale / totals)
    slots = keys_ref.shape[0]
    chunk = 64
    for start in range(0, slots, chunk):
        rows = slice(start, start + chunk)
        total = kept[0, rows, :] * factors[0:1]
        for h in range(1, HEADS):
            total = total + kept[h, rows, :] * factors[h : h + 1]
        heat_ref[rows, :] = total


def heat_map(count, stats, keys, finding, mask):
    slots = keys.shape[0]
    finds = finding.shape[0]
    return pl.pallas_call(
        functools.partial(heat_kernel, count, count * slots / HEADS),
        in_specs=[pl.BlockSpec(memory_space=pltpu.VMEM)] * 4,
        out_specs=pl.BlockSpec(memory_space=pltpu.VMEM),
        out_shape=jax.ShapeDtypeStruct((slots, finds), F32),
        scratch_shapes=[
            pltpu.VMEM((count, 2 * HEADS, finds), F32),
            pltpu.VMEM((HEADS, slots, finds), F32),
            pltpu.SemaphoreType.DMA((count,)),
            pltpu.SemaphoreType.DMA((count,)),
        ],
        compiler_params=params(SMALL_LIMIT, collective_id=0, has_side_effects=True),
        name="heat_map",
    )(stats, keys, finding, mask)


def exchange(value, mask):
    pairs = [(source, source ^ mask) for source in range(lax.axis_size("seq"))]
    return lax.ppermute(value, "seq", pairs)


def shards(embeds, destination, norm_gain, qkv_weight, out_weight, finding_queries):
    devices = lax.axis_size(("slide", "seq"))
    seq_count = lax.axis_size("seq")
    slots = embeds.shape[0] * 2
    capacity = slots // devices
    padded = -(-capacity // 8) * 8
    width = embeds.shape[1]
    buffer, counts = dispatch(destination, embeds, devices, padded)
    received, counts = route(
        buffer.reshape(devices, padded, width), counts[None], devices, seq_count
    )
    tiles = received[:, :capacity].reshape(slots, width)
    pairs, near, far, normed, bias, mask = project(
        tiles, norm_gain, counts[:, 0], qkv_weight, capacity, seq_count
    )
    one = exchange(far, 2)
    pair = exchange(near, 1)
    query = project_query(normed, qkv_weight)
    mixed, summed, stats, quarter_query = near_attention(query, pairs, bias, pair)
    one, mixed = lax.optimization_barrier((one, mixed))
    two = exchange(one, 1)
    last = far_attention(quarter_query, bias, one, two, summed, stats)
    layer_out, keys, stats = finish(mixed, last, tiles, out_weight, finding_queries, mask)
    heat = heat_map(seq_count, stats, keys, finding_queries, mask)
    return (layer_out, heat)


LOG2_3 = math.log2(3.0)


def split(index, size):
    block = ((index.astype(F32) + 0.5) * (1.0 / size)).astype(jnp.int32)
    return block, index - block * size


def chunk_position(index, quarter):
    block, inner = split(index, quarter)
    phase = 2 * jnp.where((block == 1) | (block == 3), 1, 0) + (block >= 2).astype(jnp.int32)
    return 4 * inner + phase


def write_biases(capacity, slides, seq_count, counts, bias_ref, mask_ref):
    devices, lanes = counts.shape
    slots = mask_ref.shape[0]
    chunk = slots // slides
    half, quarter = chunk // 2, chunk // 4
    slide = lax.axis_index("slide")
    seq = lax.axis_index("seq")
    core = lax.rem(seq, 2)
    chip = lax.rem(seq // 2, 2)
    base = slide * seq_count + seq - core - 2 * chip
    members = [
        base + core + 2 * chip,
        base + (1 - core) + 2 * chip,
        base + core + 2 * (1 - chip),
        base + (1 - core) + 2 * (1 - chip),
    ]
    counts = counts.astype(F32)
    lane = lax.broadcasted_iota(jnp.int32, (devices, lanes), 1)
    columns = [
        jnp.sum(jnp.where(lane == member, counts, 0.0), axis=1, keepdims=True)
        for member in members
    ]
    sender = lax.broadcasted_iota(jnp.int32, (devices, slots), 0) * capacity
    index = lax.broadcasted_iota(jnp.int32, (1, slots), 1)

    def start_of(part):
        column = slide - part
        return chunk * jnp.where(column < 0, column + slides, column)

    def row(position, reached):
        place = (position - sender).astype(F32)
        inside = jnp.logical_and(place >= 0.0, place < reached)
        return (jnp.sum(inside.astype(F32), axis=0, keepdims=True) - 1.0) * (-MASKED)

    part, inner = split(index, chunk)
    block, _ = split(inner, quarter)
    own = row(start_of(part) + chunk_position(inner, quarter), columns[0])
    bias_ref[0:1, :] = own
    member, within = split(index, slots // 2)
    part, inner = split(within, half)
    sub, inner = split(inner, quarter)
    pair_rows = []
    for parity in range(2):
        in_half = jnp.where((block >= 2) == (parity == 1), 1.0, 0.0)
        bias_ref[1 + parity : 2 + parity, :] = own + in_half
        pair = row(start_of(part) + 4 * inner + parity + 2 * sub, columns[1])
        bias_ref[7 + parity : 8 + parity, :] = pair
        pair_rows.append(pair)
    member4, within4 = split(index, slots // 4)
    part4, inner4 = split(within4, quarter)
    reached = jnp.where(member4 >= 3, columns[3], columns[2])
    for phase in range(4):
        parity = phase % 2
        in_half = jnp.where((block >= 2) == (parity == 1), 1.0, 0.0)
        mine = jnp.where(block == QUARTER_OF[phase], LOG2_3, in_half)
        bias_ref[3 + phase : 4 + phase, :] = own + mine
        in_sub = jnp.where(sub == QUARTER_OF[phase] - 2 * parity, 1.0, 0.0)
        far = row(start_of(part4) + 4 * inner4 + phase, reached)
        bias_ref[9 + phase : 10 + phase, :] = jnp.where(
            member == 0, pair_rows[parity] + in_sub, far
        )
    bias_ref[13:16, :] = jnp.zeros((3, slots), F32)
    own = (lax.broadcasted_iota(jnp.int32, (8, lanes), 1) == members[0]).astype(F32)
    reached = lax.dot_general(
        own, counts, (((1,), (1,)), ((), ())), preferred_element_type=F32
    )[0:1, :]
    place = (
        lax.broadcasted_iota(jnp.int32, (slots, devices), 0)
        - lax.broadcasted_iota(jnp.int32, (slots, devices), 1) * capacity
    ).astype(F32)
    inside = jnp.logical_and(place >= 0.0, place < reached)
    mask_ref[...] = (jnp.sum(inside.astype(F32), axis=1, keepdims=True) - 1.0) * (-MASKED)


def pick(ref, parts, start, size, cols):
    step = ref.shape[0] // parts
    return jnp.concatenate(
        [ref[c * step + start : c * step + start + size, cols] for c in range(parts)], axis=0
    )


def put(ref, parts, start, cols, value):
    step, size = ref.shape[0] // parts, value.shape[0] // parts
    for c in range(parts):
        ref[c * step + start : c * step + start + size, cols] = value[c * size : (c + 1) * size]


def scores_of(query, parts, task):
    start, size, cols, pieces = task
    keys = jnp.concatenate([ref[:, cols] for ref, _, _ in pieces], axis=0)
    bias = jnp.concatenate([line for _, _, line in pieces], axis=1)
    scores = lax.dot_general(
        pick(query, parts, start, size, cols), keys, (((1,), (1,)), ((), ())),
        preferred_element_type=F32,
    )
    return scores * FACTOR + bias


def attend(query, mixed, parts, tasks):
    scores = scores_of(query, parts, tasks[0])
    for i, (start, _, cols, pieces) in enumerate(tasks):
        later = scores_of(query, parts, tasks[i + 1]) if i + 1 < len(tasks) else None
        values = jnp.concatenate([ref[:, at] for ref, at, _ in pieces], axis=0)
        weights = jnp.exp2(scores - jnp.max(scores, axis=1, keepdims=True))
        total = jnp.sum(weights, axis=1, keepdims=True)
        summed = jnp.dot(weights.astype(BF16), values, preferred_element_type=F32)
        put(mixed, parts, start, cols, ratio(summed, total))
        scores = later


def layer_kernel(
    capacity, slides, seq_count,
    row_ref, embeds_in, gain_ref, weight_ref, out_weight_ref, finding_in,
    layer_ref, heat_ref,
    sending, received, counts_ref, all_ref, embeds_ref, finding_ref, weight, query, keys, near, far, normed_ref,
    pair, one, two, mixed, bias_ref, mask_ref, stats_ref, held,
    send, recv, count_send, count_recv, own_sem, weight_sem, near_send, near_recv,
    far_send, far_recv, pass_send, pass_recv, stat_send, stat_recv, out_sem,
):
    rows, width = embeds_ref.shape
    devices = slides * seq_count
    chunk = seq_count * capacity
    slots = slides * chunk
    half, quarter = chunk // 2, chunk // 4
    lanes = counts_ref.shape[1]
    groups = width // WIDE
    slide = lax.axis_index("slide")
    seq = lax.axis_index("seq")
    me = slide * seq_count + seq
    core_peer = seq + 1 - 2 * lax.rem(seq, 2)
    chip_peer = seq + 2 - 4 * lax.rem(seq // 2, 2)
    barrier = pltpu.get_barrier_semaphore()

    def place_of(hop):
        return (lax.rem(slide + hop // seq_count, slides), lax.rem(seq + lax.rem(hop, seq_count), seq_count))

    def remote(src, dst, send_sem, recv_sem, where):
        return pltpu.make_async_remote_copy(
            src_ref=src,
            dst_ref=dst,
            send_sem=send_sem,
            recv_sem=recv_sem,
            device_id=where,
            device_id_type=pl.DeviceIdType.MESH,
        )

    def greet(hop, carry):
        pl.semaphore_signal(
            barrier, inc=1, device_id=place_of(hop), device_id_type=pl.DeviceIdType.MESH
        )
        return carry

    lax.fori_loop(1, devices, greet, 0)
    fetch = pltpu.make_async_copy(embeds_in, embeds_ref, weight_sem.at[2])
    fetch.start()
    load = pltpu.make_async_copy(weight_ref, weight, weight_sem.at[0])
    load.start()
    look = pltpu.make_async_copy(finding_in, finding_ref, weight_sem.at[3])
    look.start()

    row = row_ref[...]
    col = jnp.transpose(jnp.broadcast_to(row.astype(F32), (128, rows)))[:, 0:1].astype(jnp.int32)
    first = lax.broadcasted_iota(jnp.int32, (rows, rows), 0)
    second = lax.broadcasted_iota(jnp.int32, (rows, rows), 1)
    same = jnp.logical_and(col == row, first < second)
    rank = jnp.sum(same.astype(F32), axis=0, keepdims=True).astype(jnp.int32)
    place = row * capacity + rank
    lane = lax.broadcasted_iota(jnp.int32, (rows, lanes), 1)
    tally = jnp.sum((col == lane).astype(F32), axis=0, keepdims=True).astype(jnp.int32)
    counts_ref[...] = jnp.broadcast_to(tally, counts_ref.shape)

    def count_copy(hop):
        return remote(
            counts_ref, all_ref.at[me], count_send.at[hop], count_recv.at[hop], place_of(hop)
        )

    def row_copy(hop):
        where = place_of(hop)
        return remote(
            sending.at[where[0] * seq_count + where[1]],
            received.at[me],
            send.at[hop],
            recv.at[hop],
            where,
        )

    def each(make, method, low, high):
        def step(hop, carry):
            getattr(make(hop), method)()
            return carry

        lax.fori_loop(low, high, step, 0)

    def fill(k):
        column = lax.rem(slide + k, slides)
        wanted = lax.broadcasted_iota(jnp.int32, (chunk, rows), 0) + column * chunk
        chosen = (wanted == place).astype(F32).astype(BF16)
        for start in range(0, width, WIDE):
            part = jnp.dot(
                chosen, embeds_ref[:, start : start + WIDE], preferred_element_type=F32
            )
            sending[pl.ds(column * seq_count, seq_count), :, start : start + WIDE] = part.reshape(
                seq_count, capacity, WIDE
            ).astype(BF16)

    fetch.wait()
    fill(0)
    pl.semaphore_wait(barrier, devices - 1)
    each(row_copy, "start", 1, seq_count)
    own = pltpu.make_async_copy(sending.at[me], received.at[me], own_sem)
    own.start()
    all_ref[pl.ds(me, 1)] = counts_ref[...][None]

    def fill_next(k, carry):
        fill(k)
        each(row_copy, "start", k * seq_count, (k + 1) * seq_count)
        return carry

    each(count_copy, "start", 1, devices)
    lax.fori_loop(1, slides, fill_next, 0)

    def near_copy(k):
        part = pl.ds(pl.multiple_of(k * half, half), half)
        return remote(
            near.at[part], pair.at[part], near_send.at[k], near_recv.at[k], (slide, core_peer)
        )

    def far_copy(k):
        part = pl.ds(pl.multiple_of(k * quarter, quarter), quarter)
        return remote(
            far.at[part], one.at[part], far_send.at[k], far_recv.at[k], (slide, chip_peer)
        )

    def pass_copy(k):
        part = pl.ds(pl.multiple_of(k * quarter, quarter), quarter)
        return remote(
            one.at[part], two.at[part], pass_send.at[k], pass_recv.at[k], (slide, core_peer)
        )

    index = lax.broadcasted_iota(jnp.int32, (chunk, 1), 0)
    position = lax.broadcasted_iota(jnp.int32, (chunk, chunk), 1)
    order = (chunk_position(index, quarter) == position).astype(F32).astype(BF16)
    index = lax.broadcasted_iota(jnp.int32, (1, chunk), 1)
    position = lax.broadcasted_iota(jnp.int32, (chunk, chunk), 0)
    back = (chunk_position(index, quarter) == position).astype(F32).astype(BF16)

    def work(k):
        c = lax.rem(slide - k + slides, slides)
        part = pl.ds(pl.multiple_of(k * chunk, chunk), chunk)
        group = pl.ds(c * seq_count, seq_count)
        square = jnp.zeros((chunk, 1), F32)
        for start in range(0, width, WIDE):
            tile = received[group, :, start : start + WIDE].astype(F32).reshape(chunk, WIDE)
            square = square + jnp.sum(tile * tile, axis=1, keepdims=True)
        inverse = lax.rsqrt(square * (1.0 / width) + EPSILON)
        for start in range(0, width, WIDE):
            tile = received[group, :, start : start + WIDE].astype(F32).reshape(chunk, WIDE)
            gain = jnp.concatenate(
                [gain_ref[i : i + 1, :] for i in range(start // HEAD, (start + WIDE) // HEAD)], axis=1
            )
            normed = (tile * inverse * gain).astype(BF16)
            normed_ref[:, start : start + WIDE] = jnp.dot(
                order, normed, preferred_element_type=F32
            ).astype(BF16)

        def pairs(g, carry):
            at = pl.multiple_of(g * WIDE, WIDE)
            value = jnp.dot(
                normed_ref[...], weight[:, pl.ds(at + width, WIDE)], preferred_element_type=F32
            ).astype(BF16)
            keys[part, pl.ds(at, WIDE)] = value
            for j in range(GROUP):
                cols = pl.ds(at + j * HEAD, HEAD)
                begin = (j % 2) * half
                near[pl.ds(pl.multiple_of(k * half, half), half), cols] = value[
                    begin : begin + half, j * HEAD : (j + 1) * HEAD
                ]
                begin = QUARTER_OF[j] * quarter
                far[pl.ds(pl.multiple_of(k * quarter, quarter), quarter), cols] = value[
                    begin : begin + quarter, j * HEAD : (j + 1) * HEAD
                ]
            return carry

        def single(g, carry):
            at = pl.multiple_of(g * WIDE, WIDE)
            query[part, pl.ds(at, WIDE)] = jnp.dot(
                normed_ref[...], weight[:, pl.ds(at, WIDE)], preferred_element_type=F32
            ).astype(BF16)
            return carry

        lax.fori_loop(0, 2 * groups, pairs, 0, unroll=True)
        far_copy(k).start()
        near_copy(k).start()
        lax.fori_loop(0, groups, single, 0, unroll=True)

    own.wait()
    load.wait()
    look.wait()

    def step(k, carry):
        @pl.when(k == 1)
        def _():
            each(count_copy, "wait", 1, devices)
            write_biases(
                capacity, slides, seq_count, jnp.max(all_ref[...], axis=1), bias_ref, mask_ref
            )

        each(row_copy, "wait_recv", jnp.maximum(k * seq_count, 1), (k + 1) * seq_count)
        work(k)
        return carry

    lax.fori_loop(0, slides, step, 0)
    again = pltpu.make_async_copy(
        out_weight_ref, weight.at[:, pl.ds(0, width)], weight_sem.at[1]
    )
    again.start()

    def forward(k, carry):
        far_copy(k).wait_recv()
        pass_copy(k).start()
        return carry

    each(near_copy, "wait_recv", 0, slides)

    def head_cols(g, j):
        at = pl.multiple_of(g * WIDE + j * HEAD, HEAD)
        return pl.ds(at, HEAD), pl.ds(pl.multiple_of(at + width, HEAD), HEAD)

    def near_pass(g, carry):
        tasks = []
        for j in range(GROUP):
            cols, at = head_cols(g, j)
            start = (j % 2) * half
            done = start + quarter - (QUARTER_OF[j] * quarter - start)
            tasks.append((half - start, half, cols, [(keys, at, bias_ref[0:1, :])]))
            tasks.append((done, quarter, cols, [
                (keys, at, bias_ref[1 + j % 2 : 2 + j % 2, :]),
                (pair, at, bias_ref[7 + j % 2 : 8 + j % 2, : slots // 2]),
            ]))
        attend(query, mixed, slides, tasks)
        return carry

    def far_pass(g, carry):
        count = slots // 4
        tasks = []
        for j in range(GROUP):
            cols, at = head_cols(g, j)
            line = slice(9 + j, 10 + j)
            tasks.append((QUARTER_OF[j] * quarter, quarter, cols, [
                (keys, at, bias_ref[3 + j : 4 + j, :]),
                (pair, at, bias_ref[line, : 2 * count]),
                (one, at, bias_ref[line, 2 * count : 3 * count]),
                (two, at, bias_ref[line, 3 * count :]),
            ]))
        attend(query, mixed, slides, tasks)
        return carry

    lax.fori_loop(0, groups - 1, near_pass, 0, unroll=True)
    lax.fori_loop(0, slides, forward, 0)
    lax.fori_loop(groups - 1, groups, near_pass, 0)
    each(pass_copy, "wait_recv", 0, slides)
    lax.fori_loop(0, groups, far_pass, 0, unroll=True)

    def restore(k, carry):
        c = lax.rem(slide - k + slides, slides)
        place = pl.ds(pl.multiple_of(c * chunk, chunk), chunk)
        part = pl.ds(pl.multiple_of(k * chunk, chunk), chunk)
        for start in range(0, width, WIDE):
            query[place, start : start + WIDE] = jnp.dot(
                back, mixed[part, start : start + WIDE], preferred_element_type=F32
            ).astype(BF16)
        return carry

    lax.fori_loop(0, slides, restore, 0, unroll=True)
    again.wait()
    def output(g, square):
        cols = pl.ds(pl.multiple_of(g * WIDE, WIDE), WIDE)
        added = jnp.dot(query[...], weight[:, cols], preferred_element_type=F32)
        tile = received[:, :, cols].astype(F32).reshape(slots, WIDE)
        out = (tile + added).astype(BF16)
        keys[:, cols] = out
        wide = out.astype(F32)
        return square + jnp.sum(wide * wide, axis=1, keepdims=True)

    square = lax.fori_loop(0, groups, output, jnp.zeros((slots, 1), F32), unroll=True)
    store = pltpu.make_async_copy(keys.at[:, pl.ds(0, width)], layer_ref, out_sem)
    store.start()
    inverse = lax.rsqrt(square * (1.0 / width) + EPSILON)
    mask = mask_ref[...]

    def stat_copy(hop):
        half = hop // seq_count
        hop_in = lax.rem(hop, seq_count)
        return remote(
            stats_ref.at[half], held.at[hop], stat_send.at[hop], stat_recv.at[hop],
            (slide, lax.rem(seq + hop_in, seq_count)),
        )

    def find(kept):
        per = HEADS // 2
        local = []
        for part in range(2):
            for i in range(per):
                h = part * per + i
                cols = slice(h * HEAD, (h + 1) * HEAD)
                found = (keys[:, cols].astype(F32) * inverse).astype(BF16)
                scores = lax.dot_general(
                    found, finding_ref[:, cols], (((1,), (1,)), ((), ())), preferred_element_type=F32
                )
                scores = scores * FACTOR + mask
                peak = jnp.max(scores, axis=0, keepdims=True)
                raised = jnp.exp2(scores - peak)
                kept[h] = raised
                local.append(peak)
                stats_ref[part, i : i + 1, :] = peak + jnp.log2(
                    jnp.sum(raised, axis=0, keepdims=True)
                )
            stats_ref[part, per:, :] = jnp.zeros((8 - per, finding_ref.shape[0]), F32)
            each(stat_copy, "start", part * seq_count + 1, (part + 1) * seq_count)
        factors = []
        for part in range(2):
            each(stat_copy, "wait_recv", part * seq_count + 1, (part + 1) * seq_count)
            logs = [stats_ref[part]] + [held[part * seq_count + hop] for hop in range(1, seq_count)]
            top = functools.reduce(jnp.maximum, logs)
            total = functools.reduce(jnp.add, [jnp.exp2(log - top) for log in logs])
            shares = (seq_count * slots / HEADS) / total
            for i in range(per):
                factors.append(
                    shares[i : i + 1] * jnp.exp2(local[part * per + i] - top[i : i + 1])
                )
        small = 64
        for start in range(0, slots, small):
            part = slice(start, start + small)
            total = kept[0, part, :] * factors[0]
            for h in range(1, HEADS):
                total = total + kept[h, part, :] * factors[h]
            heat_ref[part, :] = total

    pl.run_scoped(find, pltpu.VMEM((HEADS, slots, finding_ref.shape[0]), F32))
    each(row_copy, "wait_send", 1, devices)
    each(near_copy, "wait_send", 0, slides)
    each(far_copy, "wait_send", 0, slides)
    each(pass_copy, "wait_send", 0, slides)
    each(stat_copy, "wait_send", 1, seq_count)
    each(stat_copy, "wait_send", seq_count + 1, 2 * seq_count)
    store.wait()


def layer(destination, embeds, gain, weight, out_weight, finding, capacity, slides, seq_count):
    rows, width = embeds.shape
    finds = finding.shape[0]
    devices = slides * seq_count
    slots = devices * capacity
    chunk = seq_count * capacity
    lanes = max(128, devices)
    vmem = pl.BlockSpec(memory_space=pltpu.VMEM)
    anywhere = pl.BlockSpec(memory_space=pl.ANY)
    dma = pltpu.SemaphoreType.DMA
    return pl.pallas_call(
        functools.partial(layer_kernel, capacity, slides, seq_count),
        in_specs=[vmem, anywhere, vmem, anywhere, anywhere, anywhere],
        out_specs=[anywhere, vmem],
        out_shape=(
            jax.ShapeDtypeStruct((slots, width), BF16),
            jax.ShapeDtypeStruct((slots, finds), F32),
        ),
        scratch_shapes=[
            pltpu.VMEM((devices, capacity, width), BF16),
            pltpu.VMEM((devices, capacity, width), BF16),
            pltpu.VMEM((8, lanes), jnp.int32),
            pltpu.VMEM((devices, 8, lanes), jnp.int32),
            pltpu.VMEM(embeds.shape, BF16),
            pltpu.VMEM(finding.shape, BF16),
            pltpu.VMEM(weight.shape, BF16),
            pltpu.VMEM((slots, width), BF16),
            pltpu.VMEM((slots, 2 * width), BF16),
            pltpu.VMEM((slots // 2, 2 * width), BF16),
            pltpu.VMEM((slots // 4, 2 * width), BF16),
            pltpu.VMEM((chunk, width), BF16),
            pltpu.VMEM((slots // 2, 2 * width), BF16),
            pltpu.VMEM((slots // 4, 2 * width), BF16),
            pltpu.VMEM((slots // 4, 2 * width), BF16),
            pltpu.VMEM((slots, width), BF16),
            pltpu.VMEM((16, slots), F32),
            pltpu.VMEM((slots, 1), F32),
            pltpu.VMEM((2, 8, finds), F32),
            pltpu.VMEM((2 * seq_count, 8, finds), F32),
            dma((devices,)),
            dma((devices,)),
            dma((devices,)),
            dma((devices,)),
            dma,
            dma((4,)),
            dma((slides,)),
            dma((slides,)),
            dma((slides,)),
            dma((slides,)),
            dma((slides,)),
            dma((slides,)),
            dma((2 * seq_count,)),
            dma((2 * seq_count,)),
            dma,
        ],
        compiler_params=params(LAYER_LIMIT, collective_id=2, has_side_effects=True),
        cost_estimate=pl.CostEstimate(
            flops=8 * slots * width * width + 8 * slots * slots * width,
            bytes_accessed=30_000_000,
            transcendentals=20_000_000,
        ),
        name="layer",
    )(destination.reshape(1, rows), embeds, gain.reshape(width // HEAD, HEAD), weight, out_weight, finding)


LAYER_LIMIT = 63 * 1024 * 1024


def layer_shards(embeds, destination, norm_gain, qkv_weight, out_weight, finding_queries):
    slides = lax.axis_size("slide")
    seq_count = lax.axis_size("seq")
    slots = embeds.shape[0] * 2
    capacity = slots // (slides * seq_count)
    return layer(
        destination, embeds, norm_gain, qkv_weight, out_weight, finding_queries,
        capacity, slides, seq_count,
    )


def solution(mesh):
    in_specs = (P(("slide", "seq"), None), P(("slide", "seq"), None), P(), P(), P(), P())
    out_specs = (P(("slide", "seq"), None), P(("slide", "seq"), None))

    def program(embeds, *rest):
        devices = mesh.shape["slide"] * mesh.shape["seq"]
        capacity = embeds.shape[0] * 2 // devices // devices
        chunk = capacity * mesh.shape["seq"]
        body = layer_shards if capacity % 8 == 0 and chunk % 64 == 0 else shards
        return jax.shard_map(
            body, mesh=mesh, in_specs=in_specs, out_specs=out_specs, check_vma=False
        )(embeds, *rest)

    return program
```
